256 devices in a mesh: bx: 32 (over z, x), by: 8 (over y, core).
Axes of the slice: x: 4, y: 4, z: 8, core: 2. Of those that a mesh axis runs over, the one named last changes fastest.
Arguments:
- scalar_field: float32 [64, 1024, 1024], P(None, 'bx', 'by'), may hold values from -8 to 8
- transfer_in: bfloat16 [16, 8], replicated, may hold values from -2 to 2
- transfer_out: bfloat16 [16, 16], replicated, may hold values from -1.5 to 1.5
Outputs:
- view_x: float32 [2, 8, 64, 1024], P(None, None, 'bx', 'by')
- view_y: float32 [2, 8, 64, 1024], P(None, None, 'by', 'bx')
The draws below stay inside these ranges and needn't reach their ends.
All inputs are finite; a program needn't handle non-finite values.
Results may differ from the reference program's by a relative error of at most 0.00035.
Values sent between devices are 32-bit elements; how exact they have to be, the bound alone decides.
A program may use at most 64 MiB of HBM per device.

```python
import jax
import jax.numpy as jnp
from jax import lax

BANDS = 8
HID = 16
FEAT = 8
NZ = 64
NX = 1024
NY = 1024


def draw_scalar_field(key, part):
    key_cells, key_stripes, key_columns = jax.random.split(key, 3)
    grains = jnp.clip(jax.random.normal(key_cells, (NZ, NX, NY), jnp.float32), -2.5, 2.5)
    stripes = jnp.clip(jax.random.normal(key_stripes, (NZ, 1, NY), jnp.float32), -2.5, 2.5)
    columns = jnp.clip(jax.random.normal(key_columns, (NZ, NX, 1), jnp.float32), -2.5, 2.5)
    return 0.6 * grains + stripes + columns


def centred(key, shape, width, reach, held_as=jnp.bfloat16):
    return jnp.clip(width * jax.random.normal(key, shape, jnp.float32), -reach, reach).astype(held_as)


def setup_inputs(seed: int = 0) -> dict:
    streams_of = jax.random.split(jax.random.key(seed), 4)
    return {
        "scalar_field": draw_scalar_field(jax.random.fold_in(streams_of[3], 71), 0),
        "transfer_in": centred(streams_of[1], (HID, FEAT), FEAT ** -0.5, 2.0),
        "transfer_out": centred(streams_of[2], (2 * BANDS, HID), HID ** -0.5, 1.5),
    }


def smooth(values):
    padded = jnp.pad(values, 1)
    nearby = padded[2:, 1:-1, 1:-1] + padded[:-2, 1:-1, 1:-1]
    nearby = nearby + padded[1:-1, 2:, 1:-1] + padded[1:-1, :-2, 1:-1]
    nearby = nearby + padded[1:-1, 1:-1, 2:] + padded[1:-1, 1:-1, :-2]
    return 0.4 * values + 0.1 * nearby

def gradients(padded):
    diff_x = padded[:, 2:, :] - padded[:, :-2, :]
    grad_x = (2.0 * diff_x[1:-1, :, 1:-1] + diff_x[:-2, :, 1:-1] + diff_x[2:, :, 1:-1] + diff_x[1:-1, :, :-2] + diff_x[1:-1, :, 2:]) / 12.0
    diff_y = padded[:, :, 2:] - padded[:, :, :-2]
    grad_y = (2.0 * diff_y[1:-1, 1:-1] + diff_y[:-2, 1:-1] + diff_y[2:, 1:-1] + diff_y[1:-1, :-2] + diff_y[1:-1, 2:]) / 12.0
    diff_z = padded[2:] - padded[:-2]
    grad_z = (2.0 * diff_z[:, 1:-1, 1:-1] + diff_z[:, :-2, 1:-1] + diff_z[:, 2:, 1:-1] + diff_z[:, 1:-1, :-2] + diff_z[:, 1:-1, 2:]) / 12.0
    return (padded[1:-1, 1:-1, 1:-1], grad_x, grad_y, grad_z)

def transfer(padded, transfer_in, transfer_out):
    centre, grad_x, grad_y, grad_z = gradients(padded)
    scaled_x = 4.0 * grad_x
    scaled_y = 4.0 * grad_y
    scaled_z = 4.0 * grad_z
    magnitude = jnp.sqrt(1.0 + scaled_x * scaled_x + scaled_y * scaled_y + scaled_z * scaled_z)
    features = jnp.stack([centre, scaled_x, scaled_y, scaled_z, magnitude, centre * magnitude, centre * centre, jnp.ones_like(centre)]).astype(jnp.bfloat16)
    hidden = jax.nn.silu(jnp.einsum('hf,fzxy->hzxy', transfer_in.astype(jnp.float32), features.astype(jnp.float32))).astype(jnp.bfloat16)
    channels = jnp.einsum('ch,hzxy->czxy', transfer_out.astype(jnp.float32), hidden.astype(jnp.float32))
    return (jax.nn.softplus(channels[:BANDS]), jax.nn.softplus(channels[BANDS:]))

def reference(scalar_field, transfer_in, transfer_out):
    smoothed = smooth(smooth(scalar_field))
    padded = jnp.pad(smoothed, 1)
    planes = 8
    step_x = 2.0 / NX
    step_y = 2.0 / NY

    def advance(carried, index):
        colour, optical = carried
        window = lax.dynamic_slice_in_dim(padded, (index * planes).astype(jnp.int32), planes + 2, 1)
        emission, absorption = transfer(window, transfer_in, transfer_out)
        thickness = absorption * step_x
        running = jnp.cumsum(thickness, axis=2)
        visible = jnp.exp(-(optical[:, :, None, :] + running - thickness))
        colour = colour + lax.optimization_barrier(jnp.sum(visible * -jnp.expm1(-thickness) * emission, axis=2))
        optical = optical + running[:, :, -1, :]
        thickness_y = absorption * step_y
        running_y = jnp.cumsum(thickness_y, axis=3)
        colour_y = lax.optimization_barrier(jnp.sum(jnp.exp(-(running_y - thickness_y)) * -jnp.expm1(-thickness_y) * emission, axis=3))
        clear_y = jnp.exp(-running_y[..., -1])
        return ((colour, optical), jnp.stack([colour_y, clear_y]))
    blank = jnp.zeros((BANDS, NZ, NY), jnp.float32)
    (colour, optical), images = lax.scan(advance, (blank, blank), jnp.arange(NX // planes, dtype=jnp.int32))
    view_x = jnp.stack([colour, jnp.exp(-optical)])
    view_y = jnp.transpose(images, (1, 2, 3, 0, 4)).reshape(2, BANDS, NZ, NX)
    return (view_x, view_y)
```

```python
import jax
import jax.numpy as jnp
from jax import lax
from jax.experimental import pallas as pl
from jax.experimental.pallas import tpu as pltpu
from jax.sharding import PartitionSpec as P

BANDS = 8
HID = 16
FEAT = 8
LOG2E = 1.4426950408889634
GROUP = 4


def extended(shard, sides, width):
    for axis, dim in sides:
        peers, length = (lax.axis_size(axis), shard.shape[dim])
        up = [(i, i + 1) for i in range(peers - 1)]
        down = [(j, i) for i, j in up]
        last = lax.slice_in_dim(shard, length - width, length, axis=dim)
        initial = lax.slice_in_dim(shard, 0, width, axis=dim)
        before = lax.ppermute(last, axis, up)
        after = lax.ppermute(initial, axis, down)
        shard = jnp.concatenate([before, shard, after], axis=dim)
    return shard


def lanes_of():
    return lax.broadcasted_iota(jnp.int32, (8, 128), 1)


def softplus(v):
    grown = jnp.exp2(jnp.minimum(v * LOG2E, 126.0))
    return jnp.maximum(v, jnp.log(1.0 + grown))


def render(place_ref, tb_ref, w1_ref, w2_ref, j_ref, r_ref, s1_ref, p_ref, b_ref, d_ref, x_ref, yc_ref, yt_ref, rs_ref):
    lane = lanes_of()
    seg = lax.broadcasted_iota(jnp.int32, (8, 128), 0)
    z = lane & 63
    half = lane >> 6
    top = z == 0
    bottom = z == 63
    full_x = place_ref[2]
    full_y = place_ref[3]
    at_x = place_ref[0] * 32 + half * 16
    at_y = place_ref[1] * 128 + seg * 16

    def above(v):
        return jnp.where(top, 0.0, pltpu.roll(v, 1, 1))

    def below(v):
        return jnp.where(bottom, 0.0, pltpu.roll(v, 127, 1))

    def in_x(xp):
        g = at_x + xp
        return (g >= 0) & (g < full_x)

    def in_y(yp):
        g = at_y + yp
        return (g >= 0) & (g < full_y)

    def first(i, carry):
        mine = in_x(i - 2)
        mid = [tb_ref[i + 1, pl.ds(k, 8, stride=16), :] for k in range(22)]
        for k in range(20):
            c = mid[k + 1]
            near = tb_ref[i, pl.ds(k + 1, 8, stride=16), :] + tb_ref[i + 2, pl.ds(k + 1, 8, stride=16), :]
            near = near + mid[k] + mid[k + 2] + above(c) + below(c)
            ok = mine if 2 <= k < 18 else mine & in_y(k - 2)
            s1_ref[i, k] = jnp.where(ok, 0.4 * c + 0.1 * near, 0.0)
        return carry

    lax.fori_loop(0, 20, first, 0)

    def second(i, carry):
        mine = in_x(i - 1)
        mid = [s1_ref[i + 1, k] for k in range(20)]
        for k in range(18):
            c = mid[k + 1]
            near = s1_ref[i, k + 1] + s1_ref[i + 2, k + 1]
            near = near + mid[k] + mid[k + 2] + above(c) + below(c)
            ok = mine if 1 <= k < 17 else mine & in_y(k - 1)
            s = jnp.where(ok, 0.4 * c + 0.1 * near, 0.0)
            up, down = above(s), below(s)
            p_ref[i, k] = s
            b_ref[i, k] = 2.0 * s + (up + down)
            d_ref[i, k] = down - up
        return carry

    lax.fori_loop(0, 18, second, 0)

    for b in range(BANDS):
        yc_ref[b] = jnp.zeros((128, 128), jnp.float32)
        yt_ref[b] = jnp.ones((128, 128), jnp.float32)

    def features(i, k):
        s = p_ref[i, k]
        a = p_ref[i + 1, k + 1] - p_ref[i - 1, k - 1]
        c = p_ref[i + 1, k - 1] - p_ref[i - 1, k + 1]
        gx = (b_ref[i + 1, k] - b_ref[i - 1, k] + (a + c)) * (1.0 / 3.0)
        gy = (b_ref[i, k + 1] - b_ref[i, k - 1] + (a - c)) * (1.0 / 3.0)
        d = d_ref[i, k]
        gz = (d + d + (d_ref[i + 1, k] + d_ref[i - 1, k]) + (d_ref[i, k + 1] + d_ref[i, k - 1])) * (1.0 / 3.0)
        q = 1.0 + gx * gx + gy * gy + gz * gz
        m = q * lax.rsqrt(q)
        return s, gx, gy, gz, m, s * m, s * s

    one = jnp.ones((8, 128), jnp.float32)
    w1 = w1_ref[...]
    w2 = w2_ref[...]

    def columns(k, carry):
        def cells(g, state):
            state = list(state)
            for n in range(GROUP):
                rows = list(features(g * GROUP + n + 1, k + 1)) + [one]
                for f in range(0, FEAT, 2):
                    pair = jnp.concatenate([rows[f], rows[f + 1]], axis=0)
                    x_ref[8 * f : 8 * f + 16, 128 * n : 128 * n + 128] = pair.astype(jnp.bfloat16)
            u = jnp.dot(w1, x_ref[...], preferred_element_type=jnp.float32)
            hidden = (u + u * jnp.tanh(u)).astype(jnp.bfloat16)
            ch = jnp.dot(w2, hidden, preferred_element_type=jnp.float32)
            for n in range(GROUP):
                row = pl.multiple_of((g * GROUP + n) * 8, 8)
                for b in range(BANDS):
                    e = softplus(ch[8 * b : 8 * b + 8, 128 * n : 128 * n + 128])
                    t = softplus(ch[64 + 8 * b : 72 + 8 * b, 128 * n : 128 * n + 128])
                    q = jnp.exp2(t * (-LOG2E / 512.0))
                    tx = state[8 + b]
                    nx = tx * q
                    state[b] = state[b] + (tx - nx) * e
                    state[8 + b] = nx
                    ty = yt_ref[b, pl.ds(row, 8), :]
                    ny = ty * q
                    yc_ref[b, pl.ds(row, 8), :] = yc_ref[b, pl.ds(row, 8), :] + (ty - ny) * e
                    yt_ref[b, pl.ds(row, 8), :] = ny
            return tuple(state)

        start = (jnp.zeros((8, 128), jnp.float32),) * BANDS + (one,) * BANDS
        state = lax.fori_loop(0, 16 // GROUP, cells, start)
        colour = [state[b] + state[8 + b] * pltpu.roll(state[b], 64, 1) for b in range(BANDS)]
        clear = [state[8 + b] * pltpu.roll(state[8 + b], 64, 1) for b in range(BANDS)]
        image = jnp.transpose(jnp.concatenate(colour + clear, axis=0))
        j_ref[pl.ds(k, 64, stride=16), :] = image[0:64]
        return carry

    lax.fori_loop(0, 16, columns, 0)

    for b in range(BANDS):
        for h in range(2):
            colour = yc_ref[b, pl.ds(64 * h, 8, stride=8), :]
            clear = yt_ref[b, pl.ds(64 * h, 8, stride=8), :]
            for s in range(1, 8):
                colour = colour + clear * yc_ref[b, pl.ds(64 * h + s, 8, stride=8), :]
                clear = clear * yt_ref[b, pl.ds(64 * h + s, 8, stride=8), :]
            rs_ref[0, 16 * b + 8 * h : 16 * b + 8 * h + 8, :] = colour
            rs_ref[1, 16 * b + 8 * h : 16 * b + 8 * h + 8, :] = clear
    for kind in range(2):
        image = jnp.transpose(rs_ref[kind])
        for h in range(2):
            for p in range(8):
                r_ref[p, h, :, 128 * kind : 128 * kind + 128] = image[64 * h + 8 * p : 64 * h + 8 * p + 8]


def render_call(place, tb, w1, w2):
    vmem = pl.BlockSpec(memory_space=pltpu.VMEM)
    return pl.pallas_call(
        render,
        out_shape=(
            jax.ShapeDtypeStruct((1024, 128), jnp.float32),
            jax.ShapeDtypeStruct((8, 2, 8, 256), jnp.float32),
        ),
        in_specs=[pl.BlockSpec(memory_space=pltpu.SMEM), vmem, vmem, vmem],
        out_specs=(vmem, vmem),
        scratch_shapes=[
            pltpu.VMEM((20, 20, 8, 128), jnp.float32),
            pltpu.VMEM((18, 18, 8, 128), jnp.float32),
            pltpu.VMEM((18, 18, 8, 128), jnp.float32),
            pltpu.VMEM((18, 18, 8, 128), jnp.float32),
            pltpu.VMEM((64, 128 * GROUP), jnp.bfloat16),
            pltpu.VMEM((8, 128, 128), jnp.float32),
            pltpu.VMEM((8, 128, 128), jnp.float32),
            pltpu.VMEM((2, 128, 128), jnp.float32),
        ],
        compiler_params=pltpu.CompilerParams(vmem_limit_bytes=40 << 20),
        name="render",
    )(place, tb, w1, w2)


def fold(jr_ref, rr_ref, vx_ref, vy_ref, at_ref):
    count_x = jr_ref.shape[0]
    count_y = rr_ref.shape[0]
    lane = lax.broadcasted_iota(jnp.int32, (32, 128), 1)
    low = lane < 64

    def over(s, pair):
        front, clear = pair
        piece = jr_ref[s]
        both = jnp.where(low, pltpu.roll(piece, 64, 1), piece)
        return jnp.where(low, front, 0.0) + clear * piece, clear * both

    start = (jnp.zeros((32, 128), jnp.float32), jnp.ones((32, 128), jnp.float32))
    image, _ = lax.fori_loop(0, count_x, over, start)
    at_ref[...] = jnp.zeros_like(at_ref)
    at_ref[0:32, :] = image
    at_ref[...] = jnp.transpose(at_ref[...])
    line = lax.broadcasted_iota(jnp.int32, (16, 128), 1)
    for z in range(2):
        row = jnp.zeros((16, 128), jnp.float32)
        for s in range(8):
            part = at_ref[pl.ds(s, 16, stride=8), :]
            shift = (16 * s - 16 * z) % 128
            part = pltpu.roll(part, shift, 1) if shift else part
            row = jnp.where((line >> 4) == s, part, row)
        vx_ref[:, z, :] = row

    def over_y(s, pair):
        piece = rr_ref[s]
        return pair[0] + pair[1] * piece[:, 0:128], pair[1] * piece[:, 128:256]

    start = (jnp.zeros((16, 128), jnp.float32), jnp.ones((16, 128), jnp.float32))
    kinds = lax.fori_loop(0, count_y, over_y, start)
    lane8 = lanes_of()
    for kind in range(2):
        for b in range(BANDS):
            shift = (128 - 16 * b) % 128
            front = kinds[kind][0:8]
            back = kinds[kind][8:16]
            front = pltpu.roll(front, shift, 1) if shift else front
            back = pltpu.roll(back, shift + 16, 1) if shift < 112 else back
            vy_ref[8 * kind + b] = jnp.where(lane8 < 16, front, back)[:, 0:32]


def fold_call(jr, rr):
    vmem = pl.BlockSpec(memory_space=pltpu.VMEM)
    return pl.pallas_call(
        fold,
        out_shape=(
            jax.ShapeDtypeStruct((16, 2, 128), jnp.float32),
            jax.ShapeDtypeStruct((16, 8, 32), jnp.float32),
        ),
        in_specs=[vmem, vmem],
        out_specs=(vmem, vmem),
        scratch_shapes=[pltpu.VMEM((128, 128), jnp.float32)],
        name="fold",
    )(jr, rr)


def spread(weights, scale):
    rows, cols = weights.shape
    eye = jnp.eye(8, dtype=jnp.float32)
    big = (weights.astype(jnp.float32) * scale)[:, None, :, None] * eye[None, :, None, :]
    return big.reshape(rows * 8, cols * 8).astype(jnp.bfloat16)


def body(scalar_field, transfer_in, transfer_out):
    count_x = lax.axis_size("bx")
    count_y = lax.axis_size("by")
    wide = extended(scalar_field, (("bx", 1), ("by", 2)), 3)
    wide = jnp.pad(wide, ((0, 0), (0, 0), (0, 2)))
    halves = jnp.stack([wide[:, 0:22], wide[:, 16:38]])
    tb = jnp.transpose(halves, (2, 3, 0, 1)).reshape(22, 136, 128)
    place = jnp.stack(
        [lax.axis_index("bx"), lax.axis_index("by"), jnp.int32(32 * count_x), jnp.int32(128 * count_y)]
    ).astype(jnp.int32)
    j, r = render_call(place, tb, spread(transfer_in, 0.5), spread(transfer_out, 1.0))
    slab = 64 // count_x
    jr = lax.all_to_all(j.reshape(count_x, slab * 16, 128), "bx", split_axis=0, concat_axis=0, tiled=True)
    rr = lax.all_to_all(r.reshape(count_y, 128 // count_y, 256), "by", split_axis=0, concat_axis=0, tiled=True)
    vx, vy = fold_call(jr, rr)
    return (vx.reshape(2, 8, slab, 128), vy.reshape(2, 8, 8, 32))


def solution(mesh):
    return jax.shard_map(
        body,
        mesh=mesh,
        in_specs=(P(None, "bx", "by"), P(), P()),
        out_specs=(P(None, None, "bx", "by"), P(None, None, "by", "bx")),
        check_vma=False,
    )
```

```python
import functools

import jax
import jax.numpy as jnp
from jax import lax
from jax.experimental import pallas as pl
from jax.experimental.pallas import tpu as pltpu
from jax.sharding import PartitionSpec as P

BANDS = 8
HID = 16
FEAT = 8
LOG2E = 1.4426950408889634
MESH = pl.DeviceIdType.MESH
GROUP = 4


def extended(shard, sides, width):
    for axis, dim in sides:
        peers, length = (lax.axis_size(axis), shard.shape[dim])
        up = [(i, i + 1) for i in range(peers - 1)]
        down = [(j, i) for i, j in up]
        last = lax.slice_in_dim(shard, length - width, length, axis=dim)
        initial = lax.slice_in_dim(shard, 0, width, axis=dim)
        before = lax.ppermute(last, axis, up)
        after = lax.ppermute(initial, axis, down)
        shard = jnp.concatenate([before, shard, after], axis=dim)
    return shard


def lanes_of():
    return lax.broadcasted_iota(jnp.int32, (8, 128), 1)


def softplus(v):
    grown = jnp.exp2(jnp.minimum(v * LOG2E, 126.0))
    return jnp.maximum(v, jnp.log(1.0 + grown))


def render(place_ref, tb_ref, w1_ref, w2_ref, j_ref, r_ref, s1_ref, p_ref, b_ref, d_ref, x_ref, u_ref, ch_ref, yc_ref, yt_ref, rs_ref):
    lane = lanes_of()
    seg = lax.broadcasted_iota(jnp.int32, (8, 128), 0)
    z = lane & 63
    half = lane >> 6
    top = z == 0
    bottom = z == 63
    full_x = place_ref[2]
    full_y = place_ref[3]
    at_x = place_ref[0] * 32 + half * 16
    at_y = place_ref[1] * 128 + seg * 16

    def above(v):
        return jnp.where(top, 0.0, pltpu.roll(v, 1, 1))

    def below(v):
        return jnp.where(bottom, 0.0, pltpu.roll(v, 127, 1))

    def inside(xp, yp):
        gy = at_y + yp
        ok = (gy >= 0) & (gy < full_y)
        if xp < 0:
            ok = ok & (at_x + xp >= 0)
        if xp > 15:
            ok = ok & (at_x + xp < full_x)
        return ok

    def field(xp, yp):
        return tb_ref[xp + 3, pl.ds(yp + 8, 8, stride=16), :]

    def first(yp):
        mid = [field(xp, yp) for xp in range(-3, 19)]
        for k in range(20):
            c = mid[k + 1]
            near = field(k - 2, yp - 1) + field(k - 2, yp + 1)
            near = near + (mid[k] + mid[k + 2]) + (above(c) + below(c))
            s1_ref[k, yp + 2] = jnp.where(inside(k - 2, yp), 0.4 * c + 0.1 * near, 0.0)

    def second(yp):
        mid = [s1_ref[k, yp + 2] for k in range(20)]
        for k in range(18):
            c = mid[k + 1]
            near = s1_ref[k + 1, yp + 1] + s1_ref[k + 1, yp + 3]
            near = near + (mid[k] + mid[k + 2]) + (above(c) + below(c))
            s = jnp.where(inside(k - 1, yp), 0.4 * c + 0.1 * near, 0.0)
            up, down = above(s), below(s)
            p_ref[k, yp + 1] = s
            b_ref[k, yp + 1] = 2.0 * s + (up + down)
            d_ref[k, yp + 1] = down - up

    one = jnp.ones((8, 128), jnp.float32)
    zero = jnp.zeros((8, 128), jnp.float32)

    def features(i, k):
        s = p_ref[i, k]
        a = p_ref[i + 1, k + 1] - p_ref[i - 1, k - 1]
        c = p_ref[i + 1, k - 1] - p_ref[i - 1, k + 1]
        gx = (b_ref[i + 1, k] - b_ref[i - 1, k] + (a + c)) * (1.0 / 3.0)
        gy = (b_ref[i, k + 1] - b_ref[i, k - 1] + (a - c)) * (1.0 / 3.0)
        d = d_ref[i, k]
        gz = (d + d + (d_ref[i + 1, k] + d_ref[i - 1, k]) + (d_ref[i, k + 1] + d_ref[i, k - 1])) * (1.0 / 3.0)
        q = 1.0 + gx * gx + gy * gy + gz * gz
        m = q * lax.rsqrt(q)
        return s, gx, gy, gz, m, s * m, s * s, one

    def first_layer(g, k):
        slot = g % 2
        for n in range(GROUP):
            rows = features(g * GROUP + n + 1, k + 1)
            for f in range(0, FEAT, 2):
                pair = jnp.concatenate([rows[f], rows[f + 1]], axis=0)
                x_ref[slot, 8 * f : 8 * f + 16, 128 * n : 128 * n + 128] = pair.astype(jnp.bfloat16)
        u_ref[slot] = jnp.dot(w1_ref[...], x_ref[slot], preferred_element_type=jnp.float32)

    def second_layer(g):
        slot = g % 2
        u = u_ref[slot]
        hidden = (u + u * jnp.tanh(u)).astype(jnp.bfloat16)
        ch_ref[slot] = jnp.dot(w2_ref[...], hidden, preferred_element_type=jnp.float32)

    def views(g, state):
        slot = g % 2
        for n in range(GROUP):
            row = (g * GROUP + n) * 8
            for b in range(BANDS):
                e = softplus(ch_ref[slot, 8 * b : 8 * b + 8, 128 * n : 128 * n + 128])
                t = softplus(ch_ref[slot, 64 + 8 * b : 72 + 8 * b, 128 * n : 128 * n + 128])
                q = jnp.exp2(t * (-LOG2E / 512.0))
                tx = state[8 + b]
                nx = tx * q
                state[b] = state[b] + (tx - nx) * e
                state[8 + b] = nx
                ty = yt_ref[b, row : row + 8, :]
                ny = ty * q
                yc_ref[b, row : row + 8, :] = yc_ref[b, row : row + 8, :] + (ty - ny) * e
                yt_ref[b, row : row + 8, :] = ny

    chunks = 16 // GROUP

    def columns(k, carry):
        state = [zero] * BANDS + [one] * BANDS
        for g in range(chunks):
            ahead = g + 2
            views(g, state)
            second_layer((g + 1) % chunks)
            first_layer(ahead % chunks, k + ahead // chunks)
        second(k + 3)
        first(k + 5)
        colour = [state[b] + state[8 + b] * pltpu.roll(state[b], 64, 1) for b in range(BANDS)]
        clear = [state[8 + b] * pltpu.roll(state[8 + b], 64, 1) for b in range(BANDS)]
        image = jnp.transpose(jnp.concatenate(colour + clear, axis=0))
        j_ref[pl.ds(k, 64, stride=16), :] = image[0:64]
        return carry

    def lead_first(i, carry):
        first(i - 2)
        return carry

    def lead_second(i, carry):
        second(i - 1)
        return carry

    lax.fori_loop(0, 7, lead_first, 0)
    lax.fori_loop(0, 4, lead_second, 0)
    for b in range(BANDS):
        yc_ref[b] = jnp.zeros((128, 128), jnp.float32)
        yt_ref[b] = jnp.ones((128, 128), jnp.float32)
    first_layer(0, 0)
    first_layer(1, 0)
    second_layer(0)
    lax.fori_loop(0, 16, columns, 0)

    for b in range(BANDS):
        for h in range(2):
            colour = yc_ref[b, pl.ds(64 * h, 8, stride=8), :]
            clear = yt_ref[b, pl.ds(64 * h, 8, stride=8), :]
            for s in range(1, 8):
                colour = colour + clear * yc_ref[b, pl.ds(64 * h + s, 8, stride=8), :]
                clear = clear * yt_ref[b, pl.ds(64 * h + s, 8, stride=8), :]
            rs_ref[0, 16 * b + 8 * h : 16 * b + 8 * h + 8, :] = colour
            rs_ref[1, 16 * b + 8 * h : 16 * b + 8 * h + 8, :] = clear
    for kind in range(2):
        image = jnp.transpose(rs_ref[kind])
        for h in range(2):
            for p in range(8):
                r_ref[p, h, :, 128 * kind : 128 * kind + 128] = image[64 * h + 8 * p : 64 * h + 8 * p + 8]


def render_call(place, tb, w1, w2):
    vmem = pl.BlockSpec(memory_space=pltpu.VMEM)
    return pl.pallas_call(
        render,
        out_shape=(
            jax.ShapeDtypeStruct((1024, 128), jnp.float32),
            jax.ShapeDtypeStruct((8, 2, 8, 256), jnp.float32),
        ),
        in_specs=[pl.BlockSpec(memory_space=pltpu.SMEM), vmem, vmem, vmem],
        out_specs=(vmem, vmem),
        scratch_shapes=[
            pltpu.VMEM((20, 23, 8, 128), jnp.float32),
            pltpu.VMEM((18, 20, 8, 128), jnp.float32),
            pltpu.VMEM((18, 20, 8, 128), jnp.float32),
            pltpu.VMEM((18, 20, 8, 128), jnp.float32),
            pltpu.VMEM((2, 64, 128 * GROUP), jnp.bfloat16),
            pltpu.VMEM((2, 128, 128 * GROUP), jnp.float32),
            pltpu.VMEM((2, 128, 128 * GROUP), jnp.float32),
            pltpu.VMEM((8, 128, 128), jnp.float32),
            pltpu.VMEM((8, 128, 128), jnp.float32),
            pltpu.VMEM((2, 128, 128), jnp.float32),
        ],
        compiler_params=pltpu.CompilerParams(vmem_limit_bytes=40 << 20),
        name="render",
    )(place, tb, w1, w2)


def fold(count_x, count_y, j_ref, r_ref, vx_ref, vy_ref, jr_ref, rr_ref, at_ref, send_x, recv_x, send_y, recv_y):
    me_x = lax.axis_index("bx")
    me_y = lax.axis_index("by")

    def peer_x(hop):
        return lax.rem(me_x + hop, count_x)

    def peer_y(hop):
        return lax.rem(me_y + hop, count_y)

    barrier = pltpu.get_barrier_semaphore()

    def greet_x(hop, carry):
        pl.semaphore_signal(barrier, inc=1, device_id=(peer_x(hop), me_y), device_id_type=MESH)
        return carry

    def greet_y(hop, carry):
        pl.semaphore_signal(barrier, inc=1, device_id=(me_x, peer_y(hop)), device_id_type=MESH)
        return carry

    lax.fori_loop(1, count_x, greet_x, 0)
    lax.fori_loop(1, count_y, greet_y, 0)
    pl.semaphore_wait(barrier, count_x + count_y - 2)

    def copy_x(peer, source, hop):
        return pltpu.make_async_remote_copy(
            src_ref=j_ref.at[peer],
            dst_ref=jr_ref.at[source],
            send_sem=send_x.at[hop],
            recv_sem=recv_x.at[source],
            device_id=(peer, me_y),
            device_id_type=MESH,
        )

    def copy_y(peer, source, hop):
        return pltpu.make_async_remote_copy(
            src_ref=r_ref.at[peer],
            dst_ref=rr_ref.at[source],
            send_sem=send_y.at[hop],
            recv_sem=recv_y.at[source],
            device_id=(me_x, peer),
            device_id_type=MESH,
        )

    def send_all_y(hop, carry):
        copy_y(peer_y(hop), me_y, hop).start()
        return carry

    def send_all_x(hop, carry):
        copy_x(peer_x(hop), me_x, hop).start()
        return carry

    lax.fori_loop(1, count_x, send_all_x, 0)
    lax.fori_loop(1, count_y, send_all_y, 0)
    jr_ref[me_x] = j_ref[me_x]
    rr_ref[me_y] = r_ref[me_y]

    lane = lax.broadcasted_iota(jnp.int32, (32, 128), 1)
    low = lane < 64

    def wait_y(hop, carry):
        copy_y(me_y, peer_y(hop), hop).wait_recv()
        return carry

    lax.fori_loop(1, count_y, wait_y, 0)

    def over_y(s, pair):
        piece = rr_ref[s]
        return pair[0] + pair[1] * piece[:, 0:128], pair[1] * piece[:, 128:256]

    start = (jnp.zeros((16, 128), jnp.float32), jnp.ones((16, 128), jnp.float32))
    kinds = lax.fori_loop(0, count_y, over_y, start)
    lane8 = lanes_of()
    for kind in range(2):
        for b in range(BANDS):
            shift = (128 - 16 * b) % 128
            front = kinds[kind][0:8]
            back = kinds[kind][8:16]
            front = pltpu.roll(front, shift, 1) if shift else front
            back = pltpu.roll(back, shift + 16, 1) if shift < 112 else back
            vy_ref[8 * kind + b] = jnp.where(lane8 < 16, front, back)[:, 0:32]

    def wait_x(hop, carry):
        copy_x(me_x, peer_x(hop), hop).wait_recv()
        return carry

    lax.fori_loop(1, count_x, wait_x, 0)

    def over(s, pair):
        front, clear = pair
        piece = jr_ref[s]
        both = jnp.where(low, pltpu.roll(piece, 64, 1), piece)
        return jnp.where(low, front, 0.0) + clear * piece, clear * both

    start = (jnp.zeros((32, 128), jnp.float32), jnp.ones((32, 128), jnp.float32))
    image, _ = lax.fori_loop(0, count_x, over, start)
    at_ref[0:32, :] = image
    at_ref[32:128, :] = jnp.zeros((96, 128), jnp.float32)
    at_ref[...] = jnp.transpose(at_ref[...])
    line = lax.broadcasted_iota(jnp.int32, (16, 128), 1)
    for z in range(2):
        row = jnp.zeros((16, 128), jnp.float32)
        for s in range(8):
            part = at_ref[pl.ds(s, 16, stride=8), :]
            shift = (16 * s - 16 * z) % 128
            part = pltpu.roll(part, shift, 1) if shift else part
            row = jnp.where((line >> 4) == s, part, row)
        vx_ref[:, z, :] = row

    def sent_x(hop, carry):
        copy_x(peer_x(hop), me_x, hop).wait_send()
        return carry

    def sent_y(hop, carry):
        copy_y(peer_y(hop), me_y, hop).wait_send()
        return carry

    lax.fori_loop(1, count_x, sent_x, 0)
    lax.fori_loop(1, count_y, sent_y, 0)


def fold_call(j, r):
    count_x = j.shape[0]
    count_y = r.shape[0]
    vmem = pl.BlockSpec(memory_space=pltpu.VMEM)
    return pl.pallas_call(
        functools.partial(fold, count_x, count_y),
        out_shape=(
            jax.ShapeDtypeStruct((16, 2, 128), jnp.float32),
            jax.ShapeDtypeStruct((16, 8, 32), jnp.float32),
        ),
        in_specs=[vmem, vmem],
        out_specs=(vmem, vmem),
        scratch_shapes=[
            pltpu.VMEM(j.shape, jnp.float32),
            pltpu.VMEM(r.shape, jnp.float32),
            pltpu.VMEM((128, 128), jnp.float32),
            pltpu.SemaphoreType.DMA((count_x,)),
            pltpu.SemaphoreType.DMA((count_x,)),
            pltpu.SemaphoreType.DMA((count_y,)),
            pltpu.SemaphoreType.DMA((count_y,)),
        ],
        compiler_params=pltpu.CompilerParams(collective_id=1, has_side_effects=True),
        name="fold",
    )(j, r)


def spread(weights, scale):
    rows, cols = weights.shape
    eye = jnp.eye(8, dtype=jnp.float32)
    big = (weights.astype(jnp.float32) * scale)[:, None, :, None] * eye[None, :, None, :]
    return big.reshape(rows * 8, cols * 8).astype(jnp.bfloat16)


def body(scalar_field, transfer_in, transfer_out):
    count_x = lax.axis_size("bx")
    count_y = lax.axis_size("by")
    wide = extended(scalar_field, (("bx", 1), ("by", 2)), 3)
    wide = jnp.pad(wide, ((0, 0), (0, 0), (5, 5)))
    halves = jnp.stack([wide[:, 0:22], wide[:, 16:38]])
    tb = jnp.transpose(halves, (2, 3, 0, 1)).reshape(22, 144, 128)
    place = jnp.stack(
        [lax.axis_index("bx"), lax.axis_index("by"), jnp.int32(32 * count_x), jnp.int32(128 * count_y)]
    ).astype(jnp.int32)
    j, r = render_call(place, tb, spread(transfer_in, 0.5), spread(transfer_out, 1.0))
    slab = 64 // count_x
    vx, vy = fold_call(j.reshape(count_x, slab * 16, 128), r.reshape(count_y, 128 // count_y, 256))
    return (vx.reshape(2, 8, slab, 128), vy.reshape(2, 8, 8, 32))


def solution(mesh):
    return jax.shard_map(
        body,
        mesh=mesh,
        in_specs=(P(None, "bx", "by"), P(), P()),
        out_specs=(P(None, None, "bx", "by"), P(None, None, "by", "bx")),
        check_vma=False,
    )
```

```python
import functools

import jax
import jax.numpy as jnp
from jax import lax
from jax.experimental import pallas as pl
from jax.experimental.pallas import tpu as pltpu
from jax.sharding import PartitionSpec as P

BANDS = 8
HID = 16
FEAT = 8
LOG2E = 1.4426950408889634
MESH = pl.DeviceIdType.MESH
GROUP = 4


def lanes_of():
    return lax.broadcasted_iota(jnp.int32, (8, 128), 1)


def softplus(v):
    grown = jnp.exp2(jnp.minimum(v * LOG2E, 126.0))
    return jnp.maximum(v, jnp.log(1.0 + grown))


def halo(count_x, count_y, f_ref, tb_ref, xs_ref, xr_ref, yr_ref, cr_ref, sx, rx, sy, ry, sc, rc):
    me_x = lax.axis_index("bx")
    me_y = lax.axis_index("by")
    xs = (lax.rem(me_x + count_x - 1, count_x), lax.rem(me_x + 1, count_x))
    ys = (lax.rem(me_y + count_y - 1, count_y), lax.rem(me_y + 1, count_y))

    barrier = pltpu.get_barrier_semaphore()
    for peer in [(x, me_y) for x in xs] + [(me_x, y) for y in ys] + [(x, y) for x in xs for y in ys]:
        pl.semaphore_signal(barrier, inc=1, device_id=peer, device_id_type=MESH)

    def plane(x):
        return f_ref[pl.ds(x, 64, stride=32), :]

    for i in range(3):
        xs_ref[0, i] = plane(i)
        xs_ref[1, i] = plane(29 + i)
    pl.semaphore_wait(barrier, 8)

    copies = []
    for side in range(2):
        copies.append(
            pltpu.make_async_remote_copy(
                src_ref=xs_ref.at[side],
                dst_ref=xr_ref.at[1 - side],
                send_sem=sx.at[side],
                recv_sem=rx.at[1 - side],
                device_id=(xs[side], me_y),
                device_id_type=MESH,
            )
        )
        copies[-1].start()

    def turn(x, front, back):
        tb_ref[x + 3, 8:136, :] = jnp.transpose(jnp.concatenate([front, back], axis=0))

    edges = (pl.ds(8, 8), pl.ds(128, 8))
    ends = (pl.ds(3, 3), pl.ds(16, 3))
    for x in (0, 1, 2, 13, 14, 15):
        turn(x, plane(x), plane(16 + x))
    for side in range(2):
        for part in range(2):
            copies.append(
                pltpu.make_async_remote_copy(
                    src_ref=tb_ref.at[ends[side], edges[part]],
                    dst_ref=cr_ref.at[2 * (1 - side) + (1 - part)],
                    send_sem=sc.at[2 * side + part],
                    recv_sem=rc.at[2 * (1 - side) + (1 - part)],
                    device_id=(xs[side], ys[part]),
                    device_id_type=MESH,
                )
            )
            copies[-1].start()

    def rest(x, carry):
        turn(x, plane(x), plane(16 + x))
        return carry

    lax.fori_loop(3, 13, rest, 0)
    for part in range(2):
        copies.append(
            pltpu.make_async_remote_copy(
                src_ref=tb_ref.at[pl.ds(3, 16), edges[part]],
                dst_ref=yr_ref.at[1 - part],
                send_sem=sy.at[part],
                recv_sem=ry.at[1 - part],
                device_id=(me_x, ys[part]),
                device_id_type=MESH,
            )
        )
        copies[-1].start()

    inner_x = (me_x > 0, me_x < count_x - 1)
    inner_y = (me_y > 0, me_y < count_y - 1)
    copies[0].wait_recv()
    copies[1].wait_recv()
    for i in range(3):
        turn(i - 3, jnp.where(inner_x[0], xr_ref[0, i], 0.0), plane(13 + i))
        turn(16 + i, plane(16 + i), jnp.where(inner_x[1], xr_ref[1, i], 0.0))
    for copy in copies[2:]:
        copy.wait_recv()
    low = lax.broadcasted_iota(jnp.int32, (8, 128), 1) < 64
    rims = (pl.ds(0, 8), pl.ds(136, 8))
    for part in range(2):
        for x in range(16):
            tb_ref[x + 3, rims[part], :] = jnp.where(inner_y[part], yr_ref[part, x], 0.0)
        for i in range(3):
            far = jnp.where(inner_x[0], cr_ref[part, i], 0.0)
            edge = jnp.where(low, pltpu.roll(far, 64, 1), pltpu.roll(yr_ref[part, 13 + i], 64, 1))
            tb_ref[i, rims[part], :] = jnp.where(inner_y[part], edge, 0.0)
            far = jnp.where(inner_x[1], cr_ref[2 + part, i], 0.0)
            edge = jnp.where(low, pltpu.roll(yr_ref[part, i], 64, 1), pltpu.roll(far, 64, 1))
            tb_ref[19 + i, rims[part], :] = jnp.where(inner_y[part], edge, 0.0)
    for copy in copies:
        copy.wait_send()


def halo_call(field, count_x, count_y):
    vmem = pl.BlockSpec(memory_space=pltpu.VMEM)
    return pl.pallas_call(
        functools.partial(halo, count_x, count_y),
        out_shape=jax.ShapeDtypeStruct((22, 144, 128), jnp.float32),
        in_specs=[vmem],
        out_specs=vmem,
        scratch_shapes=[
            pltpu.VMEM((2, 3, 64, 128), jnp.float32),
            pltpu.VMEM((2, 3, 64, 128), jnp.float32),
            pltpu.VMEM((2, 16, 8, 128), jnp.float32),
            pltpu.VMEM((4, 3, 8, 128), jnp.float32),
            pltpu.SemaphoreType.DMA((2,)),
            pltpu.SemaphoreType.DMA((2,)),
            pltpu.SemaphoreType.DMA((2,)),
            pltpu.SemaphoreType.DMA((2,)),
            pltpu.SemaphoreType.DMA((4,)),
            pltpu.SemaphoreType.DMA((4,)),
        ],
        compiler_params=pltpu.CompilerParams(collective_id=0, has_side_effects=True),
        name="halo",
    )(field)


def render(place_ref, tb_ref, w1_ref, w2_ref, j_ref, r_ref, s1_ref, p_ref, b_ref, d_ref, x_ref, u_ref, ch_ref, yc_ref, yt_ref, rs_ref):
    lane = lanes_of()
    seg = lax.broadcasted_iota(jnp.int32, (8, 128), 0)
    z = lane & 63
    half = lane >> 6
    top = z == 0
    bottom = z == 63
    full_x = place_ref[2]
    full_y = place_ref[3]
    at_x = place_ref[0] * 32 + half * 16
    at_y = place_ref[1] * 128 + seg * 16

    def above(v):
        return jnp.where(top, 0.0, pltpu.roll(v, 1, 1))

    def below(v):
        return jnp.where(bottom, 0.0, pltpu.roll(v, 127, 1))

    def inside(xp, yp):
        gy = at_y + yp
        ok = (gy >= 0) & (gy < full_y)
        if xp < 0:
            ok = ok & (at_x + xp >= 0)
        if xp > 15:
            ok = ok & (at_x + xp < full_x)
        return ok

    def field(xp, yp):
        return tb_ref[xp + 3, pl.ds(yp + 8, 8, stride=16), :]

    def first(yp):
        mid = [field(xp, yp) for xp in range(-3, 19)]
        for k in range(20):
            c = mid[k + 1]
            near = field(k - 2, yp - 1) + field(k - 2, yp + 1)
            near = near + (mid[k] + mid[k + 2]) + (above(c) + below(c))
            s1_ref[k, yp + 2] = jnp.where(inside(k - 2, yp), 0.4 * c + 0.1 * near, 0.0)

    def second(yp):
        mid = [s1_ref[k, yp + 2] for k in range(20)]
        for k in range(18):
            c = mid[k + 1]
            near = s1_ref[k + 1, yp + 1] + s1_ref[k + 1, yp + 3]
            near = near + (mid[k] + mid[k + 2]) + (above(c) + below(c))
            s = jnp.where(inside(k - 1, yp), 0.4 * c + 0.1 * near, 0.0)
            up, down = above(s), below(s)
            p_ref[k, yp + 1] = s
            b_ref[k, yp + 1] = 2.0 * s + (up + down)
            d_ref[k, yp + 1] = down - up

    one = jnp.ones((8, 128), jnp.float32)
    zero = jnp.zeros((8, 128), jnp.float32)

    def features(i, k):
        s = p_ref[i, k]
        a = p_ref[i + 1, k + 1] - p_ref[i - 1, k - 1]
        c = p_ref[i + 1, k - 1] - p_ref[i - 1, k + 1]
        gx = (b_ref[i + 1, k] - b_ref[i - 1, k] + (a + c)) * (1.0 / 3.0)
        gy = (b_ref[i, k + 1] - b_ref[i, k - 1] + (a - c)) * (1.0 / 3.0)
        d = d_ref[i, k]
        gz = (d + d + (d_ref[i + 1, k] + d_ref[i - 1, k]) + (d_ref[i, k + 1] + d_ref[i, k - 1])) * (1.0 / 3.0)
        q = 1.0 + gx * gx + gy * gy + gz * gz
        m = q * lax.rsqrt(q)
        return s, gx, gy, gz, m, s * m, s * s, one

    def first_layer(g, k):
        slot = g % 2
        for n in range(GROUP):
            rows = features(g * GROUP + n + 1, k + 1)
            for f in range(0, FEAT, 2):
                pair = jnp.concatenate([rows[f], rows[f + 1]], axis=0)
                x_ref[slot, 8 * f : 8 * f + 16, 128 * n : 128 * n + 128] = pair.astype(jnp.bfloat16)
        u_ref[slot] = jnp.dot(w1_ref[...], x_ref[slot], preferred_element_type=jnp.float32)

    def second_layer(g):
        slot = g % 2
        u = u_ref[slot]
        hidden = (u + u * jnp.tanh(u)).astype(jnp.bfloat16)
        ch_ref[slot] = jnp.dot(w2_ref[...], hidden, preferred_element_type=jnp.float32)

    def views(g, state):
        slot = g % 2
        for n in range(GROUP):
            row = (g * GROUP + n) * 8
            for b in range(BANDS):
                e = softplus(ch_ref[slot, 8 * b : 8 * b + 8, 128 * n : 128 * n + 128])
                t = softplus(ch_ref[slot, 64 + 8 * b : 72 + 8 * b, 128 * n : 128 * n + 128])
                q = jnp.exp2(t * (-LOG2E / 512.0))
                tx = state[8 + b]
                nx = tx * q
                state[b] = state[b] + (tx - nx) * e
                state[8 + b] = nx
                ty = yt_ref[b, row : row + 8, :]
                ny = ty * q
                yc_ref[b, row : row + 8, :] = yc_ref[b, row : row + 8, :] + (ty - ny) * e
                yt_ref[b, row : row + 8, :] = ny

    chunks = 16 // GROUP

    def columns(k, carry):
        state = [zero] * BANDS + [one] * BANDS
        for g in range(chunks):
            ahead = g + 2
            views(g, state)
            second_layer((g + 1) % chunks)
            first_layer(ahead % chunks, k + ahead // chunks)
        second(k + 3)
        first(k + 5)
        colour = [state[b] + state[8 + b] * pltpu.roll(state[b], 64, 1) for b in range(BANDS)]
        clear = [state[8 + b] * pltpu.roll(state[8 + b], 64, 1) for b in range(BANDS)]
        image = jnp.transpose(jnp.concatenate(colour + clear, axis=0))
        j_ref[pl.ds(k, 64, stride=16), :] = image[0:64]
        return carry

    def lead_first(i, carry):
        first(i - 2)
        return carry

    def lead_second(i, carry):
        second(i - 1)
        return carry

    lax.fori_loop(0, 7, lead_first, 0)
    lax.fori_loop(0, 4, lead_second, 0)
    for b in range(BANDS):
        yc_ref[b] = jnp.zeros((128, 128), jnp.float32)
        yt_ref[b] = jnp.ones((128, 128), jnp.float32)
    first_layer(0, 0)
    first_layer(1, 0)
    second_layer(0)
    lax.fori_loop(0, 16, columns, 0)

    for b in range(BANDS):
        for h in range(2):
            colour = yc_ref[b, pl.ds(64 * h, 8, stride=8), :]
            clear = yt_ref[b, pl.ds(64 * h, 8, stride=8), :]
            for s in range(1, 8):
                colour = colour + clear * yc_ref[b, pl.ds(64 * h + s, 8, stride=8), :]
                clear = clear * yt_ref[b, pl.ds(64 * h + s, 8, stride=8), :]
            rs_ref[0, 16 * b + 8 * h : 16 * b + 8 * h + 8, :] = colour
            rs_ref[1, 16 * b + 8 * h : 16 * b + 8 * h + 8, :] = clear
    for kind in range(2):
        image = jnp.transpose(rs_ref[kind])
        for h in range(2):
            for p in range(8):
                r_ref[p, h, :, 128 * kind : 128 * kind + 128] = image[64 * h + 8 * p : 64 * h + 8 * p + 8]


def render_call(place, tb, w1, w2):
    vmem = pl.BlockSpec(memory_space=pltpu.VMEM)
    return pl.pallas_call(
        render,
        out_shape=(
            jax.ShapeDtypeStruct((1024, 128), jnp.float32),
            jax.ShapeDtypeStruct((8, 2, 8, 256), jnp.float32),
        ),
        in_specs=[pl.BlockSpec(memory_space=pltpu.SMEM), vmem, vmem, vmem],
        out_specs=(vmem, vmem),
        scratch_shapes=[
            pltpu.VMEM((20, 23, 8, 128), jnp.float32),
            pltpu.VMEM((18, 20, 8, 128), jnp.float32),
            pltpu.VMEM((18, 20, 8, 128), jnp.float32),
            pltpu.VMEM((18, 20, 8, 128), jnp.float32),
            pltpu.VMEM((2, 64, 128 * GROUP), jnp.bfloat16),
            pltpu.VMEM((2, 128, 128 * GROUP), jnp.float32),
            pltpu.VMEM((2, 128, 128 * GROUP), jnp.float32),
            pltpu.VMEM((8, 128, 128), jnp.float32),
            pltpu.VMEM((8, 128, 128), jnp.float32),
            pltpu.VMEM((2, 128, 128), jnp.float32),
        ],
        compiler_params=pltpu.CompilerParams(vmem_limit_bytes=20 << 20),
        name="render",
    )(place, tb, w1, w2)


def exchange(count_x, count_y, j_ref, r_ref, jr_ref, rr_ref, send_x, recv_x, send_y, recv_y):
    me_x = lax.axis_index("bx")
    me_y = lax.axis_index("by")

    def peer_x(hop):
        return lax.rem(me_x + hop, count_x)

    def peer_y(hop):
        return lax.rem(me_y + hop, count_y)

    barrier = pltpu.get_barrier_semaphore()

    def greet_x(hop, carry):
        pl.semaphore_signal(barrier, inc=1, device_id=(peer_x(hop), me_y), device_id_type=MESH)
        return carry

    def greet_y(hop, carry):
        pl.semaphore_signal(barrier, inc=1, device_id=(me_x, peer_y(hop)), device_id_type=MESH)
        return carry

    lax.fori_loop(1, count_x, greet_x, 0)
    lax.fori_loop(1, count_y, greet_y, 0)
    pl.semaphore_wait(barrier, count_x + count_y - 2)

    def copy_x(peer, source, hop):
        return pltpu.make_async_remote_copy(
            src_ref=j_ref.at[peer],
            dst_ref=jr_ref.at[source],
            send_sem=send_x.at[hop],
            recv_sem=recv_x.at[source],
            device_id=(peer, me_y),
            device_id_type=MESH,
        )

    def copy_y(peer, source, hop):
        return pltpu.make_async_remote_copy(
            src_ref=r_ref.at[peer],
            dst_ref=rr_ref.at[source],
            send_sem=send_y.at[hop],
            recv_sem=recv_y.at[source],
            device_id=(me_x, peer),
            device_id_type=MESH,
        )

    def send_all_y(hop, carry):
        copy_y(peer_y(hop), me_y, hop).start()
        return carry

    def send_all_x(hop, carry):
        copy_x(peer_x(hop), me_x, hop).start()
        return carry

    lax.fori_loop(1, count_x, send_all_x, 0)
    lax.fori_loop(1, count_y, send_all_y, 0)
    jr_ref[me_x] = j_ref[me_x]
    rr_ref[me_y] = r_ref[me_y]

    def wait_y(hop, carry):
        copy_y(me_y, peer_y(hop), hop).wait_recv()
        return carry

    def wait_x(hop, carry):
        copy_x(me_x, peer_x(hop), hop).wait_recv()
        return carry

    def sent_x(hop, carry):
        copy_x(peer_x(hop), me_x, hop).wait_send()
        return carry

    def sent_y(hop, carry):
        copy_y(peer_y(hop), me_y, hop).wait_send()
        return carry

    lax.fori_loop(1, count_x, sent_x, 0)
    lax.fori_loop(1, count_y, sent_y, 0)
    lax.fori_loop(1, count_y, wait_y, 0)
    lax.fori_loop(1, count_x, wait_x, 0)


def exchange_call(j, r):
    count_x = j.shape[0]
    count_y = r.shape[0]
    vmem = pl.BlockSpec(memory_space=pltpu.VMEM)
    return pl.pallas_call(
        functools.partial(exchange, count_x, count_y),
        out_shape=(
            jax.ShapeDtypeStruct(j.shape, jnp.float32),
            jax.ShapeDtypeStruct(r.shape, jnp.float32),
        ),
        in_specs=[vmem, vmem],
        out_specs=(vmem, vmem),
        scratch_shapes=[
            pltpu.SemaphoreType.DMA((count_x,)),
            pltpu.SemaphoreType.DMA((count_x,)),
            pltpu.SemaphoreType.DMA((count_y,)),
            pltpu.SemaphoreType.DMA((count_y,)),
        ],
        compiler_params=pltpu.CompilerParams(collective_id=1, has_side_effects=True),
        name="exchange",
    )(j, r)


def fold(count_x, count_y, jr_ref, rr_ref, vx_ref, vy_ref, at_ref):
    lane = lax.broadcasted_iota(jnp.int32, (32, 128), 1)
    low = lane < 64

    def over_y(s, pair):
        piece = rr_ref[s]
        return pair[0] + pair[1] * piece[:, 0:128], pair[1] * piece[:, 128:256]

    start = (jnp.zeros((16, 128), jnp.float32), jnp.ones((16, 128), jnp.float32))
    kinds = lax.fori_loop(0, count_y, over_y, start)
    lane8 = lanes_of()
    for kind in range(2):
        for b in range(BANDS):
            shift = (128 - 16 * b) % 128
            front = kinds[kind][0:8]
            back = kinds[kind][8:16]
            front = pltpu.roll(front, shift, 1) if shift else front
            back = pltpu.roll(back, shift + 16, 1) if shift < 112 else back
            vy_ref[8 * kind + b] = jnp.where(lane8 < 16, front, back)[:, 0:32]

    def over(s, pair):
        front, clear = pair
        piece = jr_ref[s]
        both = jnp.where(low, pltpu.roll(piece, 64, 1), piece)
        return jnp.where(low, front, 0.0) + clear * piece, clear * both

    start = (jnp.zeros((32, 128), jnp.float32), jnp.ones((32, 128), jnp.float32))
    image, _ = lax.fori_loop(0, count_x, over, start)
    at_ref[0:32, :] = image
    at_ref[32:128, :] = jnp.zeros((96, 128), jnp.float32)
    at_ref[...] = jnp.transpose(at_ref[...])
    line = lax.broadcasted_iota(jnp.int32, (16, 128), 1)
    for z in range(2):
        row = jnp.zeros((16, 128), jnp.float32)
        for s in range(8):
            part = at_ref[pl.ds(s, 16, stride=8), :]
            shift = (16 * s - 16 * z) % 128
            part = pltpu.roll(part, shift, 1) if shift else part
            row = jnp.where((line >> 4) == s, part, row)
        vx_ref[:, z, :] = row


def fold_call(jr, rr):
    vmem = pl.BlockSpec(memory_space=pltpu.VMEM)
    return pl.pallas_call(
        functools.partial(fold, jr.shape[0], rr.shape[0]),
        out_shape=(
            jax.ShapeDtypeStruct((16, 2, 128), jnp.float32),
            jax.ShapeDtypeStruct((16, 8, 32), jnp.float32),
        ),
        in_specs=[vmem, vmem],
        out_specs=(vmem, vmem),
        scratch_shapes=[pltpu.VMEM((128, 128), jnp.float32)],
        name="fold",
    )(jr, rr)


def spread(weights, scale):
    rows, cols = weights.shape
    eye = jnp.eye(8, dtype=jnp.float32)
    big = (weights.astype(jnp.float32) * scale)[:, None, :, None] * eye[None, :, None, :]
    return big.reshape(rows * 8, cols * 8).astype(jnp.bfloat16)


def body(scalar_field, transfer_in, transfer_out):
    count_x = lax.axis_size("bx")
    count_y = lax.axis_size("by")
    tb = halo_call(scalar_field.reshape(2048, 128), count_x, count_y)
    place = jnp.stack(
        [lax.axis_index("bx"), lax.axis_index("by"), jnp.int32(32 * count_x), jnp.int32(128 * count_y)]
    ).astype(jnp.int32)
    j, r = render_call(place, tb, spread(transfer_in, 0.5), spread(transfer_out, 1.0))
    slab = 64 // count_x
    jr, rr = exchange_call(j.reshape(count_x, slab * 16, 128), r.reshape(count_y, 128 // count_y, 256))
    vx, vy = fold_call(jr, rr)
    return (vx.reshape(2, 8, slab, 128), vy.reshape(2, 8, 8, 32))


def solution(mesh):
    return jax.shard_map(
        body,
        mesh=mesh,
        in_specs=(P(None, "bx", "by"), P(), P()),
        out_specs=(P(None, None, "bx", "by"), P(None, None, "by", "bx")),
        check_vma=False,
    )
```

```python
import functools

import jax
import jax.numpy as jnp
from jax import lax
from jax.experimental import pallas as pl
from jax.experimental.pallas import tpu as pltpu
from jax.sharding import PartitionSpec as P

BANDS = 8
HID = 16
FEAT = 8
LOG2E = 1.4426950408889634
MESH = pl.DeviceIdType.MESH
GROUP = 4


def lanes_of():
    return lax.broadcasted_iota(jnp.int32, (8, 128), 1)


def softplus(v):
    grown = jnp.exp2(jnp.minimum(v * LOG2E, 126.0))
    return jnp.maximum(v, jnp.log(1.0 + grown))


def widen(big_ref, weights_ref, scale):
    rows, cols = weights_ref.shape
    up = lax.broadcasted_iota(jnp.int32, (8 * rows, rows), 0) >> 3
    up = (up == lax.broadcasted_iota(jnp.int32, (8 * rows, rows), 1)).astype(jnp.float32)
    out = lax.broadcasted_iota(jnp.int32, (cols, 8 * cols), 1) >> 3
    out = (out == lax.broadcasted_iota(jnp.int32, (cols, 8 * cols), 0)).astype(jnp.float32)
    tall = jnp.dot(up.astype(jnp.bfloat16), weights_ref[...], preferred_element_type=jnp.float32)
    wide = jnp.dot(tall.astype(jnp.bfloat16), out.astype(jnp.bfloat16), preferred_element_type=jnp.float32)
    at_row = lax.broadcasted_iota(jnp.int32, wide.shape, 0) & 7
    at_col = lax.broadcasted_iota(jnp.int32, wide.shape, 1) & 7
    big_ref[...] = jnp.where(at_row == at_col, wide * scale, 0.0).astype(jnp.bfloat16)


def march(
    count_x, count_y, f_ref, win_ref, wout_ref, vx_ref, vy_ref,
    tb_ref, xs_ref, xr_ref, yr_ref, cr_ref,
    w1_ref, w2_ref, s1_ref, p_ref, b_ref, d_ref, x_ref, u_ref, ch_ref, yc_ref, yt_ref, rs_ref,
    j_ref, jr_ref, r_ref, rr_ref, at_ref,
    sx, rx, sy, ry, sc, rc, send_x, recv_x, send_y, recv_y,
):
    me_x = lax.axis_index("bx")
    me_y = lax.axis_index("by")
    xs = (lax.rem(me_x + count_x - 1, count_x), lax.rem(me_x + 1, count_x))
    ys = (lax.rem(me_y + count_y - 1, count_y), lax.rem(me_y + 1, count_y))

    def peer_x(hop):
        return lax.rem(me_x + hop, count_x)

    def peer_y(hop):
        return lax.rem(me_y + hop, count_y)

    barrier = pltpu.get_barrier_semaphore()

    def greet_x(hop, carry):
        pl.semaphore_signal(barrier, inc=1, device_id=(peer_x(hop), me_y), device_id_type=MESH)
        return carry

    def greet_y(hop, carry):
        pl.semaphore_signal(barrier, inc=1, device_id=(me_x, peer_y(hop)), device_id_type=MESH)
        return carry

    for x in xs:
        for y in ys:
            pl.semaphore_signal(barrier, inc=1, device_id=(x, y), device_id_type=MESH)
    lax.fori_loop(1, count_x, greet_x, 0)
    lax.fori_loop(1, count_y, greet_y, 0)

    def plane(x):
        return f_ref[pl.ds(x, 64, stride=32), :]

    for i in range(3):
        xs_ref[0, i] = plane(i)
        xs_ref[1, i] = plane(29 + i)
    widen(w1_ref, win_ref, 0.5)
    widen(w2_ref, wout_ref, 1.0)
    pl.semaphore_wait(barrier, count_x + count_y + 2)

    copies = []
    for side in range(2):
        copies.append(
            pltpu.make_async_remote_copy(
                src_ref=xs_ref.at[side],
                dst_ref=xr_ref.at[1 - side],
                send_sem=sx.at[side],
                recv_sem=rx.at[1 - side],
                device_id=(xs[side], me_y),
                device_id_type=MESH,
            )
        )
        copies[-1].start()

    def turn(x, front, back):
        tb_ref[x + 3, 8:136, :] = jnp.transpose(jnp.concatenate([front, back], axis=0))

    edges = (pl.ds(8, 8), pl.ds(128, 8))
    ends = (pl.ds(3, 3), pl.ds(16, 3))
    for x in (0, 1, 2, 13, 14, 15):
        turn(x, plane(x), plane(16 + x))
    for side in range(2):
        for part in range(2):
            copies.append(
                pltpu.make_async_remote_copy(
                    src_ref=tb_ref.at[ends[side], edges[part]],
                    dst_ref=cr_ref.at[2 * (1 - side) + (1 - part)],
                    send_sem=sc.at[2 * side + part],
                    recv_sem=rc.at[2 * (1 - side) + (1 - part)],
                    device_id=(xs[side], ys[part]),
                    device_id_type=MESH,
                )
            )
            copies[-1].start()

    def rest(x, carry):
        turn(x, plane(x), plane(16 + x))
        return carry

    lax.fori_loop(3, 13, rest, 0)
    for part in range(2):
        copies.append(
            pltpu.make_async_remote_copy(
                src_ref=tb_ref.at[pl.ds(3, 16), edges[part]],
                dst_ref=yr_ref.at[1 - part],
                send_sem=sy.at[part],
                recv_sem=ry.at[1 - part],
                device_id=(me_x, ys[part]),
                device_id_type=MESH,
            )
        )
        copies[-1].start()

    inner_x = (me_x > 0, me_x < count_x - 1)
    inner_y = (me_y > 0, me_y < count_y - 1)
    copies[0].wait_recv()
    copies[1].wait_recv()
    for i in range(3):
        turn(i - 3, jnp.where(inner_x[0], xr_ref[0, i], 0.0), plane(13 + i))
        turn(16 + i, plane(16 + i), jnp.where(inner_x[1], xr_ref[1, i], 0.0))
    for copy in copies[2:]:
        copy.wait_recv()
    low = lanes_of() < 64
    rims = (pl.ds(0, 8), pl.ds(136, 8))
    for part in range(2):
        for x in range(16):
            tb_ref[x + 3, rims[part], :] = jnp.where(inner_y[part], yr_ref[part, x], 0.0)
        for i in range(3):
            far = jnp.where(inner_x[0], cr_ref[part, i], 0.0)
            edge = jnp.where(low, pltpu.roll(far, 64, 1), pltpu.roll(yr_ref[part, 13 + i], 64, 1))
            tb_ref[i, rims[part], :] = jnp.where(inner_y[part], edge, 0.0)
            far = jnp.where(inner_x[1], cr_ref[2 + part, i], 0.0)
            edge = jnp.where(low, pltpu.roll(yr_ref[part, i], 64, 1), pltpu.roll(far, 64, 1))
            tb_ref[19 + i, rims[part], :] = jnp.where(inner_y[part], edge, 0.0)
    for copy in copies:
        copy.wait_send()

    lane = lanes_of()
    seg = lax.broadcasted_iota(jnp.int32, (8, 128), 0)
    z = lane & 63
    half = lane >> 6
    top = z == 0
    bottom = z == 63
    full_x = 32 * count_x
    full_y = 128 * count_y
    at_x = me_x * 32 + half * 16
    at_y = me_y * 128 + seg * 16

    def above(v):
        return jnp.where(top, 0.0, pltpu.roll(v, 1, 1))

    def below(v):
        return jnp.where(bottom, 0.0, pltpu.roll(v, 127, 1))

    def inside(xp, yp):
        gy = at_y + yp
        ok = (gy >= 0) & (gy < full_y)
        if xp < 0:
            ok = ok & (at_x + xp >= 0)
        if xp > 15:
            ok = ok & (at_x + xp < full_x)
        return ok

    def field(xp, yp):
        return tb_ref[xp + 3, pl.ds(yp + 8, 8, stride=16), :]

    def first(yp):
        mid = [field(xp, yp) for xp in range(-3, 19)]
        for k in range(20):
            c = mid[k + 1]
            near = field(k - 2, yp - 1) + field(k - 2, yp + 1)
            near = near + (mid[k] + mid[k + 2]) + (above(c) + below(c))
            s1_ref[k, yp + 2] = jnp.where(inside(k - 2, yp), 0.4 * c + 0.1 * near, 0.0)

    def second(yp):
        mid = [s1_ref[k, yp + 2] for k in range(20)]
        for k in range(18):
            c = mid[k + 1]
            near = s1_ref[k + 1, yp + 1] + s1_ref[k + 1, yp + 3]
            near = near + (mid[k] + mid[k + 2]) + (above(c) + below(c))
            s = jnp.where(inside(k - 1, yp), 0.4 * c + 0.1 * near, 0.0)
            up, down = above(s), below(s)
            p_ref[k, yp + 1] = s
            b_ref[k, yp + 1] = 2.0 * s + (up + down)
            d_ref[k, yp + 1] = down - up

    one = jnp.ones((8, 128), jnp.float32)
    zero = jnp.zeros((8, 128), jnp.float32)

    def features(i, k):
        s = p_ref[i, k]
        a = p_ref[i + 1, k + 1] - p_ref[i - 1, k - 1]
        c = p_ref[i + 1, k - 1] - p_ref[i - 1, k + 1]
        gx = (b_ref[i + 1, k] - b_ref[i - 1, k] + (a + c)) * (1.0 / 3.0)
        gy = (b_ref[i, k + 1] - b_ref[i, k - 1] + (a - c)) * (1.0 / 3.0)
        d = d_ref[i, k]
        gz = (d + d + (d_ref[i + 1, k] + d_ref[i - 1, k]) + (d_ref[i, k + 1] + d_ref[i, k - 1])) * (1.0 / 3.0)
        q = 1.0 + gx * gx + gy * gy + gz * gz
        m = q * lax.rsqrt(q)
        return s, gx, gy, gz, m, s * m, s * s, one

    def first_layer(g, k):
        slot = g
        for n in range(GROUP):
            rows = features(g * GROUP + n + 1, k + 1)
            for f in range(0, FEAT, 2):
                pair = jnp.concatenate([rows[f], rows[f + 1]], axis=0)
                x_ref[slot, 8 * f : 8 * f + 16, 128 * n : 128 * n + 128] = pair.astype(jnp.bfloat16)
        u_ref[slot] = jnp.dot(w1_ref[...], x_ref[slot], preferred_element_type=jnp.float32)

    def second_layer(g):
        slot = g
        u = u_ref[slot]
        hidden = (u + u * jnp.tanh(u)).astype(jnp.bfloat16)
        ch_ref[slot] = jnp.dot(w2_ref[...], hidden, preferred_element_type=jnp.float32)

    def views(g, state):
        slot = g
        for n in range(GROUP):
            row = (g * GROUP + n) * 8
            for b in range(BANDS):
                e = softplus(ch_ref[slot, 8 * b : 8 * b + 8, 128 * n : 128 * n + 128])
                t = softplus(ch_ref[slot, 64 + 8 * b : 72 + 8 * b, 128 * n : 128 * n + 128])
                q = jnp.exp2(t * (-LOG2E / 512.0))
                tx = state[8 + b]
                nx = tx * q
                state[b] = state[b] + (tx - nx) * e
                state[8 + b] = nx
                ty = yt_ref[b, row : row + 8, :]
                ny = ty * q
                yc_ref[b, row : row + 8, :] = yc_ref[b, row : row + 8, :] + (ty - ny) * e
                yt_ref[b, row : row + 8, :] = ny

    chunks = 16 // GROUP

    def column(k):
        state = [zero] * BANDS + [one] * BANDS
        for g in range(chunks):
            views(g, state)
            second_layer((g + 2) % chunks)
            first_layer((g + 4) % chunks, k + (g + 4) // chunks)
        second(k + 3)
        first(k + 5)
        colour = [state[b] + state[8 + b] * pltpu.roll(state[b], 64, 1) for b in range(BANDS)]
        clear = [state[8 + b] * pltpu.roll(state[8 + b], 64, 1) for b in range(BANDS)]
        image = jnp.transpose(jnp.concatenate(colour + clear, axis=0))
        j_ref[pl.ds((k // 4) * 256 + k % 4, 64, stride=4), :] = image[0:64]

    def lead_first(i, carry):
        first(i - 2)
        return carry

    def lead_second(i, carry):
        second(i - 1)
        return carry

    def slab(start):
        return pl.ds(pl.multiple_of(start, 8), 8)

    def send_slabs(c):
        def one_peer(hop, carry):
            peer = peer_x(hop)
            pltpu.make_async_remote_copy(
                src_ref=j_ref.at[slab(c * 256 + peer * 8)],
                dst_ref=jr_ref.at[slab(c * 256 + me_x * 8)],
                send_sem=send_x.at[c],
                recv_sem=recv_x.at[c],
                device_id=(peer, me_y),
                device_id_type=MESH,
            ).start()
            return carry

        lax.fori_loop(1, count_x, one_peer, 0)
        jr_ref[slab(c * 256 + me_x * 8), :] = j_ref[slab(c * 256 + me_x * 8), :]

    def slabs_moved(c):
        many = pl.ds(0, (count_x - 1) * 8)
        return pltpu.make_async_remote_copy(
            src_ref=j_ref.at[many],
            dst_ref=jr_ref.at[many],
            send_sem=send_x.at[c],
            recv_sem=recv_x.at[c],
            device_id=(xs[1], me_y),
            device_id_type=MESH,
        )

    def rows_moved():
        many = pl.ds(0, count_y - 1)
        return pltpu.make_async_remote_copy(
            src_ref=r_ref.at[many],
            dst_ref=rr_ref.at[many],
            send_sem=send_y,
            recv_sem=recv_y,
            device_id=(me_x, ys[1]),
            device_id_type=MESH,
        )

    lax.fori_loop(0, 7, lead_first, 0)
    lax.fori_loop(0, 4, lead_second, 0)
    for b in range(BANDS):
        yc_ref[b] = jnp.zeros((128, 128), jnp.float32)
        yt_ref[b] = jnp.ones((128, 128), jnp.float32)
    for g in range(4):
        first_layer(g, 0)
    for g in range(2):
        second_layer(g)

    def part(c, carry):
        def one_column(n, carry):
            column(4 * c + n)
            return carry

        lax.fori_loop(0, 4, one_column, 0)
        send_slabs(c)
        return carry

    lax.fori_loop(0, 4, part, 0)

    for b in range(BANDS):
        for h in range(2):
            colour = yc_ref[b, pl.ds(64 * h, 8, stride=8), :]
            clear = yt_ref[b, pl.ds(64 * h, 8, stride=8), :]
            for s in range(1, 8):
                colour = colour + clear * yc_ref[b, pl.ds(64 * h + s, 8, stride=8), :]
                clear = clear * yt_ref[b, pl.ds(64 * h + s, 8, stride=8), :]
            rs_ref[0, 16 * b + 8 * h : 16 * b + 8 * h + 8, :] = colour
            rs_ref[1, 16 * b + 8 * h : 16 * b + 8 * h + 8, :] = clear
    for kind in range(2):
        image = jnp.transpose(rs_ref[kind])
        for h in range(2):
            for p in range(8):
                r_ref[p, 8 * h : 8 * h + 8, 128 * kind : 128 * kind + 128] = image[64 * h + 8 * p : 64 * h + 8 * p + 8]


    def send_rows(hop, carry):
        peer = peer_y(hop)
        pltpu.make_async_remote_copy(
            src_ref=r_ref.at[peer],
            dst_ref=rr_ref.at[me_y],
            send_sem=send_y,
            recv_sem=recv_y,
            device_id=(me_x, peer),
            device_id_type=MESH,
        ).start()
        return carry

    lax.fori_loop(1, count_y, send_rows, 0)
    rr_ref[me_y] = r_ref[me_y]

    at_ref[...] = jnp.zeros_like(at_ref)

    def fold_x(c):
        slabs_moved(c).wait_recv()
        image, clear = zero, one
        for s in range(count_x):
            piece = jr_ref[c * 256 + s * 8 : c * 256 + s * 8 + 8, :]
            both = jnp.where(low, pltpu.roll(piece, 64, 1), piece)
            image = jnp.where(low, image, 0.0) + clear * piece
            clear = clear * both
        for z in range(2):
            at_ref[16 * z + 4 * c : 16 * z + 4 * c + 4, :] = image[4 * z : 4 * z + 4]

    for c in range(3):
        fold_x(c)

    rows_moved().wait_recv()
    colour, clear = rr_ref[0, :, 0:128], rr_ref[0, :, 128:256]
    for s in range(1, count_y):
        colour = colour + clear * rr_ref[s, :, 0:128]
        clear = clear * rr_ref[s, :, 128:256]
    for kind, image in enumerate((colour, clear)):
        for b in range(BANDS):
            shift = (128 - 16 * b) % 128
            front = image[0:8]
            back = image[8:16]
            front = pltpu.roll(front, shift, 1) if shift else front
            back = pltpu.roll(back, shift + 16, 1) if shift < 112 else back
            vy_ref[8 * kind + b] = jnp.where(lane < 16, front, back)[:, 0:32]

    fold_x(3)
    at_ref[...] = jnp.transpose(at_ref[...])
    line = lax.broadcasted_iota(jnp.int32, (16, 128), 1)
    for z in range(2):
        row = jnp.zeros((16, 128), jnp.float32)
        for s in range(8):
            piece = at_ref[pl.ds(s, 16, stride=8), :]
            shift = (16 * s - 16 * z) % 128
            piece = pltpu.roll(piece, shift, 1) if shift else piece
            row = jnp.where((line >> 4) == s, piece, row)
        vx_ref[:, z, :] = row

    for c in range(4):
        slabs_moved(c).wait_send()
    rows_moved().wait_send()


def march_call(field, transfer_in, transfer_out, count_x, count_y):
    vmem = pl.BlockSpec(memory_space=pltpu.VMEM)

    def held(*shape, dtype=jnp.float32):
        return pltpu.VMEM(shape, dtype)

    return pl.pallas_call(
        functools.partial(march, count_x, count_y),
        out_shape=(
            jax.ShapeDtypeStruct((16, 2, 128), jnp.float32),
            jax.ShapeDtypeStruct((16, 8, 32), jnp.float32),
        ),
        in_specs=[vmem] * 3,
        out_specs=(vmem, vmem),
        scratch_shapes=[
            held(22, 144, 128),
            held(2, 3, 64, 128),
            held(2, 3, 64, 128),
            held(2, 16, 8, 128),
            held(4, 3, 8, 128),
            held(128, 64, dtype=jnp.bfloat16),
            held(128, 128, dtype=jnp.bfloat16),
            held(20, 23, 8, 128),
            held(18, 20, 8, 128),
            held(18, 20, 8, 128),
            held(18, 20, 8, 128),
            held(16 // GROUP, 64, 128 * GROUP, dtype=jnp.bfloat16),
            held(16 // GROUP, 128, 128 * GROUP),
            held(16 // GROUP, 128, 128 * GROUP),
            held(8, 128, 128),
            held(8, 128, 128),
            held(2, 128, 128),
            held(1024, 128),
            held(1024, 128),
            held(8, 16, 256),
            held(8, 16, 256),
            held(128, 128),
            pltpu.SemaphoreType.DMA((2,)),
            pltpu.SemaphoreType.DMA((2,)),
            pltpu.SemaphoreType.DMA((2,)),
            pltpu.SemaphoreType.DMA((2,)),
            pltpu.SemaphoreType.DMA((4,)),
            pltpu.SemaphoreType.DMA((4,)),
            pltpu.SemaphoreType.DMA((4,)),
            pltpu.SemaphoreType.DMA((4,)),
            pltpu.SemaphoreType.DMA,
            pltpu.SemaphoreType.DMA,
        ],
        compiler_params=pltpu.CompilerParams(collective_id=0, has_side_effects=True, vmem_limit_bytes=40 << 20),
        name="march",
    )(field, transfer_in, transfer_out)


def emit(ax_ref, ay_ref, vx_ref, vy_ref):
    vx_ref[...] = ax_ref[...]
    vy_ref[...] = ay_ref[...]


def emit_call(ax, ay):
    vmem = pl.BlockSpec(memory_space=pltpu.VMEM)
    return pl.pallas_call(
        emit,
        out_shape=(jax.ShapeDtypeStruct(ax.shape, ax.dtype), jax.ShapeDtypeStruct(ay.shape, ay.dtype)),
        in_specs=[vmem, vmem],
        out_specs=(vmem, vmem),
        name="emit",
    )(ax, ay)


def body(scalar_field, transfer_in, transfer_out):
    count_x = lax.axis_size("bx")
    count_y = lax.axis_size("by")
    ax, ay = march_call(scalar_field.reshape(2048, 128), transfer_in, transfer_out, count_x, count_y)
    vx, vy = emit_call(ax, ay)
    return (vx.reshape(2, 8, 2, 128), vy.reshape(2, 8, 8, 32))


def solution(mesh):
    return jax.shard_map(
        body,
        mesh=mesh,
        in_specs=(P(None, "bx", "by"), P(), P()),
        out_specs=(P(None, None, "bx", "by"), P(None, None, "by", "bx")),
        check_vma=False,
    )
```

```python
import functools

import jax
import jax.numpy as jnp
from jax import lax
from jax.experimental import pallas as pl
from jax.experimental.pallas import tpu as pltpu
from jax.sharding import PartitionSpec as P

BANDS = 8
HID = 16
FEAT = 8
LOG2E = 1.4426950408889634
LN2 = 0.6931471805599453
MESH = pl.DeviceIdType.MESH
GROUP = 4


def lanes_of():
    return lax.broadcasted_iota(jnp.int32, (8, 128), 1)


def softplus(v):
    v = v * LOG2E
    return jnp.maximum(v, lax.log2(1.0 + jnp.exp2(jnp.minimum(v, 126.0))))


def widen(big_ref, weights_ref, scale):
    cols, rows = weights_ref.shape
    up = lax.broadcasted_iota(jnp.int32, (8 * rows, rows), 0) >> 3
    up = (up == lax.broadcasted_iota(jnp.int32, (8 * rows, rows), 1)).astype(jnp.float32)
    out = lax.broadcasted_iota(jnp.int32, (cols, 8 * cols), 1) >> 3
    out = (out == lax.broadcasted_iota(jnp.int32, (cols, 8 * cols), 0)).astype(jnp.float32)
    tall = lax.dot_general(
        up.astype(jnp.bfloat16), weights_ref[...], (((1,), (1,)), ((), ())), preferred_element_type=jnp.float32
    )
    wide = jnp.dot(tall.astype(jnp.bfloat16), out.astype(jnp.bfloat16), preferred_element_type=jnp.float32)
    at_row = lax.broadcasted_iota(jnp.int32, wide.shape, 0) & 7
    at_col = lax.broadcasted_iota(jnp.int32, wide.shape, 1) & 7
    big_ref[...] = jnp.where(at_row == at_col, wide * scale, 0.0).astype(jnp.bfloat16)


def march(
    count_x, count_y, field_ref, win_ref, wout_ref, vx_ref, vy_ref,
    tb_ref, xs_ref, xr_ref, yr_ref, cr_ref,
    w1_ref, w2_ref, s1_ref, p_ref, b_ref, d_ref, x_ref, u_ref, ch_ref, yc_ref, yt_ref, rs_ref,
    j_ref, jr_ref, r_ref, rr_ref, at_ref, st_ref, f_ref, load,
    sx, rx, sy, ry, sc, rc, send_x, recv_x, send_y, recv_y,
):
    me_x = lax.axis_index("bx")
    me_y = lax.axis_index("by")
    xs = (lax.rem(me_x + count_x - 1, count_x), lax.rem(me_x + 1, count_x))
    ys = (lax.rem(me_y + count_y - 1, count_y), lax.rem(me_y + 1, count_y))

    def peer_x(hop):
        return lax.rem(me_x + hop, count_x)

    def peer_y(hop):
        return lax.rem(me_y + hop, count_y)

    fetch = pltpu.make_async_copy(field_ref, f_ref, load)
    fetch.start()
    barrier = pltpu.get_barrier_semaphore()

    def greet_x(hop, carry):
        pl.semaphore_signal(barrier, inc=1, device_id=(peer_x(hop), me_y), device_id_type=MESH)
        return carry

    def greet_y(hop, carry):
        pl.semaphore_signal(barrier, inc=1, device_id=(me_x, peer_y(hop)), device_id_type=MESH)
        return carry

    for x in xs:
        for y in ys:
            pl.semaphore_signal(barrier, inc=1, device_id=(x, y), device_id_type=MESH)
    lax.fori_loop(1, count_x, greet_x, 0)
    lax.fori_loop(1, count_y, greet_y, 0)

    def plane(x):
        return f_ref[pl.ds(x, 64, stride=32), :]

    widen(w1_ref, win_ref, 0.5)
    widen(w2_ref, wout_ref, 1.0)
    fetch.wait()
    for i in range(3):
        xs_ref[0, i] = plane(i)
        xs_ref[1, i] = plane(29 + i)
    pl.semaphore_wait(barrier, count_x + count_y + 2)

    copies = []
    for side in range(2):
        copies.append(
            pltpu.make_async_remote_copy(
                src_ref=xs_ref.at[side],
                dst_ref=xr_ref.at[1 - side],
                send_sem=sx.at[side],
                recv_sem=rx.at[1 - side],
                device_id=(xs[side], me_y),
                device_id_type=MESH,
            )
        )
        copies[-1].start()

    def turn(x, front, back):
        tb_ref[x + 3, 8:136, :] = jnp.transpose(jnp.concatenate([front, back], axis=0))

    edges = (pl.ds(8, 8), pl.ds(128, 8))
    ends = (pl.ds(3, 3), pl.ds(16, 3))
    for x in (0, 1, 2, 13, 14, 15):
        turn(x, plane(x), plane(16 + x))
    for side in range(2):
        for part in range(2):
            copies.append(
                pltpu.make_async_remote_copy(
                    src_ref=tb_ref.at[ends[side], edges[part]],
                    dst_ref=cr_ref.at[2 * (1 - side) + (1 - part)],
                    send_sem=sc.at[2 * side + part],
                    recv_sem=rc.at[2 * (1 - side) + (1 - part)],
                    device_id=(xs[side], ys[part]),
                    device_id_type=MESH,
                )
            )
            copies[-1].start()

    for x in range(3, 13):
        turn(x, plane(x), plane(16 + x))
    for part in range(2):
        copies.append(
            pltpu.make_async_remote_copy(
                src_ref=tb_ref.at[pl.ds(3, 16), edges[part]],
                dst_ref=yr_ref.at[1 - part],
                send_sem=sy.at[part],
                recv_sem=ry.at[1 - part],
                device_id=(me_x, ys[part]),
                device_id_type=MESH,
            )
        )
        copies[-1].start()

    inner_x = (me_x > 0, me_x < count_x - 1)
    inner_y = (me_y > 0, me_y < count_y - 1)
    copies[0].wait_recv()
    copies[1].wait_recv()
    for i in range(3):
        turn(i - 3, jnp.where(inner_x[0], xr_ref[0, i], 0.0), plane(13 + i))
        turn(16 + i, plane(16 + i), jnp.where(inner_x[1], xr_ref[1, i], 0.0))
    for copy in copies[2:]:
        copy.wait_recv()
    low = lanes_of() < 64
    rims = (pl.ds(0, 8), pl.ds(136, 8))
    for part in range(2):
        for x in range(16):
            tb_ref[x + 3, rims[part], :] = jnp.where(inner_y[part], yr_ref[part, x], 0.0)
        for i in range(3):
            far = jnp.where(inner_x[0], cr_ref[part, i], 0.0)
            edge = jnp.where(low, pltpu.roll(far, 64, 1), pltpu.roll(yr_ref[part, 13 + i], 64, 1))
            tb_ref[i, rims[part], :] = jnp.where(inner_y[part], edge, 0.0)
            far = jnp.where(inner_x[1], cr_ref[2 + part, i], 0.0)
            edge = jnp.where(low, pltpu.roll(yr_ref[part, i], 64, 1), pltpu.roll(far, 64, 1))
            tb_ref[19 + i, rims[part], :] = jnp.where(inner_y[part], edge, 0.0)
    for copy in copies:
        copy.wait_send()

    lane = lanes_of()
    seg = lax.broadcasted_iota(jnp.int32, (8, 128), 0)
    z = lane & 63
    half = lane >> 6
    top = z == 0
    bottom = z == 63
    full_x = 32 * count_x
    full_y = 128 * count_y
    at_x = me_x * 32 + half * 16
    at_y = me_y * 128 + seg * 16

    def above(v):
        return jnp.where(top, 0.0, pltpu.roll(v, 1, 1))

    def below(v):
        return jnp.where(bottom, 0.0, pltpu.roll(v, 127, 1))

    def inside(xp, yp):
        gy = at_y + yp
        ok = (gy >= 0) & (gy < full_y)
        if xp < 0:
            ok = ok & (at_x + xp >= 0)
        if xp > 15:
            ok = ok & (at_x + xp < full_x)
        return ok

    def field(xp, yp):
        return tb_ref[xp + 3, pl.ds(yp + 8, 8, stride=16), :]

    def first(yp):
        mid = [field(xp, yp) for xp in range(-3, 19)]
        for k in range(20):
            c = mid[k + 1]
            near = field(k - 2, yp - 1) + field(k - 2, yp + 1)
            near = near + (mid[k] + mid[k + 2]) + (above(c) + below(c))
            s1_ref[k, yp + 2] = jnp.where(inside(k - 2, yp), 0.4 * c + 0.1 * near, 0.0)

    def second(yp):
        mid = [s1_ref[k, yp + 2] for k in range(20)]
        for k in range(18):
            c = mid[k + 1]
            near = s1_ref[k + 1, yp + 1] + s1_ref[k + 1, yp + 3]
            near = near + (mid[k] + mid[k + 2]) + (above(c) + below(c))
            s = jnp.where(inside(k - 1, yp), 0.4 * c + 0.1 * near, 0.0)
            up, down = above(s), below(s)
            p_ref[k, yp + 1] = s
            b_ref[k, yp + 1] = 2.0 * s + (up + down)
            d_ref[k, yp + 1] = down - up

    one = jnp.ones((8, 128), jnp.float32)
    zero = jnp.zeros((8, 128), jnp.float32)

    def features(i, k):
        s = p_ref[i, k]
        a = p_ref[i + 1, k + 1] - p_ref[i - 1, k - 1]
        c = p_ref[i + 1, k - 1] - p_ref[i - 1, k + 1]
        gx = (b_ref[i + 1, k] - b_ref[i - 1, k] + (a + c)) * (1.0 / 3.0)
        gy = (b_ref[i, k + 1] - b_ref[i, k - 1] + (a - c)) * (1.0 / 3.0)
        d = d_ref[i, k]
        gz = (d + d + (d_ref[i + 1, k] + d_ref[i - 1, k]) + (d_ref[i, k + 1] + d_ref[i, k - 1])) * (1.0 / 3.0)
        q = 1.0 + gx * gx + gy * gy + gz * gz
        m = q * lax.rsqrt(q)
        return s, gx, gy, gz, m, s * m, s * s, one

    def first_layer(g, k):
        slot = g
        for n in range(GROUP):
            rows = features(g * GROUP + n + 1, k + 1)
            for f in range(0, FEAT, 2):
                pair = jnp.concatenate([rows[f], rows[f + 1]], axis=0)
                x_ref[slot, 8 * f : 8 * f + 16, 128 * n : 128 * n + 128] = pair.astype(jnp.bfloat16)
        u_ref[slot] = jnp.dot(w1_ref[...], x_ref[slot], preferred_element_type=jnp.float32)

    def second_layer(g):
        slot = g
        u = u_ref[slot]
        hidden = (u + u * jnp.tanh(u)).astype(jnp.bfloat16)
        ch_ref[slot] = jnp.dot(w2_ref[...], hidden, preferred_element_type=jnp.float32)

    def views(g, state):
        slot = g
        for n in range(GROUP):
            row = (g * GROUP + n) * 8
            for b in range(BANDS):
                e = softplus(ch_ref[slot, 8 * b : 8 * b + 8, 128 * n : 128 * n + 128])
                t = softplus(ch_ref[slot, 64 + 8 * b : 72 + 8 * b, 128 * n : 128 * n + 128])
                q = jnp.exp2(t * (-1.0 / 512.0))
                tx = state[8 + b]
                nx = tx * q
                state[b] = state[b] + (tx - nx) * e
                state[8 + b] = nx
                ty = yt_ref[b, row : row + 8, :]
                ny = ty * q
                yc_ref[b, row : row + 8, :] = yc_ref[b, row : row + 8, :] + (ty - ny) * e
                yt_ref[b, row : row + 8, :] = ny

    chunks = 16 // GROUP

    def deliver(row):
        state = [st_ref[b] for b in range(2 * BANDS)]
        colour = [(state[b] + state[8 + b] * pltpu.roll(state[b], 64, 1)) * LN2 for b in range(BANDS)]
        clear = [state[8 + b] * pltpu.roll(state[8 + b], 64, 1) for b in range(BANDS)]
        image = jnp.transpose(jnp.concatenate(colour + clear, axis=0))
        j_ref[pl.ds(row, 64, stride=4), :] = image[0:64]

    def column(k):
        past = (k + 15) // 16
        deliver(past * (((k + 3) // 4 - 1) * 256 + (k + 3) % 4) + (1 - past) * 1024)
        state = [zero] * BANDS + [one] * BANDS
        for g in range(chunks):
            views(g, state)
            second_layer((g + 2) % chunks)
            first_layer((g + 4) % chunks, k + (g + 4) // chunks)
        second(k + 3)
        first(k + 5)
        for b in range(2 * BANDS):
            st_ref[b] = state[b]

    def slab(start):
        return pl.ds(pl.multiple_of(start, 8), 8)

    def send_slabs(c):
        def one_peer(hop, carry):
            peer = peer_x(hop)
            pltpu.make_async_remote_copy(
                src_ref=j_ref.at[slab(c * 256 + peer * 8)],
                dst_ref=jr_ref.at[slab(c * 256 + me_x * 8)],
                send_sem=send_x.at[c],
                recv_sem=recv_x.at[c],
                device_id=(peer, me_y),
                device_id_type=MESH,
            ).start()
            return carry

        for hop in range(1, count_x):
            one_peer(hop, 0)
        jr_ref[slab(c * 256 + me_x * 8), :] = j_ref[slab(c * 256 + me_x * 8), :]

    def slabs_moved(c):
        many = pl.ds(0, (count_x - 1) * 8)
        return pltpu.make_async_remote_copy(
            src_ref=j_ref.at[many],
            dst_ref=jr_ref.at[many],
            send_sem=send_x.at[c],
            recv_sem=recv_x.at[c],
            device_id=(xs[1], me_y),
            device_id_type=MESH,
        )

    def rows_moved():
        many = pl.ds(0, count_y - 1)
        return pltpu.make_async_remote_copy(
            src_ref=r_ref.at[many],
            dst_ref=rr_ref.at[many],
            send_sem=send_y,
            recv_sem=recv_y,
            device_id=(me_x, ys[1]),
            device_id_type=MESH,
        )

    for yp in range(-2, 5):
        first(yp)
    for yp in range(-1, 3):
        second(yp)
    for b in range(BANDS):
        yc_ref[b] = jnp.zeros((128, 128), jnp.float32)
        yt_ref[b] = jnp.ones((128, 128), jnp.float32)
    for g in range(4):
        first_layer(g, 0)
    for g in range(2):
        second_layer(g)

    def one_column(k, carry):
        column(k)

        @pl.when((k > 0) & (k % 4 == 0))
        def _():
            send_slabs(k // 4 - 1)

        return carry

    lax.fori_loop(0, 16, one_column, 0)
    deliver(3 * 256 + 3)
    send_slabs(3)

    for b in range(BANDS):
        for h in range(2):
            colour = yc_ref[b, pl.ds(64 * h, 8, stride=8), :]
            clear = yt_ref[b, pl.ds(64 * h, 8, stride=8), :]
            for s in range(1, 8):
                colour = colour + clear * yc_ref[b, pl.ds(64 * h + s, 8, stride=8), :]
                clear = clear * yt_ref[b, pl.ds(64 * h + s, 8, stride=8), :]
            rs_ref[0, 16 * b + 8 * h : 16 * b + 8 * h + 8, :] = colour * LN2
            rs_ref[1, 16 * b + 8 * h : 16 * b + 8 * h + 8, :] = clear
    for kind in range(2):
        image = jnp.transpose(rs_ref[kind])
        for h in range(2):
            for p in range(8):
                r_ref[p, 8 * h : 8 * h + 8, 128 * kind : 128 * kind + 128] = image[64 * h + 8 * p : 64 * h + 8 * p + 8]


    def send_rows(hop, carry):
        peer = peer_y(hop)
        pltpu.make_async_remote_copy(
            src_ref=r_ref.at[peer],
            dst_ref=rr_ref.at[me_y],
            send_sem=send_y,
            recv_sem=recv_y,
            device_id=(me_x, peer),
            device_id_type=MESH,
        ).start()
        return carry

    lax.fori_loop(1, count_y, send_rows, 0)
    rr_ref[me_y] = r_ref[me_y]

    at_ref[...] = jnp.zeros_like(at_ref)

    def fold_x(c):
        slabs_moved(c).wait_recv()
        image, clear = zero, one
        for s in range(count_x):
            piece = jr_ref[c * 256 + s * 8 : c * 256 + s * 8 + 8, :]
            both = jnp.where(low, pltpu.roll(piece, 64, 1), piece)
            image = jnp.where(low, image, 0.0) + clear * piece
            clear = clear * both
        for z in range(2):
            at_ref[16 * z + 4 * c : 16 * z + 4 * c + 4, :] = image[4 * z : 4 * z + 4]

    for c in range(3):
        fold_x(c)

    rows_moved().wait_recv()
    colour, clear = rr_ref[0, :, 0:128], rr_ref[0, :, 128:256]
    for s in range(1, count_y):
        colour = colour + clear * rr_ref[s, :, 0:128]
        clear = clear * rr_ref[s, :, 128:256]
    for kind, image in enumerate((colour, clear)):
        for b in range(BANDS):
            shift = (128 - 16 * b) % 128
            front = image[0:8]
            back = image[8:16]
            front = pltpu.roll(front, shift, 1) if shift else front
            back = pltpu.roll(back, shift + 16, 1) if shift < 112 else back
            vy_ref[8 * kind + b] = jnp.where(lane < 16, front, back)[:, 0:32]

    fold_x(3)
    at_ref[...] = jnp.transpose(at_ref[...])
    line = lax.broadcasted_iota(jnp.int32, (16, 128), 1)
    for z in range(2):
        row = jnp.zeros((16, 128), jnp.float32)
        for s in range(8):
            piece = at_ref[pl.ds(s, 16, stride=8), :]
            shift = (16 * s - 16 * z) % 128
            piece = pltpu.roll(piece, shift, 1) if shift else piece
            row = jnp.where((line >> 4) == s, piece, row)
        vx_ref[:, z, :] = row

    for c in range(4):
        slabs_moved(c).wait_send()
    rows_moved().wait_send()


def march_call(field, transfer_in, transfer_out, count_x, count_y):
    vmem = pl.BlockSpec(memory_space=pltpu.VMEM)

    def held(*shape, dtype=jnp.float32):
        return pltpu.VMEM(shape, dtype)

    return pl.pallas_call(
        functools.partial(march, count_x, count_y),
        out_shape=(
            jax.ShapeDtypeStruct((16, 2, 128), jnp.float32),
            jax.ShapeDtypeStruct((16, 8, 32), jnp.float32),
        ),
        in_specs=[pl.BlockSpec(memory_space=pltpu.HBM), vmem, vmem],
        out_specs=(vmem, vmem),
        scratch_shapes=[
            held(22, 144, 128),
            held(2, 3, 64, 128),
            held(2, 3, 64, 128),
            held(2, 16, 8, 128),
            held(4, 3, 8, 128),
            held(128, 64, dtype=jnp.bfloat16),
            held(128, 128, dtype=jnp.bfloat16),
            held(20, 23, 8, 128),
            held(18, 20, 8, 128),
            held(18, 20, 8, 128),
            held(18, 20, 8, 128),
            held(16 // GROUP, 64, 128 * GROUP, dtype=jnp.bfloat16),
            held(16 // GROUP, 128, 128 * GROUP),
            held(16 // GROUP, 128, 128 * GROUP),
            held(8, 128, 128),
            held(8, 128, 128),
            held(2, 128, 128),
            held(1280, 128),
            held(1024, 128),
            held(8, 16, 256),
            held(8, 16, 256),
            held(128, 128),
            held(16, 8, 128),
            held(2048, 128),
            pltpu.SemaphoreType.DMA,
            pltpu.SemaphoreType.DMA((2,)),
            pltpu.SemaphoreType.DMA((2,)),
            pltpu.SemaphoreType.DMA((2,)),
            pltpu.SemaphoreType.DMA((2,)),
            pltpu.SemaphoreType.DMA((4,)),
            pltpu.SemaphoreType.DMA((4,)),
            pltpu.SemaphoreType.DMA((4,)),
            pltpu.SemaphoreType.DMA((4,)),
            pltpu.SemaphoreType.DMA,
            pltpu.SemaphoreType.DMA,
        ],
        compiler_params=pltpu.CompilerParams(collective_id=0, has_side_effects=True, vmem_limit_bytes=24 << 20),
        name="march",
    )(field, transfer_in, transfer_out)


def emit(ax_ref, ay_ref, vx_ref, vy_ref, done):
    moves = (pltpu.make_async_copy(ax_ref, vx_ref, done.at[0]), pltpu.make_async_copy(ay_ref, vy_ref, done.at[1]))
    for move in moves:
        move.start()
    for move in moves:
        move.wait()


def emit_call(ax, ay):
    anywhere = pl.BlockSpec(memory_space=pl.ANY)
    return pl.pallas_call(
        emit,
        out_shape=(jax.ShapeDtypeStruct(ax.shape, ax.dtype), jax.ShapeDtypeStruct(ay.shape, ay.dtype)),
        in_specs=[anywhere, anywhere],
        out_specs=(anywhere, anywhere),
        scratch_shapes=[pltpu.SemaphoreType.DMA((2,))],
        compiler_params=pltpu.CompilerParams(vmem_limit_bytes=1 << 20),
        name="emit",
    )(ax, ay)


def body(scalar_field, transfer_in, transfer_out):
    count_x = lax.axis_size("bx")
    count_y = lax.axis_size("by")
    ax, ay = march_call(
        scalar_field.reshape(2048, 128), transfer_in.T, transfer_out.T, count_x, count_y
    )
    vx, vy = emit_call(ax, ay)
    return (vx.reshape(2, 8, 2, 128), vy.reshape(2, 8, 8, 32))


def solution(mesh):
    return jax.shard_map(
        body,
        mesh=mesh,
        in_specs=(P(None, "bx", "by"), P(), P()),
        out_specs=(P(None, None, "bx", "by"), P(None, None, "by", "bx")),
        check_vma=False,
    )
```

```python
import functools

import jax
import jax.numpy as jnp
from jax import lax
from jax.experimental import pallas as pl
from jax.experimental.pallas import tpu as pltpu
from jax.sharding import PartitionSpec as P

BANDS = 8
HID = 16
FEAT = 8
LOG2E = 1.4426950408889634
LN2 = 0.6931471805599453
MESH = pl.DeviceIdType.MESH
GROUP = 4


def lanes_of():
    return lax.broadcasted_iota(jnp.int32, (8, 128), 1)


def softplus(v):
    v = v * LOG2E
    return jnp.maximum(v, lax.log2(1.0 + jnp.exp2(jnp.minimum(v, 126.0))))


def widen(big_ref, weights, scale):
    rows, cols = weights.shape
    up = lax.broadcasted_iota(jnp.int32, (8 * rows, rows), 0) >> 3
    up = (up == lax.broadcasted_iota(jnp.int32, (8 * rows, rows), 1)).astype(jnp.float32)
    out = lax.broadcasted_iota(jnp.int32, (cols, 8 * cols), 1) >> 3
    out = (out == lax.broadcasted_iota(jnp.int32, (cols, 8 * cols), 0)).astype(jnp.float32)
    tall = jnp.dot(up.astype(jnp.bfloat16), weights, preferred_element_type=jnp.float32)
    wide = jnp.dot(tall.astype(jnp.bfloat16), out.astype(jnp.bfloat16), preferred_element_type=jnp.float32)
    at_row = lax.broadcasted_iota(jnp.int32, wide.shape, 0) & 7
    at_col = lax.broadcasted_iota(jnp.int32, wide.shape, 1) & 7
    big_ref[...] = jnp.where(at_row == at_col, wide * scale, 0.0).astype(jnp.bfloat16)


def march(
    count_x, count_y, field_ref, win_ref, wout_ref, vx_ref, vy_ref,
    tb_ref, xs_ref, xr_ref, yr_ref, cr_ref,
    w1_ref, w2_ref, s1_ref, p_ref, b_ref, d_ref, x_ref, u_ref, ch_ref, yc_ref, yt_ref, rs_ref,
    j_ref, jr_ref, r_ref, rr_ref, at_ref, st_ref, f_ref, load,
    sx, rx, sy, ry, sc, rc, send_x, recv_x, send_y, recv_y,
):
    me_x = lax.axis_index("bx")
    me_y = lax.axis_index("by")
    xs = (lax.rem(me_x + count_x - 1, count_x), lax.rem(me_x + 1, count_x))
    ys = (lax.rem(me_y + count_y - 1, count_y), lax.rem(me_y + 1, count_y))

    def peer_x(hop):
        return lax.rem(me_x + hop, count_x)

    def peer_y(hop):
        return lax.rem(me_y + hop, count_y)

    fetch = pltpu.make_async_copy(field_ref, f_ref, load)
    fetch.start()
    barrier = pltpu.get_barrier_semaphore()

    def greet_x(hop, carry):
        pl.semaphore_signal(barrier, inc=1, device_id=(peer_x(hop), me_y), device_id_type=MESH)
        return carry

    def greet_y(hop, carry):
        pl.semaphore_signal(barrier, inc=1, device_id=(me_x, peer_y(hop)), device_id_type=MESH)
        return carry

    for x in xs:
        for y in ys:
            pl.semaphore_signal(barrier, inc=1, device_id=(x, y), device_id_type=MESH)
    for hop in range(1, count_x):
        greet_x(hop, 0)
    for hop in range(1, count_y):
        greet_y(hop, 0)

    def plane(x):
        return f_ref[pl.ds(x, 64, stride=32), :]

    widen(w1_ref, jnp.transpose(win_ref[...].astype(jnp.float32)).astype(jnp.bfloat16), 0.5)
    widen(w2_ref, wout_ref[...], 1.0)
    fetch.wait()
    for i in range(3):
        xs_ref[0, i] = plane(i)
        xs_ref[1, i] = plane(29 + i)
    pl.semaphore_wait(barrier, count_x + count_y + 2)

    copies = []
    for side in range(2):
        copies.append(
            pltpu.make_async_remote_copy(
                src_ref=xs_ref.at[side],
                dst_ref=xr_ref.at[1 - side],
                send_sem=sx.at[side],
                recv_sem=rx.at[1 - side],
                device_id=(xs[side], me_y),
                device_id_type=MESH,
            )
        )
        copies[-1].start()

    def turn(x, front, back):
        tb_ref[x + 3, 8:136, :] = jnp.transpose(jnp.concatenate([front, back], axis=0))

    edges = (pl.ds(8, 8), pl.ds(128, 8))
    ends = (pl.ds(3, 3), pl.ds(16, 3))
    for x in (0, 1, 2, 13, 14, 15):
        turn(x, plane(x), plane(16 + x))
    for side in range(2):
        for part in range(2):
            copies.append(
                pltpu.make_async_remote_copy(
                    src_ref=tb_ref.at[ends[side], edges[part]],
                    dst_ref=cr_ref.at[2 * (1 - side) + (1 - part)],
                    send_sem=sc.at[2 * side + part],
                    recv_sem=rc.at[2 * (1 - side) + (1 - part)],
                    device_id=(xs[side], ys[part]),
                    device_id_type=MESH,
                )
            )
            copies[-1].start()

    for x in range(3, 13):
        turn(x, plane(x), plane(16 + x))
    for part in range(2):
        copies.append(
            pltpu.make_async_remote_copy(
                src_ref=tb_ref.at[pl.ds(3, 16), edges[part]],
                dst_ref=yr_ref.at[1 - part],
                send_sem=sy.at[part],
                recv_sem=ry.at[1 - part],
                device_id=(me_x, ys[part]),
                device_id_type=MESH,
            )
        )
        copies[-1].start()

    lane = lanes_of()
    seg = lax.broadcasted_iota(jnp.int32, (8, 128), 0)
    z = lane & 63
    half = lane >> 6
    top = z == 0
    bottom = z == 63
    full_x = 32 * count_x
    full_y = 128 * count_y
    at_x = me_x * 32 + half * 16
    at_y = me_y * 128 + seg * 16

    def above(v):
        return jnp.where(top, 0.0, pltpu.roll(v, 1, 1))

    def below(v):
        return jnp.where(bottom, 0.0, pltpu.roll(v, 127, 1))

    def inside(xp, yp):
        gy = at_y + yp
        ok = (gy >= 0) & (gy < full_y)
        if xp < 0:
            ok = ok & (at_x + xp >= 0)
        if xp > 15:
            ok = ok & (at_x + xp < full_x)
        return ok

    def field(xp, yp):
        return tb_ref[xp + 3, pl.ds(yp + 8, 8, stride=16), :]

    def first(yp, cells, masked=True):
        mid = {xp: field(xp, yp) for xp in sorted({c + o for c in cells for o in (-1, 0, 1)})}
        for xp in cells:
            c = mid[xp]
            near = field(xp, yp - 1) + field(xp, yp + 1)
            near = near + (mid[xp - 1] + mid[xp + 1]) + (above(c) + below(c))
            s = 0.4 * c + 0.1 * near
            s1_ref[xp + 2, yp + 2] = jnp.where(inside(xp, yp), s, 0.0) if masked else s

    def second(yp, cells, masked=True):
        mid = {xp: s1_ref[xp + 2, yp + 2] for xp in sorted({c + o for c in cells for o in (-1, 0, 1)})}
        around = [above(mid[xp]) + below(mid[xp]) for xp in cells]
        rows = []
        for xp, ends in zip(cells, around):
            c = mid[xp]
            near = s1_ref[xp + 2, yp + 1] + s1_ref[xp + 2, yp + 3]
            near = near + (mid[xp - 1] + mid[xp + 1]) + ends
            s = 0.4 * c + 0.1 * near
            rows.append(jnp.where(inside(xp, yp), s, 0.0) if masked else s)
        ups = [above(s) for s in rows]
        downs = [below(s) for s in rows]
        for xp, s, up, down in zip(cells, rows, ups, downs):
            p_ref[xp + 1, yp + 1] = s
            b_ref[xp + 1, yp + 1] = 2.0 * s + (up + down)
            d_ref[xp + 1, yp + 1] = down - up

    inner_first, outer_first = range(1, 15), (-2, -1, 0, 15, 16, 17)
    inner_second, outer_second = range(2, 14), (-1, 0, 1, 14, 15, 16)
    all_first, all_second = range(-2, 18), range(-1, 17)

    def early_first(i, carry):
        for n in range(7):
            first(1 + 7 * i + n, inner_first, False)
        return carry

    def early_second(i, carry):
        for n in range(2):
            second(2 + 2 * i + n, inner_second, False)
        return carry

    lax.fori_loop(0, 2, early_first, 0)
    lax.fori_loop(0, 6, early_second, 0)

    inner_x = (me_x > 0, me_x < count_x - 1)
    inner_y = (me_y > 0, me_y < count_y - 1)
    copies[0].wait_recv()
    copies[1].wait_recv()
    for i in range(3):
        turn(i - 3, jnp.where(inner_x[0], xr_ref[0, i], 0.0), plane(13 + i))
        turn(16 + i, plane(16 + i), jnp.where(inner_x[1], xr_ref[1, i], 0.0))
    for copy in copies[2:]:
        copy.wait_recv()
    low = lanes_of() < 64
    rims = (pl.ds(0, 8), pl.ds(136, 8))
    for part in range(2):
        for x in range(16):
            tb_ref[x + 3, rims[part], :] = jnp.where(inner_y[part], yr_ref[part, x], 0.0)
        for i in range(3):
            far = jnp.where(inner_x[0], cr_ref[part, i], 0.0)
            edge = jnp.where(low, pltpu.roll(far, 64, 1), pltpu.roll(yr_ref[part, 13 + i], 64, 1))
            tb_ref[i, rims[part], :] = jnp.where(inner_y[part], edge, 0.0)
            far = jnp.where(inner_x[1], cr_ref[2 + part, i], 0.0)
            edge = jnp.where(low, pltpu.roll(yr_ref[part, i], 64, 1), pltpu.roll(far, 64, 1))
            tb_ref[19 + i, rims[part], :] = jnp.where(inner_y[part], edge, 0.0)
    for copy in copies:
        copy.wait_send()

    one = jnp.ones((8, 128), jnp.float32)
    zero = jnp.zeros((8, 128), jnp.float32)

    def features(i, k):
        s = p_ref[i, k]
        a = p_ref[i + 1, k + 1] - p_ref[i - 1, k - 1]
        c = p_ref[i + 1, k - 1] - p_ref[i - 1, k + 1]
        gx = (b_ref[i + 1, k] - b_ref[i - 1, k] + (a + c)) * (1.0 / 3.0)
        gy = (b_ref[i, k + 1] - b_ref[i, k - 1] + (a - c)) * (1.0 / 3.0)
        d = d_ref[i, k]
        gz = (d + d + (d_ref[i + 1, k] + d_ref[i - 1, k]) + (d_ref[i, k + 1] + d_ref[i, k - 1])) * (1.0 / 3.0)
        q = 1.0 + gx * gx + gy * gy + gz * gz
        m = q * lax.rsqrt(q)
        return s, gx, gy, gz, m, s * m, s * s, one

    def first_layer(g, k):
        slot = g
        for n in range(GROUP):
            rows = features(g * GROUP + n + 1, k + 1)
            for f in range(0, FEAT, 2):
                pair = jnp.concatenate([rows[f], rows[f + 1]], axis=0)
                x_ref[slot, 8 * f : 8 * f + 16, 128 * n : 128 * n + 128] = pair.astype(jnp.bfloat16)
        u_ref[slot] = jnp.dot(w1_ref[...], x_ref[slot], preferred_element_type=jnp.float32)

    def second_layer(g):
        slot = g
        u = u_ref[slot]
        hidden = (u + u * jnp.tanh(u)).astype(jnp.bfloat16)
        ch_ref[slot] = jnp.dot(w2_ref[...], hidden, preferred_element_type=jnp.float32)

    def views(g, state):
        slot = g
        for n in range(GROUP):
            row = (g * GROUP + n) * 8
            for b in range(BANDS):
                e = softplus(ch_ref[slot, 8 * b : 8 * b + 8, 128 * n : 128 * n + 128])
                t = softplus(ch_ref[slot, 64 + 8 * b : 72 + 8 * b, 128 * n : 128 * n + 128])
                q = jnp.exp2(t * (-1.0 / 512.0))
                tx = state[8 + b]
                nx = tx * q
                state[b] = state[b] + (tx - nx) * e
                state[8 + b] = nx
                ty = yt_ref[b, row : row + 8, :]
                ny = ty * q
                yc_ref[b, row : row + 8, :] = yc_ref[b, row : row + 8, :] + (ty - ny) * e
                yt_ref[b, row : row + 8, :] = ny

    chunks = 16 // GROUP

    def deliver(row):
        state = [st_ref[b] for b in range(2 * BANDS)]
        colour = [(state[b] + state[8 + b] * pltpu.roll(state[b], 64, 1)) * LN2 for b in range(BANDS)]
        clear = [state[8 + b] * pltpu.roll(state[8 + b], 64, 1) for b in range(BANDS)]
        image = jnp.transpose(jnp.concatenate(colour + clear, axis=0))
        j_ref[pl.ds(row, 64, stride=4), :] = image[0:64]

    def column(k, cells):
        past = (k + 15) // 16
        deliver(past * (((k + 3) // 4 - 1) * 256 + (k + 3) % 4) + (1 - past) * 1024)
        state = [zero] * BANDS + [one] * BANDS
        for g in range(chunks):
            views(g, state)
            second_layer((g + 2) % chunks)
            first_layer((g + 4) % chunks, k + (g + 4) // chunks)
        if cells:
            second(k + 3, cells[1])
            first(k + 5, cells[0])
        for b in range(2 * BANDS):
            st_ref[b] = state[b]

    def slab(start):
        return pl.ds(pl.multiple_of(start, 8), 8)

    def send_slabs(c):
        def one_peer(hop, carry):
            peer = peer_x(hop)
            pltpu.make_async_remote_copy(
                src_ref=j_ref.at[slab(c * 256 + peer * 8)],
                dst_ref=jr_ref.at[slab(c * 256 + me_x * 8)],
                send_sem=send_x.at[c],
                recv_sem=recv_x.at[c],
                device_id=(peer, me_y),
                device_id_type=MESH,
            ).start()
            return carry

        for hop in range(1, count_x):
            one_peer(hop, 0)
        jr_ref[slab(c * 256 + me_x * 8), :] = j_ref[slab(c * 256 + me_x * 8), :]

    def slabs_moved(c):
        many = pl.ds(0, (count_x - 1) * 8)
        return pltpu.make_async_remote_copy(
            src_ref=j_ref.at[many],
            dst_ref=jr_ref.at[many],
            send_sem=send_x.at[c],
            recv_sem=recv_x.at[c],
            device_id=(xs[1], me_y),
            device_id_type=MESH,
        )

    def rows_moved():
        many = pl.ds(0, count_y - 1)
        return pltpu.make_async_remote_copy(
            src_ref=r_ref.at[many],
            dst_ref=rr_ref.at[many],
            send_sem=send_y,
            recv_sem=recv_y,
            device_id=(me_x, ys[1]),
            device_id_type=MESH,
        )

    for yp in range(-2, 5):
        first(yp, all_first if yp < 1 else outer_first)
    for yp in range(-1, 3):
        second(yp, all_second if yp < 2 else outer_second)
    for b in range(BANDS):
        yc_ref[b] = jnp.zeros((128, 128), jnp.float32)
        yt_ref[b] = jnp.ones((128, 128), jnp.float32)
    for g in range(4):
        first_layer(g, 0)
    for g in range(2):
        second_layer(g)

    def run(begin, end, cells):
        def one_column(k, carry):
            column(k, cells)

            @pl.when((k > 0) & (k % 4 == 0))
            def _():
                send_slabs(k // 4 - 1)

            return carry

        lax.fori_loop(begin, end, one_column, 0)

    run(0, 10, (outer_first, outer_second))
    run(10, 14, (all_first, all_second))
    run(14, 16, None)
    deliver(3 * 256 + 3)

    for b in range(BANDS):
        for h in range(2):
            colour = yc_ref[b, pl.ds(64 * h, 8, stride=8), :]
            clear = yt_ref[b, pl.ds(64 * h, 8, stride=8), :]
            for s in range(1, 8):
                colour = colour + clear * yc_ref[b, pl.ds(64 * h + s, 8, stride=8), :]
                clear = clear * yt_ref[b, pl.ds(64 * h + s, 8, stride=8), :]
            rs_ref[0, 16 * b + 8 * h : 16 * b + 8 * h + 8, :] = colour * LN2
            rs_ref[1, 16 * b + 8 * h : 16 * b + 8 * h + 8, :] = clear
    for kind in range(2):
        image = jnp.transpose(rs_ref[kind])
        for h in range(2):
            for p in range(8):
                r_ref[p, 8 * h : 8 * h + 8, 128 * kind : 128 * kind + 128] = image[64 * h + 8 * p : 64 * h + 8 * p + 8]


    def send_rows(hop, carry):
        peer = peer_y(hop)
        pltpu.make_async_remote_copy(
            src_ref=r_ref.at[peer],
            dst_ref=rr_ref.at[me_y],
            send_sem=send_y,
            recv_sem=recv_y,
            device_id=(me_x, peer),
            device_id_type=MESH,
        ).start()
        return carry

    for hop in range(1, count_y):
        send_rows(hop, 0)
    send_slabs(3)
    rr_ref[me_y] = r_ref[me_y]

    at_ref[...] = jnp.zeros_like(at_ref)

    def fold_x(c):
        slabs_moved(c).wait_recv()
        image, clear = zero, one
        for s in range(count_x):
            piece = jr_ref[c * 256 + s * 8 : c * 256 + s * 8 + 8, :]
            both = jnp.where(low, pltpu.roll(piece, 64, 1), piece)
            image = jnp.where(low, image, 0.0) + clear * piece
            clear = clear * both
        for z in range(2):
            at_ref[16 * z + 4 * c : 16 * z + 4 * c + 4, :] = image[4 * z : 4 * z + 4]

    for c in range(3):
        fold_x(c)

    rows_moved().wait_recv()
    colour, clear = rr_ref[0, :, 0:128], rr_ref[0, :, 128:256]
    for s in range(1, count_y):
        colour = colour + clear * rr_ref[s, :, 0:128]
        clear = clear * rr_ref[s, :, 128:256]
    for kind, image in enumerate((colour, clear)):
        for b in range(BANDS):
            shift = (128 - 16 * b) % 128
            front = image[0:8]
            back = image[8:16]
            front = pltpu.roll(front, shift, 1) if shift else front
            back = pltpu.roll(back, shift + 16, 1) if shift < 112 else back
            vy_ref[8 * kind + b] = jnp.where(lane < 16, front, back)[:, 0:32]

    fold_x(3)
    at_ref[...] = jnp.transpose(at_ref[...])
    line = lax.broadcasted_iota(jnp.int32, (16, 128), 1)
    for z in range(2):
        row = jnp.zeros((16, 128), jnp.float32)
        for s in range(8):
            piece = at_ref[pl.ds(s, 16, stride=8), :]
            shift = (16 * s - 16 * z) % 128
            piece = pltpu.roll(piece, shift, 1) if shift else piece
            row = jnp.where((line >> 4) == s, piece, row)
        vx_ref[:, z, :] = row

    for c in range(4):
        slabs_moved(c).wait_send()
    rows_moved().wait_send()


def march_call(field, transfer_in, transfer_out, count_x, count_y):
    vmem = pl.BlockSpec(memory_space=pltpu.VMEM)

    def held(*shape, dtype=jnp.float32):
        return pltpu.VMEM(shape, dtype)

    return pl.pallas_call(
        functools.partial(march, count_x, count_y),
        out_shape=(
            jax.ShapeDtypeStruct((16, 2, 128), jnp.float32),
            jax.ShapeDtypeStruct((16, 8, 32), jnp.float32),
        ),
        in_specs=[pl.BlockSpec(memory_space=pltpu.HBM), vmem, vmem],
        out_specs=(vmem, vmem),
        scratch_shapes=[
            held(22, 144, 128),
            held(2, 3, 64, 128),
            held(2, 3, 64, 128),
            held(2, 16, 8, 128),
            held(4, 3, 8, 128),
            held(128, 64, dtype=jnp.bfloat16),
            held(128, 128, dtype=jnp.bfloat16),
            held(20, 23, 8, 128),
            held(18, 20, 8, 128),
            held(18, 20, 8, 128),
            held(18, 20, 8, 128),
            held(16 // GROUP, 64, 128 * GROUP, dtype=jnp.bfloat16),
            held(16 // GROUP, 128, 128 * GROUP),
            held(16 // GROUP, 128, 128 * GROUP),
            held(8, 128, 128),
            held(8, 128, 128),
            held(2, 128, 128),
            held(1280, 128),
            held(1024, 128),
            held(8, 16, 256),
            held(8, 16, 256),
            held(128, 128),
            held(16, 8, 128),
            held(2048, 128),
            pltpu.SemaphoreType.DMA,
            pltpu.SemaphoreType.DMA((2,)),
            pltpu.SemaphoreType.DMA((2,)),
            pltpu.SemaphoreType.DMA((2,)),
            pltpu.SemaphoreType.DMA((2,)),
            pltpu.SemaphoreType.DMA((4,)),
            pltpu.SemaphoreType.DMA((4,)),
            pltpu.SemaphoreType.DMA((4,)),
            pltpu.SemaphoreType.DMA((4,)),
            pltpu.SemaphoreType.DMA,
            pltpu.SemaphoreType.DMA,
        ],
        compiler_params=pltpu.CompilerParams(collective_id=0, has_side_effects=True, vmem_limit_bytes=24 << 20),
        name="march",
    )(field, transfer_in, transfer_out)


def emit(ax_ref, ay_ref, vx_ref, vy_ref, done):
    moves = (pltpu.make_async_copy(ax_ref, vx_ref, done.at[0]), pltpu.make_async_copy(ay_ref, vy_ref, done.at[1]))
    for move in moves:
        move.start()
    for move in moves:
        move.wait()


def emit_call(ax, ay):
    anywhere = pl.BlockSpec(memory_space=pl.ANY)
    return pl.pallas_call(
        emit,
        out_shape=(jax.ShapeDtypeStruct(ax.shape, ax.dtype), jax.ShapeDtypeStruct(ay.shape, ay.dtype)),
        in_specs=[anywhere, anywhere],
        out_specs=(anywhere, anywhere),
        scratch_shapes=[pltpu.SemaphoreType.DMA((2,))],
        compiler_params=pltpu.CompilerParams(vmem_limit_bytes=1 << 20),
        name="emit",
    )(ax, ay)


def body(scalar_field, transfer_in, transfer_out):
    count_x = lax.axis_size("bx")
    count_y = lax.axis_size("by")
    ax, ay = march_call(
        pltpu.with_memory_space_constraint(scalar_field.reshape(2048, 128), pltpu.HBM), transfer_in.T, transfer_out, count_x, count_y
    )
    vx, vy = emit_call(ax, ay)
    return (vx.reshape(2, 8, 2, 128), vy.reshape(2, 8, 8, 32))


def solution(mesh):
    return jax.shard_map(
        body,
        mesh=mesh,
        in_specs=(P(None, "bx", "by"), P(), P()),
        out_specs=(P(None, None, "bx", "by"), P(None, None, "by", "bx")),
        check_vma=False,
    )
```

```python
import functools

import jax
import jax.numpy as jnp
from jax import lax
from jax.experimental import pallas as pl
from jax.experimental.pallas import tpu as pltpu
from jax.sharding import PartitionSpec as P

BANDS = 8
HID = 16
FEAT = 8
LOG2E = 1.4426950408889634
LN2 = 0.6931471805599453
MESH = pl.DeviceIdType.MESH
GROUP = 4


def lanes_of():
    return lax.broadcasted_iota(jnp.int32, (8, 128), 1)


def softplus(v):
    return jnp.maximum(v, lax.log2(1.0 + jnp.exp2(jnp.minimum(v, 126.0))))


def widen(big_ref, weights, scale):
    rows, cols = weights.shape
    up = lax.broadcasted_iota(jnp.int32, (8 * rows, rows), 0) >> 3
    up = (up == lax.broadcasted_iota(jnp.int32, (8 * rows, rows), 1)).astype(jnp.float32)
    out = lax.broadcasted_iota(jnp.int32, (cols, 8 * cols), 1) >> 3
    out = (out == lax.broadcasted_iota(jnp.int32, (cols, 8 * cols), 0)).astype(jnp.float32)
    tall = jnp.dot(up.astype(jnp.bfloat16), weights, preferred_element_type=jnp.float32)
    wide = jnp.dot(tall.astype(jnp.bfloat16), out.astype(jnp.bfloat16), preferred_element_type=jnp.float32)
    at_row = lax.broadcasted_iota(jnp.int32, wide.shape, 0) & 7
    at_col = lax.broadcasted_iota(jnp.int32, wide.shape, 1) & 7
    wide = jnp.where(at_row == at_col, wide * scale, 0.0)
    big_ref[:, 0 : wide.shape[1]] = wide.astype(jnp.bfloat16)
    if big_ref.shape[1] > wide.shape[1]:
        wide = wide - wide.astype(jnp.bfloat16).astype(jnp.float32)
        big_ref[:, wide.shape[1] :] = wide.astype(jnp.bfloat16)


def march(
    count_x, count_y, field_ref, win_hbm, wout_hbm, vx_ref, vy_ref,
    tb_ref, xs_ref, xr_ref, yr_ref, cr_ref,
    w1_ref, w2_ref, s1_ref, p_ref, b_ref, d_ref, x_ref, u_ref, ch_ref, yc_ref, yt_ref, rs_ref,
    j_ref, jr_ref, r_ref, rr_ref, at_ref, st_ref, f_ref, win_ref, wout_ref, load,
    sx, rx, sy, ry, sc, rc, send_x, recv_x, send_y, recv_y,
):
    me_x = lax.axis_index("bx")
    me_y = lax.axis_index("by")
    xs = (lax.rem(me_x + count_x - 1, count_x), lax.rem(me_x + 1, count_x))
    ys = (lax.rem(me_y + count_y - 1, count_y), lax.rem(me_y + 1, count_y))

    def peer_x(hop):
        return lax.rem(me_x + hop, count_x)

    def peer_y(hop):
        return lax.rem(me_y + hop, count_y)

    fetches = (
        pltpu.make_async_copy(win_hbm, win_ref, load.at[0]),
        pltpu.make_async_copy(wout_hbm, wout_ref, load.at[1]),
        pltpu.make_async_copy(field_ref, f_ref, load.at[2]),
    )
    for fetch in fetches:
        fetch.start()
    barrier = pltpu.get_barrier_semaphore()

    def greet_x(hop, carry):
        pl.semaphore_signal(barrier, inc=1, device_id=(peer_x(hop), me_y), device_id_type=MESH)
        return carry

    def greet_y(hop, carry):
        pl.semaphore_signal(barrier, inc=1, device_id=(me_x, peer_y(hop)), device_id_type=MESH)
        return carry

    for x in xs:
        for y in ys:
            pl.semaphore_signal(barrier, inc=1, device_id=(x, y), device_id_type=MESH)
    for hop in range(1, count_x):
        greet_x(hop, 0)
    for hop in range(1, count_y):
        greet_y(hop, 0)

    def plane(x):
        return f_ref[pl.ds(x, 64, stride=32), :]

    fetches[0].wait()
    fetches[1].wait()
    widen(w1_ref, jnp.transpose(win_ref[...].astype(jnp.float32)).astype(jnp.bfloat16), 0.5)
    widen(w2_ref, wout_ref[...], LOG2E)
    fetches[2].wait()
    for i in range(3):
        xs_ref[0, i] = plane(i)
        xs_ref[1, i] = plane(29 + i)
    pl.semaphore_wait(barrier, count_x + count_y + 2)

    copies = []
    for side in range(2):
        copies.append(
            pltpu.make_async_remote_copy(
                src_ref=xs_ref.at[side],
                dst_ref=xr_ref.at[1 - side],
                send_sem=sx.at[side],
                recv_sem=rx.at[1 - side],
                device_id=(xs[side], me_y),
                device_id_type=MESH,
            )
        )
        copies[-1].start()

    def turn(x, front, back):
        tb_ref[x + 3, 8:136, :] = jnp.transpose(jnp.concatenate([front, back], axis=0))

    edges = (pl.ds(8, 8), pl.ds(128, 8))
    ends = (pl.ds(3, 3), pl.ds(16, 3))
    for x in (0, 1, 2, 13, 14, 15):
        turn(x, plane(x), plane(16 + x))
    for side in range(2):
        for part in range(2):
            copies.append(
                pltpu.make_async_remote_copy(
                    src_ref=tb_ref.at[ends[side], edges[part]],
                    dst_ref=cr_ref.at[2 * (1 - side) + (1 - part)],
                    send_sem=sc.at[2 * side + part],
                    recv_sem=rc.at[2 * (1 - side) + (1 - part)],
                    device_id=(xs[side], ys[part]),
                    device_id_type=MESH,
                )
            )
            copies[-1].start()

    for x in range(3, 13):
        turn(x, plane(x), plane(16 + x))
    for part in range(2):
        copies.append(
            pltpu.make_async_remote_copy(
                src_ref=tb_ref.at[pl.ds(3, 16), edges[part]],
                dst_ref=yr_ref.at[1 - part],
                send_sem=sy.at[part],
                recv_sem=ry.at[1 - part],
                device_id=(me_x, ys[part]),
                device_id_type=MESH,
            )
        )
        copies[-1].start()

    lane = lanes_of()
    seg = lax.broadcasted_iota(jnp.int32, (8, 128), 0)
    z = lane & 63
    half = lane >> 6
    top = z == 0
    bottom = z == 63
    full_x = 32 * count_x
    full_y = 128 * count_y
    at_x = me_x * 32 + half * 16
    at_y = me_y * 128 + seg * 16

    def above(v):
        return jnp.where(top, 0.0, pltpu.roll(v, 1, 1))

    def below(v):
        return jnp.where(bottom, 0.0, pltpu.roll(v, 127, 1))

    def inside(xp, yp):
        gy = at_y + yp
        ok = (gy >= 0) & (gy < full_y)
        if xp < 0:
            ok = ok & (at_x + xp >= 0)
        if xp > 15:
            ok = ok & (at_x + xp < full_x)
        return ok

    def field(xp, yp):
        return tb_ref[xp + 3, pl.ds(yp + 8, 8, stride=16), :]

    def first(yp, cells, masked=True):
        mid = {xp: field(xp, yp) for xp in sorted({c + o for c in cells for o in (-1, 0, 1)})}
        for xp in cells:
            c = mid[xp]
            near = field(xp, yp - 1) + field(xp, yp + 1)
            near = near + (mid[xp - 1] + mid[xp + 1]) + (above(c) + below(c))
            s = 0.4 * c + 0.1 * near
            s1_ref[xp + 2, yp + 2] = jnp.where(inside(xp, yp), s, 0.0) if masked else s

    def second(yp, cells, masked=True):
        mid = {xp: s1_ref[xp + 2, yp + 2] for xp in sorted({c + o for c in cells for o in (-1, 0, 1)})}
        around = [above(mid[xp]) + below(mid[xp]) for xp in cells]
        rows = []
        for xp, ends in zip(cells, around):
            c = mid[xp]
            near = s1_ref[xp + 2, yp + 1] + s1_ref[xp + 2, yp + 3]
            near = near + (mid[xp - 1] + mid[xp + 1]) + ends
            s = 0.4 * c + 0.1 * near
            rows.append(jnp.where(inside(xp, yp), s, 0.0) if masked else s)
        ups = [above(s) for s in rows]
        downs = [below(s) for s in rows]
        for xp, s, up, down in zip(cells, rows, ups, downs):
            p_ref[xp + 1, yp + 1] = s
            b_ref[xp + 1, yp + 1] = 2.0 * s + (up + down)
            d_ref[xp + 1, yp + 1] = down - up

    inner_first, outer_first = range(1, 15), (-2, -1, 0, 15, 16, 17)
    inner_second, outer_second = range(2, 14), (-1, 0, 1, 14, 15, 16)
    all_first, all_second = range(-2, 18), range(-1, 17)

    def early_first(i, carry):
        for n in range(7):
            first(1 + 7 * i + n, inner_first, False)
        return carry

    def early_second(i, carry):
        for n in range(2):
            second(2 + 2 * i + n, inner_second, False)
        return carry

    lax.fori_loop(0, 2, early_first, 0)
    lax.fori_loop(0, 6, early_second, 0)

    inner_x = (me_x > 0, me_x < count_x - 1)
    inner_y = (me_y > 0, me_y < count_y - 1)
    copies[0].wait_recv()
    copies[1].wait_recv()
    for i in range(3):
        turn(i - 3, jnp.where(inner_x[0], xr_ref[0, i], 0.0), plane(13 + i))
        turn(16 + i, plane(16 + i), jnp.where(inner_x[1], xr_ref[1, i], 0.0))
    for copy in copies[2:]:
        copy.wait_recv()
    low = lanes_of() < 64
    rims = (pl.ds(0, 8), pl.ds(136, 8))
    for part in range(2):
        for x in range(16):
            tb_ref[x + 3, rims[part], :] = jnp.where(inner_y[part], yr_ref[part, x], 0.0)
        for i in range(3):
            far = jnp.where(inner_x[0], cr_ref[part, i], 0.0)
            edge = jnp.where(low, pltpu.roll(far, 64, 1), pltpu.roll(yr_ref[part, 13 + i], 64, 1))
            tb_ref[i, rims[part], :] = jnp.where(inner_y[part], edge, 0.0)
            far = jnp.where(inner_x[1], cr_ref[2 + part, i], 0.0)
            edge = jnp.where(low, pltpu.roll(yr_ref[part, i], 64, 1), pltpu.roll(far, 64, 1))
            tb_ref[19 + i, rims[part], :] = jnp.where(inner_y[part], edge, 0.0)
    for copy in copies:
        copy.wait_send()

    one = jnp.ones((8, 128), jnp.float32)
    zero = jnp.zeros((8, 128), jnp.float32)

    def features(i, k):
        s = p_ref[i, k]
        a = p_ref[i + 1, k + 1] - p_ref[i - 1, k - 1]
        c = p_ref[i + 1, k - 1] - p_ref[i - 1, k + 1]
        gx = (b_ref[i + 1, k] - b_ref[i - 1, k] + (a + c)) * (1.0 / 3.0)
        gy = (b_ref[i, k + 1] - b_ref[i, k - 1] + (a - c)) * (1.0 / 3.0)
        d = d_ref[i, k]
        gz = (d + d + (d_ref[i + 1, k] + d_ref[i - 1, k]) + (d_ref[i, k + 1] + d_ref[i, k - 1])) * (1.0 / 3.0)
        q = 1.0 + gx * gx + gy * gy + gz * gz
        m = q * lax.rsqrt(q)
        return s, gx, gy, gz, m, s * m, s * s, one

    def first_layer(g, k):
        slot = g
        for n in range(GROUP):
            rows = features(g * GROUP + n + 1, k + 1)
            for f in range(0, FEAT, 2):
                pair = jnp.concatenate([rows[f], rows[f + 1]], axis=0)
                x_ref[slot, 8 * f : 8 * f + 16, 128 * n : 128 * n + 128] = pair.astype(jnp.bfloat16)
        u_ref[slot] = jnp.dot(w1_ref[...], x_ref[slot], preferred_element_type=jnp.float32)

    def second_layer(g):
        slot = g
        u = u_ref[slot]
        hidden = (u + u * jnp.tanh(u)).astype(jnp.bfloat16)
        hidden = jnp.concatenate([hidden, hidden], axis=0)
        ch_ref[slot] = jnp.dot(w2_ref[...], hidden, preferred_element_type=jnp.float32)

    def views(g, state):
        slot = g
        for n in range(GROUP):
            row = (g * GROUP + n) * 8
            for b in range(BANDS):
                e = softplus(ch_ref[slot, 8 * b : 8 * b + 8, 128 * n : 128 * n + 128])
                t = softplus(ch_ref[slot, 64 + 8 * b : 72 + 8 * b, 128 * n : 128 * n + 128])
                q = jnp.exp2(t * (-1.0 / 512.0))
                tx = state[8 + b]
                nx = tx * q
                state[b] = state[b] + (tx - nx) * e
                state[8 + b] = nx
                ty = yt_ref[b, row : row + 8, :]
                ny = ty * q
                yc_ref[b, row : row + 8, :] = yc_ref[b, row : row + 8, :] + (ty - ny) * e
                yt_ref[b, row : row + 8, :] = ny

    chunks = 16 // GROUP

    def deliver(row):
        state = [st_ref[b] for b in range(2 * BANDS)]
        colour = [(state[b] + state[8 + b] * pltpu.roll(state[b], 64, 1)) * LN2 for b in range(BANDS)]
        clear = [state[8 + b] * pltpu.roll(state[8 + b], 64, 1) for b in range(BANDS)]
        image = jnp.transpose(jnp.concatenate(colour + clear, axis=0))
        j_ref[pl.ds(row, 64, stride=4), :] = image[0:64]

    def column(k, cells):
        past = (k + 15) // 16
        deliver(past * (((k + 3) // 4 - 1) * 256 + (k + 3) % 4) + (1 - past) * 1024)
        state = [zero] * BANDS + [one] * BANDS
        for g in range(chunks):
            views(g, state)
            second_layer((g + 2) % chunks)
            first_layer((g + 4) % chunks, k + (g + 4) // chunks)
        if cells:
            second(k + 3, cells[1])
            first(k + 5, cells[0])
        for b in range(2 * BANDS):
            st_ref[b] = state[b]

    def slab(start):
        return pl.ds(pl.multiple_of(start, 8), 8)

    def send_slabs(c):
        def one_peer(hop, carry):
            peer = peer_x(hop)
            pltpu.make_async_remote_copy(
                src_ref=j_ref.at[slab(c * 256 + peer * 8)],
                dst_ref=jr_ref.at[slab(c * 256 + me_x * 8)],
                send_sem=send_x.at[c],
                recv_sem=recv_x.at[c],
                device_id=(peer, me_y),
                device_id_type=MESH,
            ).start()
            return carry

        for hop in range(1, count_x):
            one_peer(hop, 0)
        jr_ref[slab(c * 256 + me_x * 8), :] = j_ref[slab(c * 256 + me_x * 8), :]

    def slabs_moved(c):
        many = pl.ds(0, (count_x - 1) * 8)
        return pltpu.make_async_remote_copy(
            src_ref=j_ref.at[many],
            dst_ref=jr_ref.at[many],
            send_sem=send_x.at[c],
            recv_sem=recv_x.at[c],
            device_id=(xs[1], me_y),
            device_id_type=MESH,
        )

    def rows_moved():
        many = pl.ds(0, count_y - 1)
        return pltpu.make_async_remote_copy(
            src_ref=r_ref.at[many],
            dst_ref=rr_ref.at[many],
            send_sem=send_y,
            recv_sem=recv_y,
            device_id=(me_x, ys[1]),
            device_id_type=MESH,
        )

    for yp in range(-2, 5):
        first(yp, all_first if yp < 1 else outer_first)
    for yp in range(-1, 3):
        second(yp, all_second if yp < 2 else outer_second)
    for b in range(BANDS):
        yc_ref[b] = jnp.zeros((128, 128), jnp.float32)
        yt_ref[b] = jnp.ones((128, 128), jnp.float32)
    for g in range(4):
        first_layer(g, 0)
    for g in range(2):
        second_layer(g)

    def run(begin, end, cells):
        def one_column(k, carry):
            column(k, cells)

            @pl.when((k > 0) & (k % 4 == 0))
            def _():
                send_slabs(k // 4 - 1)

            return carry

        lax.fori_loop(begin, end, one_column, 0)

    run(0, 10, (outer_first, outer_second))
    run(10, 14, (all_first, all_second))
    run(14, 16, None)
    deliver(3 * 256 + 3)

    for b in range(BANDS):
        for h in range(2):
            colour = yc_ref[b, pl.ds(64 * h, 8, stride=8), :]
            clear = yt_ref[b, pl.ds(64 * h, 8, stride=8), :]
            for s in range(1, 8):
                colour = colour + clear * yc_ref[b, pl.ds(64 * h + s, 8, stride=8), :]
                clear = clear * yt_ref[b, pl.ds(64 * h + s, 8, stride=8), :]
            rs_ref[0, 16 * b + 8 * h : 16 * b + 8 * h + 8, :] = colour * LN2
            rs_ref[1, 16 * b + 8 * h : 16 * b + 8 * h + 8, :] = clear
    for kind in range(2):
        image = jnp.transpose(rs_ref[kind])
        for h in range(2):
            for p in range(8):
                r_ref[p, 8 * h : 8 * h + 8, 128 * kind : 128 * kind + 128] = image[64 * h + 8 * p : 64 * h + 8 * p + 8]


    def send_rows(hop, carry):
        peer = peer_y(hop)
        pltpu.make_async_remote_copy(
            src_ref=r_ref.at[peer],
            dst_ref=rr_ref.at[me_y],
            send_sem=send_y,
            recv_sem=recv_y,
            device_id=(me_x, peer),
            device_id_type=MESH,
        ).start()
        return carry

    for hop in range(1, count_y):
        send_rows(hop, 0)
    send_slabs(3)
    rr_ref[me_y] = r_ref[me_y]

    at_ref[...] = jnp.zeros_like(at_ref)

    def fold_x(c):
        slabs_moved(c).wait_recv()
        image, clear = zero, one
        for s in range(count_x):
            piece = jr_ref[c * 256 + s * 8 : c * 256 + s * 8 + 8, :]
            both = jnp.where(low, pltpu.roll(piece, 64, 1), piece)
            image = jnp.where(low, image, 0.0) + clear * piece
            clear = clear * both
        for z in range(2):
            at_ref[16 * z + 4 * c : 16 * z + 4 * c + 4, :] = image[4 * z : 4 * z + 4]

    for c in range(3):
        fold_x(c)

    rows_moved().wait_recv()
    colour, clear = rr_ref[0, :, 0:128], rr_ref[0, :, 128:256]
    for s in range(1, count_y):
        colour = colour + clear * rr_ref[s, :, 0:128]
        clear = clear * rr_ref[s, :, 128:256]
    for kind, image in enumerate((colour, clear)):
        for b in range(BANDS):
            shift = (128 - 16 * b) % 128
            front = image[0:8]
            back = image[8:16]
            front = pltpu.roll(front, shift, 1) if shift else front
            back = pltpu.roll(back, shift + 16, 1) if shift < 112 else back
            vy_ref[8 * kind + b] = jnp.where(lane < 16, front, back)[:, 0:32]

    fold_x(3)
    at_ref[...] = jnp.transpose(at_ref[...])
    line = lax.broadcasted_iota(jnp.int32, (16, 128), 1)
    for z in range(2):
        row = jnp.zeros((16, 128), jnp.float32)
        for s in range(8):
            piece = at_ref[pl.ds(s, 16, stride=8), :]
            shift = (16 * s - 16 * z) % 128
            piece = pltpu.roll(piece, shift, 1) if shift else piece
            row = jnp.where((line >> 4) == s, piece, row)
        vx_ref[:, z, :] = row

    for c in range(4):
        slabs_moved(c).wait_send()
    rows_moved().wait_send()


def march_call(field, transfer_in, transfer_out, count_x, count_y):
    vmem = pl.BlockSpec(memory_space=pltpu.VMEM)

    def held(*shape, dtype=jnp.float32):
        return pltpu.VMEM(shape, dtype)

    return pl.pallas_call(
        functools.partial(march, count_x, count_y),
        out_shape=(
            jax.ShapeDtypeStruct((16, 2, 128), jnp.float32),
            jax.ShapeDtypeStruct((16, 8, 32), jnp.float32),
        ),
        in_specs=[pl.BlockSpec(memory_space=pltpu.HBM)] * 3,
        out_specs=(vmem, vmem),
        scratch_shapes=[
            held(22, 144, 128),
            held(2, 3, 64, 128),
            held(2, 3, 64, 128),
            held(2, 16, 8, 128),
            held(4, 3, 8, 128),
            held(128, 64, dtype=jnp.bfloat16),
            held(128, 256, dtype=jnp.bfloat16),
            held(20, 23, 8, 128),
            held(18, 20, 8, 128),
            held(18, 20, 8, 128),
            held(18, 20, 8, 128),
            held(16 // GROUP, 64, 128 * GROUP, dtype=jnp.bfloat16),
            held(16 // GROUP, 128, 128 * GROUP),
            held(16 // GROUP, 128, 128 * GROUP),
            held(8, 128, 128),
            held(8, 128, 128),
            held(2, 128, 128),
            held(1280, 128),
            held(1024, 128),
            held(8, 16, 256),
            held(8, 16, 256),
            held(128, 128),
            held(16, 8, 128),
            held(2048, 128),
            held(8, 16, dtype=jnp.bfloat16),
            held(16, 16, dtype=jnp.bfloat16),
            pltpu.SemaphoreType.DMA((3,)),
            pltpu.SemaphoreType.DMA((2,)),
            pltpu.SemaphoreType.DMA((2,)),
            pltpu.SemaphoreType.DMA((2,)),
            pltpu.SemaphoreType.DMA((2,)),
            pltpu.SemaphoreType.DMA((4,)),
            pltpu.SemaphoreType.DMA((4,)),
            pltpu.SemaphoreType.DMA((4,)),
            pltpu.SemaphoreType.DMA((4,)),
            pltpu.SemaphoreType.DMA,
            pltpu.SemaphoreType.DMA,
        ],
        compiler_params=pltpu.CompilerParams(collective_id=0, has_side_effects=True, vmem_limit_bytes=24 << 20),
        name="march",
    )(field, transfer_in, transfer_out)


def emit(ax_ref, ay_ref, vx_ref, vy_ref, done):
    moves = (pltpu.make_async_copy(ax_ref, vx_ref, done.at[0]), pltpu.make_async_copy(ay_ref, vy_ref, done.at[1]))
    for move in moves:
        move.start()
    for move in moves:
        move.wait()


def emit_call(ax, ay):
    anywhere = pl.BlockSpec(memory_space=pl.ANY)
    return pl.pallas_call(
        emit,
        out_shape=(jax.ShapeDtypeStruct(ax.shape, ax.dtype), jax.ShapeDtypeStruct(ay.shape, ay.dtype)),
        in_specs=[anywhere, anywhere],
        out_specs=(anywhere, anywhere),
        scratch_shapes=[pltpu.SemaphoreType.DMA((2,))],
        compiler_params=pltpu.CompilerParams(vmem_limit_bytes=1 << 20),
        name="emit",
    )(ax, ay)


def body(scalar_field, transfer_in, transfer_out):
    count_x = lax.axis_size("bx")
    count_y = lax.axis_size("by")
    ax, ay = march_call(
        pltpu.with_memory_space_constraint(scalar_field.reshape(2048, 128), pltpu.HBM),
        pltpu.with_memory_space_constraint(transfer_in.T, pltpu.HBM),
        pltpu.with_memory_space_constraint(transfer_out, pltpu.HBM),
        count_x,
        count_y,
    )
    vx, vy = emit_call(ax, ay)
    return (vx.reshape(2, 8, 2, 128), vy.reshape(2, 8, 8, 32))


def solution(mesh):
    return jax.shard_map(
        body,
        mesh=mesh,
        in_specs=(P(None, "bx", "by"), P(), P()),
        out_specs=(P(None, None, "bx", "by"), P(None, None, "by", "bx")),
        check_vma=False,
    )
```

```python
import functools

import jax
import jax.numpy as jnp
from jax import lax
from jax.experimental import pallas as pl
from jax.experimental.pallas import tpu as pltpu
from jax.sharding import PartitionSpec as P

BANDS = 8
HID = 16
FEAT = 8
LOG2E = 1.4426950408889634
LN2 = 0.6931471805599453
MESH = pl.DeviceIdType.MESH
GROUP = 2


def lanes_of():
    return lax.broadcasted_iota(jnp.int32, (8, 128), 1)


def softplus(v):
    return jnp.maximum(v, lax.log2(1.0 + jnp.exp2(jnp.minimum(v, 126.0))))


def widen(big_ref, weights, scale):
    rows, cols = weights.shape
    up = lax.broadcasted_iota(jnp.int32, (8 * rows, rows), 0) >> 3
    up = (up == lax.broadcasted_iota(jnp.int32, (8 * rows, rows), 1)).astype(jnp.float32)
    out = lax.broadcasted_iota(jnp.int32, (cols, 8 * cols), 1) >> 3
    out = (out == lax.broadcasted_iota(jnp.int32, (cols, 8 * cols), 0)).astype(jnp.float32)
    tall = jnp.dot(up.astype(jnp.bfloat16), weights, preferred_element_type=jnp.float32)
    wide = jnp.dot(tall.astype(jnp.bfloat16), out.astype(jnp.bfloat16), preferred_element_type=jnp.float32)
    at_row = lax.broadcasted_iota(jnp.int32, wide.shape, 0) & 7
    at_col = lax.broadcasted_iota(jnp.int32, wide.shape, 1) & 7
    wide = jnp.where(at_row == at_col, wide * scale, 0.0)
    big_ref[:, 0 : wide.shape[1]] = wide.astype(jnp.bfloat16)
    if big_ref.shape[1] > wide.shape[1]:
        wide = wide - wide.astype(jnp.bfloat16).astype(jnp.float32)
        big_ref[:, wide.shape[1] :] = wide.astype(jnp.bfloat16)


def march(
    count_x, count_y, field_ref, win_hbm, wout_hbm, vx_ref, vy_ref,
    tb_ref, xs_ref, xr_ref, yr_ref, cr_ref,
    w1_ref, w2_ref, s1_ref, p_ref, b_ref, d_ref, x_ref, u_ref, ch_ref, yc_ref, yt_ref, rs_ref,
    j_ref, jr_ref, r_ref, rr_ref, at_ref, st_ref, f_ref, win_ref, wout_ref, load,
    sx, rx, sy, ry, sc, rc, send_x, recv_x, send_y, recv_y,
):
    me_x = lax.axis_index("bx")
    me_y = lax.axis_index("by")
    xs = (lax.rem(me_x + count_x - 1, count_x), lax.rem(me_x + 1, count_x))
    ys = (lax.rem(me_y + count_y - 1, count_y), lax.rem(me_y + 1, count_y))

    def peer_x(hop):
        return lax.rem(me_x + hop, count_x)

    def peer_y(hop):
        return lax.rem(me_y + hop, count_y)

    fetches = (
        pltpu.make_async_copy(win_hbm, win_ref, load.at[0]),
        pltpu.make_async_copy(wout_hbm, wout_ref, load.at[1]),
        pltpu.make_async_copy(field_ref, f_ref, load.at[2]),
    )
    for fetch in fetches:
        fetch.start()
    barrier = pltpu.get_barrier_semaphore()

    def greet_x(hop, carry):
        pl.semaphore_signal(barrier, inc=1, device_id=(peer_x(hop), me_y), device_id_type=MESH)
        return carry

    def greet_y(hop, carry):
        pl.semaphore_signal(barrier, inc=1, device_id=(me_x, peer_y(hop)), device_id_type=MESH)
        return carry

    for x in xs:
        for y in ys:
            pl.semaphore_signal(barrier, inc=1, device_id=(x, y), device_id_type=MESH)
    for hop in range(1, count_x):
        greet_x(hop, 0)
    for hop in range(1, count_y):
        greet_y(hop, 0)

    def plane(x):
        return f_ref[pl.ds(x, 64, stride=32), :]

    fetches[0].wait()
    fetches[1].wait()
    widen(w1_ref, jnp.transpose(win_ref[...].astype(jnp.float32)).astype(jnp.bfloat16), 0.5)
    widen(w2_ref, wout_ref[...], LOG2E)
    fetches[2].wait()
    for i in range(3):
        xs_ref[0, i] = plane(i)
        xs_ref[1, i] = plane(29 + i)
    pl.semaphore_wait(barrier, count_x + count_y + 2)

    copies = []
    for side in range(2):
        copies.append(
            pltpu.make_async_remote_copy(
                src_ref=xs_ref.at[side],
                dst_ref=xr_ref.at[1 - side],
                send_sem=sx.at[side],
                recv_sem=rx.at[1 - side],
                device_id=(xs[side], me_y),
                device_id_type=MESH,
            )
        )
        copies[-1].start()

    def turn(x, front, back):
        tb_ref[x + 3, 8:136, :] = jnp.transpose(jnp.concatenate([front, back], axis=0))

    edges = (pl.ds(8, 8), pl.ds(128, 8))
    ends = (pl.ds(3, 3), pl.ds(16, 3))
    for x in (0, 1, 2, 13, 14, 15):
        turn(x, plane(x), plane(16 + x))
    for side in range(2):
        for part in range(2):
            copies.append(
                pltpu.make_async_remote_copy(
                    src_ref=tb_ref.at[ends[side], edges[part]],
                    dst_ref=cr_ref.at[2 * (1 - side) + (1 - part)],
                    send_sem=sc.at[2 * side + part],
                    recv_sem=rc.at[2 * (1 - side) + (1 - part)],
                    device_id=(xs[side], ys[part]),
                    device_id_type=MESH,
                )
            )
            copies[-1].start()

    for x in range(3, 13):
        turn(x, plane(x), plane(16 + x))
    for part in range(2):
        copies.append(
            pltpu.make_async_remote_copy(
                src_ref=tb_ref.at[pl.ds(3, 16), edges[part]],
                dst_ref=yr_ref.at[1 - part],
                send_sem=sy.at[part],
                recv_sem=ry.at[1 - part],
                device_id=(me_x, ys[part]),
                device_id_type=MESH,
            )
        )
        copies[-1].start()

    lane = lanes_of()
    seg = lax.broadcasted_iota(jnp.int32, (8, 128), 0)
    z = lane & 63
    half = lane >> 6
    top = z == 0
    bottom = z == 63
    full_x = 32 * count_x
    full_y = 128 * count_y
    at_x = me_x * 32 + half * 16
    at_y = me_y * 128 + seg * 16

    def above(v):
        return jnp.where(top, 0.0, pltpu.roll(v, 1, 1))

    def below(v):
        return jnp.where(bottom, 0.0, pltpu.roll(v, 127, 1))

    def inside(xp, yp):
        gy = at_y + yp
        ok = (gy >= 0) & (gy < full_y)
        if xp < 0:
            ok = ok & (at_x + xp >= 0)
        if xp > 15:
            ok = ok & (at_x + xp < full_x)
        return ok

    def field(xp, yp):
        return tb_ref[xp + 3, pl.ds(yp + 8, 8, stride=16), :]

    def first(yp, cells, masked=True):
        mid = {xp: field(xp, yp) for xp in sorted({c + o for c in cells for o in (-1, 0, 1)})}
        for xp in cells:
            c = mid[xp]
            near = field(xp, yp - 1) + field(xp, yp + 1)
            near = near + (mid[xp - 1] + mid[xp + 1]) + (above(c) + below(c))
            s = 0.4 * c + 0.1 * near
            s1_ref[xp + 2, yp + 2] = jnp.where(inside(xp, yp), s, 0.0) if masked else s

    def second(yp, cells, masked=True):
        mid = {xp: s1_ref[xp + 2, yp + 2] for xp in sorted({c + o for c in cells for o in (-1, 0, 1)})}
        around = [above(mid[xp]) + below(mid[xp]) for xp in cells]
        rows = []
        for xp, ends in zip(cells, around):
            c = mid[xp]
            near = s1_ref[xp + 2, yp + 1] + s1_ref[xp + 2, yp + 3]
            near = near + (mid[xp - 1] + mid[xp + 1]) + ends
            s = 0.4 * c + 0.1 * near
            rows.append(jnp.where(inside(xp, yp), s, 0.0) if masked else s)
        ups = [above(s) for s in rows]
        downs = [below(s) for s in rows]
        for xp, s, up, down in zip(cells, rows, ups, downs):
            p_ref[xp + 1, yp + 1] = s
            b_ref[xp + 1, yp + 1] = 2.0 * s + (up + down)
            d_ref[xp + 1, yp + 1] = down - up

    inner_first, outer_first = range(1, 15), (-2, -1, 0, 15, 16, 17)
    inner_second, outer_second = range(2, 14), (-1, 0, 1, 14, 15, 16)
    all_first, all_second = range(-2, 18), range(-1, 17)

    def early_first(i, carry):
        for n in range(7):
            first(1 + 7 * i + n, inner_first, False)
        return carry

    def early_second(i, carry):
        for n in range(2):
            second(2 + 2 * i + n, inner_second, False)
        return carry

    lax.fori_loop(0, 2, early_first, 0)
    lax.fori_loop(0, 6, early_second, 0)

    inner_x = (me_x > 0, me_x < count_x - 1)
    inner_y = (me_y > 0, me_y < count_y - 1)
    copies[0].wait_recv()
    copies[1].wait_recv()
    for i in range(3):
        turn(i - 3, jnp.where(inner_x[0], xr_ref[0, i], 0.0), plane(13 + i))
        turn(16 + i, plane(16 + i), jnp.where(inner_x[1], xr_ref[1, i], 0.0))
    for copy in copies[2:]:
        copy.wait_recv()
    low = lanes_of() < 64
    rims = (pl.ds(0, 8), pl.ds(136, 8))
    for part in range(2):
        for x in range(16):
            tb_ref[x + 3, rims[part], :] = jnp.where(inner_y[part], yr_ref[part, x], 0.0)
        for i in range(3):
            far = jnp.where(inner_x[0], cr_ref[part, i], 0.0)
            edge = jnp.where(low, pltpu.roll(far, 64, 1), pltpu.roll(yr_ref[part, 13 + i], 64, 1))
            tb_ref[i, rims[part], :] = jnp.where(inner_y[part], edge, 0.0)
            far = jnp.where(inner_x[1], cr_ref[2 + part, i], 0.0)
            edge = jnp.where(low, pltpu.roll(yr_ref[part, i], 64, 1), pltpu.roll(far, 64, 1))
            tb_ref[19 + i, rims[part], :] = jnp.where(inner_y[part], edge, 0.0)
    for copy in copies:
        copy.wait_send()

    one = jnp.ones((8, 128), jnp.float32)
    zero = jnp.zeros((8, 128), jnp.float32)

    def features(i, k):
        s = p_ref[i, k]
        a = p_ref[i + 1, k + 1] - p_ref[i - 1, k - 1]
        c = p_ref[i + 1, k - 1] - p_ref[i - 1, k + 1]
        gx = (b_ref[i + 1, k] - b_ref[i - 1, k] + (a + c)) * (1.0 / 3.0)
        gy = (b_ref[i, k + 1] - b_ref[i, k - 1] + (a - c)) * (1.0 / 3.0)
        d = d_ref[i, k]
        gz = (d + d + (d_ref[i + 1, k] + d_ref[i - 1, k]) + (d_ref[i, k + 1] + d_ref[i, k - 1])) * (1.0 / 3.0)
        q = 1.0 + gx * gx + gy * gy + gz * gz
        m = q * lax.rsqrt(q)
        return s, gx, gy, gz, m, s * m, s * s, one

    def first_layer(g, k):
        slot = g
        for n in range(GROUP):
            rows = features(g * GROUP + n + 1, k + 1)
            for f in range(0, FEAT, 2):
                pair = jnp.concatenate([rows[f], rows[f + 1]], axis=0)
                x_ref[slot, 8 * f : 8 * f + 16, 128 * n : 128 * n + 128] = pair.astype(jnp.bfloat16)
        u_ref[slot] = jnp.dot(w1_ref[...], x_ref[slot], preferred_element_type=jnp.float32)

    def second_layer(g):
        slot = g
        u = u_ref[slot]
        hidden = (u + u * jnp.tanh(u)).astype(jnp.bfloat16)
        hidden = jnp.concatenate([hidden, hidden], axis=0)
        ch_ref[slot] = jnp.dot(w2_ref[...], hidden, preferred_element_type=jnp.float32)

    def views(g, state):
        slot = g
        for n in range(GROUP):
            row = (g * GROUP + n) * 8
            for b in range(BANDS):
                e = softplus(ch_ref[slot, 8 * b : 8 * b + 8, 128 * n : 128 * n + 128])
                t = softplus(ch_ref[slot, 64 + 8 * b : 72 + 8 * b, 128 * n : 128 * n + 128])
                q = jnp.exp2(t * (-1.0 / 512.0))
                tx = state[8 + b]
                nx = tx * q
                state[b] = state[b] + (tx - nx) * e
                state[8 + b] = nx
                ty = yt_ref[b, row : row + 8, :]
                ny = ty * q
                yc_ref[b, row : row + 8, :] = yc_ref[b, row : row + 8, :] + (ty - ny) * e
                yt_ref[b, row : row + 8, :] = ny

    chunks = 16 // GROUP

    def deliver(row):
        state = [st_ref[b] for b in range(2 * BANDS)]
        colour = [(state[b] + state[8 + b] * pltpu.roll(state[b], 64, 1)) * LN2 for b in range(BANDS)]
        clear = [state[8 + b] * pltpu.roll(state[8 + b], 64, 1) for b in range(BANDS)]
        image = jnp.transpose(jnp.concatenate(colour + clear, axis=0))
        j_ref[pl.ds(row, 64, stride=4), :] = image[0:64]

    def column(k, cells):
        past = (k + 15) // 16
        deliver(past * (((k + 3) // 4 - 1) * 256 + (k + 3) % 4) + (1 - past) * 1024)
        state = [zero] * BANDS + [one] * BANDS
        for g in range(chunks):
            first_layer((g + 8) % chunks, k + (g + 8) // chunks)
            views(g, state)
            second_layer((g + 4) % chunks)
        if cells:
            second(k + 3, cells[1])
            first(k + 5, cells[0])
        for b in range(2 * BANDS):
            st_ref[b] = state[b]

    def slab(start):
        return pl.ds(pl.multiple_of(start, 8), 8)

    def send_slabs(c):
        def one_peer(hop, carry):
            peer = peer_x(hop)
            pltpu.make_async_remote_copy(
                src_ref=j_ref.at[slab(c * 256 + peer * 8)],
                dst_ref=jr_ref.at[slab(c * 256 + me_x * 8)],
                send_sem=send_x.at[c],
                recv_sem=recv_x.at[c],
                device_id=(peer, me_y),
                device_id_type=MESH,
            ).start()
            return carry

        for hop in sorted(range(1, count_x), key=lambda h: abs(h - count_x // 2)):
            one_peer(hop, 0)
        jr_ref[slab(c * 256 + me_x * 8), :] = j_ref[slab(c * 256 + me_x * 8), :]

    def slabs_moved(c):
        many = pl.ds(0, (count_x - 1) * 8)
        return pltpu.make_async_remote_copy(
            src_ref=j_ref.at[many],
            dst_ref=jr_ref.at[many],
            send_sem=send_x.at[c],
            recv_sem=recv_x.at[c],
            device_id=(xs[1], me_y),
            device_id_type=MESH,
        )

    def rows_moved():
        many = pl.ds(0, count_y - 1)
        return pltpu.make_async_remote_copy(
            src_ref=r_ref.at[many],
            dst_ref=rr_ref.at[many],
            send_sem=send_y,
            recv_sem=recv_y,
            device_id=(me_x, ys[1]),
            device_id_type=MESH,
        )

    for yp in range(-2, 5):
        first(yp, all_first if yp < 1 else outer_first)
    for yp in range(-1, 3):
        second(yp, all_second if yp < 2 else outer_second)
    for b in range(BANDS):
        yc_ref[b] = jnp.zeros((128, 128), jnp.float32)
        yt_ref[b] = jnp.ones((128, 128), jnp.float32)
    for g in range(8):
        first_layer(g, 0)
    for g in range(4):
        second_layer(g)

    def run(begin, end, cells):
        def one_column(k, carry):
            column(k, cells)

            @pl.when((k > 0) & (k % 4 == 0))
            def _():
                send_slabs(k // 4 - 1)

            return carry

        lax.fori_loop(begin, end, one_column, 0)

    run(0, 10, (outer_first, outer_second))
    run(10, 14, (all_first, all_second))
    run(14, 16, None)
    deliver(3 * 256 + 3)

    for b in range(BANDS):
        for h in range(2):
            colour = yc_ref[b, pl.ds(64 * h, 8, stride=8), :]
            clear = yt_ref[b, pl.ds(64 * h, 8, stride=8), :]
            for s in range(1, 8):
                colour = colour + clear * yc_ref[b, pl.ds(64 * h + s, 8, stride=8), :]
                clear = clear * yt_ref[b, pl.ds(64 * h + s, 8, stride=8), :]
            rs_ref[0, 16 * b + 8 * h : 16 * b + 8 * h + 8, :] = colour * LN2
            rs_ref[1, 16 * b + 8 * h : 16 * b + 8 * h + 8, :] = clear
    for kind in range(2):
        image = jnp.transpose(rs_ref[kind])
        for h in range(2):
            for p in range(8):
                r_ref[p, 8 * h : 8 * h + 8, 128 * kind : 128 * kind + 128] = image[64 * h + 8 * p : 64 * h + 8 * p + 8]


    def send_rows(hop, carry):
        peer = peer_y(hop)
        pltpu.make_async_remote_copy(
            src_ref=r_ref.at[peer],
            dst_ref=rr_ref.at[me_y],
            send_sem=send_y,
            recv_sem=recv_y,
            device_id=(me_x, peer),
            device_id_type=MESH,
        ).start()
        return carry

    for hop in sorted(range(1, count_y), key=lambda h: abs(h - count_y // 2)):
        send_rows(hop, 0)
    send_slabs(3)
    rr_ref[me_y] = r_ref[me_y]

    at_ref[...] = jnp.zeros_like(at_ref)

    def fold_x(c):
        slabs_moved(c).wait_recv()
        image, clear = zero, one
        for s in range(count_x):
            piece = jr_ref[c * 256 + s * 8 : c * 256 + s * 8 + 8, :]
            both = jnp.where(low, pltpu.roll(piece, 64, 1), piece)
            image = jnp.where(low, image, 0.0) + clear * piece
            clear = clear * both
        for z in range(2):
            at_ref[16 * z + 4 * c : 16 * z + 4 * c + 4, :] = image[4 * z : 4 * z + 4]

    for c in range(3):
        fold_x(c)

    rows_moved().wait_recv()
    colour, clear = rr_ref[0, :, 0:128], rr_ref[0, :, 128:256]
    for s in range(1, count_y):
        colour = colour + clear * rr_ref[s, :, 0:128]
        clear = clear * rr_ref[s, :, 128:256]
    for kind, image in enumerate((colour, clear)):
        for b in range(BANDS):
            shift = (128 - 16 * b) % 128
            front = image[0:8]
            back = image[8:16]
            front = pltpu.roll(front, shift, 1) if shift else front
            back = pltpu.roll(back, shift + 16, 1) if shift < 112 else back
            vy_ref[8 * kind + b] = jnp.where(lane < 16, front, back)[:, 0:32]

    fold_x(3)
    at_ref[...] = jnp.transpose(at_ref[...])
    line = lax.broadcasted_iota(jnp.int32, (16, 128), 1)
    for z in range(2):
        row = jnp.zeros((16, 128), jnp.float32)
        for s in range(8):
            piece = at_ref[pl.ds(s, 16, stride=8), :]
            shift = (16 * s - 16 * z) % 128
            piece = pltpu.roll(piece, shift, 1) if shift else piece
            row = jnp.where((line >> 4) == s, piece, row)
        vx_ref[:, z, :] = row

    for c in range(4):
        slabs_moved(c).wait_send()
    rows_moved().wait_send()


def march_call(field, transfer_in, transfer_out, count_x, count_y):
    vmem = pl.BlockSpec(memory_space=pltpu.VMEM)

    def held(*shape, dtype=jnp.float32):
        return pltpu.VMEM(shape, dtype)

    return pl.pallas_call(
        functools.partial(march, count_x, count_y),
        out_shape=(
            jax.ShapeDtypeStruct((16, 2, 128), jnp.float32),
            jax.ShapeDtypeStruct((16, 8, 32), jnp.float32),
        ),
        in_specs=[pl.BlockSpec(memory_space=pltpu.HBM)] * 3,
        out_specs=(vmem, vmem),
        scratch_shapes=[
            held(22, 144, 128),
            held(2, 3, 64, 128),
            held(2, 3, 64, 128),
            held(2, 16, 8, 128),
            held(4, 3, 8, 128),
            held(128, 64, dtype=jnp.bfloat16),
            held(128, 256, dtype=jnp.bfloat16),
            held(20, 23, 8, 128),
            held(18, 20, 8, 128),
            held(18, 20, 8, 128),
            held(18, 20, 8, 128),
            held(16 // GROUP, 64, 128 * GROUP, dtype=jnp.bfloat16),
            held(16 // GROUP, 128, 128 * GROUP),
            held(16 // GROUP, 128, 128 * GROUP),
            held(8, 128, 128),
            held(8, 128, 128),
            held(2, 128, 128),
            held(1280, 128),
            held(1024, 128),
            held(8, 16, 256),
            held(8, 16, 256),
            held(128, 128),
            held(16, 8, 128),
            held(2048, 128),
            held(8, 16, dtype=jnp.bfloat16),
            held(16, 16, dtype=jnp.bfloat16),
            pltpu.SemaphoreType.DMA((3,)),
            pltpu.SemaphoreType.DMA((2,)),
            pltpu.SemaphoreType.DMA((2,)),
            pltpu.SemaphoreType.DMA((2,)),
            pltpu.SemaphoreType.DMA((2,)),
            pltpu.SemaphoreType.DMA((4,)),
            pltpu.SemaphoreType.DMA((4,)),
            pltpu.SemaphoreType.DMA((4,)),
            pltpu.SemaphoreType.DMA((4,)),
            pltpu.SemaphoreType.DMA,
            pltpu.SemaphoreType.DMA,
        ],
        compiler_params=pltpu.CompilerParams(collective_id=0, has_side_effects=True, vmem_limit_bytes=24 << 20),
        name="march",
    )(field, transfer_in, transfer_out)


def emit(ax_ref, ay_ref, vx_ref, vy_ref, done):
    moves = (pltpu.make_async_copy(ax_ref, vx_ref, done.at[0]), pltpu.make_async_copy(ay_ref, vy_ref, done.at[1]))
    for move in moves:
        move.start()
    for move in moves:
        move.wait()


def emit_call(ax, ay):
    anywhere = pl.BlockSpec(memory_space=pl.ANY)
    return pl.pallas_call(
        emit,
        out_shape=(jax.ShapeDtypeStruct(ax.shape, ax.dtype), jax.ShapeDtypeStruct(ay.shape, ay.dtype)),
        in_specs=[anywhere, anywhere],
        out_specs=(anywhere, anywhere),
        scratch_shapes=[pltpu.SemaphoreType.DMA((2,))],
        compiler_params=pltpu.CompilerParams(vmem_limit_bytes=1 << 20),
        name="emit",
    )(ax, ay)


def body(scalar_field, transfer_in, transfer_out):
    count_x = lax.axis_size("bx")
    count_y = lax.axis_size("by")
    ax, ay = march_call(
        pltpu.with_memory_space_constraint(scalar_field.reshape(2048, 128), pltpu.HBM),
        pltpu.with_memory_space_constraint(transfer_in.T, pltpu.HBM),
        pltpu.with_memory_space_constraint(transfer_out, pltpu.HBM),
        count_x,
        count_y,
    )
    vx, vy = emit_call(ax, ay)
    return (vx.reshape(2, 8, 2, 128), vy.reshape(2, 8, 8, 32))


def solution(mesh):
    return jax.shard_map(
        body,
        mesh=mesh,
        in_specs=(P(None, "bx", "by"), P(), P()),
        out_specs=(P(None, None, "bx", "by"), P(None, None, "by", "bx")),
        check_vma=False,
    )
```

```python
import functools

import jax
import jax.numpy as jnp
from jax import lax
from jax.experimental import pallas as pl
from jax.experimental.pallas import tpu as pltpu
from jax.sharding import PartitionSpec as P

BANDS = 8
HID = 16
FEAT = 8
LOG2E = 1.4426950408889634
LN2 = 0.6931471805599453
MESH = pl.DeviceIdType.MESH
GROUP = 2


def lanes_of():
    return lax.broadcasted_iota(jnp.int32, (8, 128), 1)


def softplus(v):
    return jnp.maximum(v, lax.log2(1.0 + jnp.exp2(jnp.minimum(v, 126.0))))


def widen(big_ref, weights, scale):
    rows, cols = weights.shape
    up = lax.broadcasted_iota(jnp.int32, (8 * rows, rows), 0) >> 3
    up = (up == lax.broadcasted_iota(jnp.int32, (8 * rows, rows), 1)).astype(jnp.float32)
    out = lax.broadcasted_iota(jnp.int32, (cols, 8 * cols), 1) >> 3
    out = (out == lax.broadcasted_iota(jnp.int32, (cols, 8 * cols), 0)).astype(jnp.float32)
    tall = jnp.dot(up.astype(jnp.bfloat16), weights, preferred_element_type=jnp.float32)
    wide = jnp.dot(tall.astype(jnp.bfloat16), out.astype(jnp.bfloat16), preferred_element_type=jnp.float32)
    at_row = lax.broadcasted_iota(jnp.int32, wide.shape, 0) & 7
    at_col = lax.broadcasted_iota(jnp.int32, wide.shape, 1) & 7
    wide = jnp.where(at_row == at_col, wide * scale, 0.0)
    big_ref[:, 0 : wide.shape[1]] = wide.astype(jnp.bfloat16)
    if big_ref.shape[1] > wide.shape[1]:
        wide = wide - wide.astype(jnp.bfloat16).astype(jnp.float32)
        big_ref[:, wide.shape[1] :] = wide.astype(jnp.bfloat16)


def march(
    count_x, count_y, field_ref, win_hbm, wout_hbm, vx_ref, vy_ref,
    tb_ref, xs_ref, xr_ref, yr_ref, cr_ref,
    w1_ref, w2_ref, s1_ref, p_ref, b_ref, d_ref, x_ref, u_ref, ch_ref, yc_ref, yt_ref, rs_ref,
    j_ref, jr_ref, r_ref, rr_ref, at_ref, st_ref, f_ref, win_ref, wout_ref, load,
    sx, rx, sy, ry, sc, rc, send_x, recv_x, send_y, recv_y,
):
    me_x = lax.axis_index("bx")
    me_y = lax.axis_index("by")
    xs = (lax.rem(me_x + count_x - 1, count_x), lax.rem(me_x + 1, count_x))
    ys = (lax.rem(me_y + count_y - 1, count_y), lax.rem(me_y + 1, count_y))

    def peer_x(hop):
        return lax.rem(me_x + hop, count_x)

    def peer_y(hop):
        return lax.rem(me_y + hop, count_y)

    fetches = (
        pltpu.make_async_copy(win_hbm, win_ref, load.at[0]),
        pltpu.make_async_copy(wout_hbm, wout_ref, load.at[1]),
    ) + tuple(
        pltpu.make_async_copy(field_ref.at[pl.ds(256 * n, 256)], f_ref.at[pl.ds(256 * n, 256)], load.at[2 + n])
        for n in range(8)
    )
    for fetch in fetches:
        fetch.start()
    barrier = pltpu.get_barrier_semaphore()

    def greet_x(hop, carry):
        pl.semaphore_signal(barrier, inc=1, device_id=(peer_x(hop), me_y), device_id_type=MESH)
        return carry

    def greet_y(hop, carry):
        pl.semaphore_signal(barrier, inc=1, device_id=(me_x, peer_y(hop)), device_id_type=MESH)
        return carry

    for x in xs:
        for y in ys:
            pl.semaphore_signal(barrier, inc=1, device_id=(x, y), device_id_type=MESH)
    for hop in range(1, count_x):
        greet_x(hop, 0)
    for hop in range(1, count_y):
        greet_y(hop, 0)

    def plane(x):
        return f_ref[pl.ds(x, 64, stride=32), :]

    fetches[0].wait()
    fetches[1].wait()
    widen(w1_ref, jnp.transpose(win_ref[...].astype(jnp.float32)).astype(jnp.bfloat16), 0.5)
    widen(w2_ref, wout_ref[...], LOG2E)
    for fetch in fetches[2:]:
        fetch.wait()
    for i in range(3):
        xs_ref[0, i] = plane(i)
        xs_ref[1, i] = plane(29 + i)
    pl.semaphore_wait(barrier, count_x + count_y + 2)

    copies = []
    for side in range(2):
        copies.append(
            pltpu.make_async_remote_copy(
                src_ref=xs_ref.at[side],
                dst_ref=xr_ref.at[1 - side],
                send_sem=sx.at[side],
                recv_sem=rx.at[1 - side],
                device_id=(xs[side], me_y),
                device_id_type=MESH,
            )
        )
        copies[-1].start()

    def turn(x, front, back):
        tb_ref[x + 3, 8:136, :] = jnp.transpose(jnp.concatenate([front, back], axis=0))

    edges = (pl.ds(8, 8), pl.ds(128, 8))
    ends = (pl.ds(3, 3), pl.ds(16, 3))
    for x in (0, 1, 2, 13, 14, 15):
        turn(x, plane(x), plane(16 + x))
    for side in range(2):
        for part in range(2):
            copies.append(
                pltpu.make_async_remote_copy(
                    src_ref=tb_ref.at[ends[side], edges[part]],
                    dst_ref=cr_ref.at[2 * (1 - side) + (1 - part)],
                    send_sem=sc.at[2 * side + part],
                    recv_sem=rc.at[2 * (1 - side) + (1 - part)],
                    device_id=(xs[side], ys[part]),
                    device_id_type=MESH,
                )
            )
            copies[-1].start()

    for x in range(3, 13):
        turn(x, plane(x), plane(16 + x))
    for part in range(2):
        copies.append(
            pltpu.make_async_remote_copy(
                src_ref=tb_ref.at[pl.ds(3, 16), edges[part]],
                dst_ref=yr_ref.at[1 - part],
                send_sem=sy.at[part],
                recv_sem=ry.at[1 - part],
                device_id=(me_x, ys[part]),
                device_id_type=MESH,
            )
        )
        copies[-1].start()

    lane = lanes_of()
    seg = lax.broadcasted_iota(jnp.int32, (8, 128), 0)
    z = lane & 63
    half = lane >> 6
    top = z == 0
    bottom = z == 63
    full_x = 32 * count_x
    full_y = 128 * count_y
    at_x = me_x * 32 + half * 16
    at_y = me_y * 128 + seg * 16

    def above(v):
        return jnp.where(top, 0.0, pltpu.roll(v, 1, 1))

    def below(v):
        return jnp.where(bottom, 0.0, pltpu.roll(v, 127, 1))

    def inside(xp, yp):
        gy = at_y + yp
        ok = (gy >= 0) & (gy < full_y)
        if xp < 0:
            ok = ok & (at_x + xp >= 0)
        if xp > 15:
            ok = ok & (at_x + xp < full_x)
        return ok

    def field(xp, yp):
        return tb_ref[xp + 3, pl.ds(yp + 8, 8, stride=16), :]

    def first(yp, cells, masked=True):
        mid = {xp: field(xp, yp) for xp in sorted({c + o for c in cells for o in (-1, 0, 1)})}
        for xp in cells:
            c = mid[xp]
            near = field(xp, yp - 1) + field(xp, yp + 1)
            near = near + (mid[xp - 1] + mid[xp + 1]) + (above(c) + below(c))
            s = 0.4 * c + 0.1 * near
            s1_ref[xp + 2, yp + 2] = jnp.where(inside(xp, yp), s, 0.0) if masked else s

    def second(yp, cells, masked=True):
        mid = {xp: s1_ref[xp + 2, yp + 2] for xp in sorted({c + o for c in cells for o in (-1, 0, 1)})}
        around = [above(mid[xp]) + below(mid[xp]) for xp in cells]
        rows = []
        for xp, ends in zip(cells, around):
            c = mid[xp]
            near = s1_ref[xp + 2, yp + 1] + s1_ref[xp + 2, yp + 3]
            near = near + (mid[xp - 1] + mid[xp + 1]) + ends
            s = 0.4 * c + 0.1 * near
            rows.append(jnp.where(inside(xp, yp), s, 0.0) if masked else s)
        ups = [above(s) for s in rows]
        downs = [below(s) for s in rows]
        for xp, s, up, down in zip(cells, rows, ups, downs):
            p_ref[xp + 1, yp + 1] = s
            b_ref[xp + 1, yp + 1] = 2.0 * s + (up + down)
            d_ref[xp + 1, yp + 1] = down - up

    inner_first, outer_first = range(1, 15), (-2, -1, 0, 15, 16, 17)
    inner_second, outer_second = range(2, 14), (-1, 0, 1, 14, 15, 16)
    all_first, all_second = range(-2, 18), range(-1, 17)

    def early_first(i, carry):
        for n in range(7):
            first(1 + 7 * i + n, inner_first, False)
        return carry

    def early_second(i, carry):
        for n in range(2):
            second(2 + 2 * i + n, inner_second, False)
        return carry

    lax.fori_loop(0, 2, early_first, 0)
    lax.fori_loop(0, 6, early_second, 0)

    inner_x = (me_x > 0, me_x < count_x - 1)
    inner_y = (me_y > 0, me_y < count_y - 1)
    copies[0].wait_recv()
    copies[1].wait_recv()
    for i in range(3):
        turn(i - 3, jnp.where(inner_x[0], xr_ref[0, i], 0.0), plane(13 + i))
        turn(16 + i, plane(16 + i), jnp.where(inner_x[1], xr_ref[1, i], 0.0))
    for copy in copies[2:]:
        copy.wait_recv()
    low = lanes_of() < 64
    rims = (pl.ds(0, 8), pl.ds(136, 8))
    for part in range(2):
        for x in range(16):
            tb_ref[x + 3, rims[part], :] = jnp.where(inner_y[part], yr_ref[part, x], 0.0)
        for i in range(3):
            far = jnp.where(inner_x[0], cr_ref[part, i], 0.0)
            edge = jnp.where(low, pltpu.roll(far, 64, 1), pltpu.roll(yr_ref[part, 13 + i], 64, 1))
            tb_ref[i, rims[part], :] = jnp.where(inner_y[part], edge, 0.0)
            far = jnp.where(inner_x[1], cr_ref[2 + part, i], 0.0)
            edge = jnp.where(low, pltpu.roll(yr_ref[part, i], 64, 1), pltpu.roll(far, 64, 1))
            tb_ref[19 + i, rims[part], :] = jnp.where(inner_y[part], edge, 0.0)
    for copy in copies:
        copy.wait_send()

    one = jnp.ones((8, 128), jnp.float32)
    zero = jnp.zeros((8, 128), jnp.float32)

    def features(i, k):
        s = p_ref[i, k]
        a = p_ref[i + 1, k + 1] - p_ref[i - 1, k - 1]
        c = p_ref[i + 1, k - 1] - p_ref[i - 1, k + 1]
        gx = (b_ref[i + 1, k] - b_ref[i - 1, k] + (a + c)) * (1.0 / 3.0)
        gy = (b_ref[i, k + 1] - b_ref[i, k - 1] + (a - c)) * (1.0 / 3.0)
        d = d_ref[i, k]
        gz = (d + d + (d_ref[i + 1, k] + d_ref[i - 1, k]) + (d_ref[i, k + 1] + d_ref[i, k - 1])) * (1.0 / 3.0)
        q = 1.0 + gx * gx + gy * gy + gz * gz
        m = q * lax.rsqrt(q)
        return s, gx, gy, gz, m, s * m, s * s, one

    def first_layer(g, k):
        slot = g
        for n in range(GROUP):
            rows = features(g * GROUP + n + 1, k + 1)
            for f in range(0, FEAT, 2):
                pair = jnp.concatenate([rows[f], rows[f + 1]], axis=0)
                x_ref[slot, 8 * f : 8 * f + 16, 128 * n : 128 * n + 128] = pair.astype(jnp.bfloat16)
        u_ref[slot] = jnp.dot(w1_ref[...], x_ref[slot], preferred_element_type=jnp.float32)

    def second_layer(g):
        slot = g
        u = u_ref[slot]
        hidden = (u + u * jnp.tanh(u)).astype(jnp.bfloat16)
        hidden = jnp.concatenate([hidden, hidden], axis=0)
        ch_ref[slot] = jnp.dot(w2_ref[...], hidden, preferred_element_type=jnp.float32)

    def views(g, state):
        slot = g
        for n in range(GROUP):
            row = (g * GROUP + n) * 8
            for b in range(BANDS):
                e = softplus(ch_ref[slot, 8 * b : 8 * b + 8, 128 * n : 128 * n + 128])
                t = softplus(ch_ref[slot, 64 + 8 * b : 72 + 8 * b, 128 * n : 128 * n + 128])
                q = jnp.exp2(t * (-1.0 / 512.0))
                tx = state[8 + b]
                nx = tx * q
                state[b] = state[b] + (tx - nx) * e
                state[8 + b] = nx
                ty = yt_ref[b, row : row + 8, :]
                ny = ty * q
                yc_ref[b, row : row + 8, :] = yc_ref[b, row : row + 8, :] + (ty - ny) * e
                yt_ref[b, row : row + 8, :] = ny

    chunks = 16 // GROUP

    def deliver(row):
        state = [st_ref[b] for b in range(2 * BANDS)]
        colour = [(state[b] + state[8 + b] * pltpu.roll(state[b], 64, 1)) * LN2 for b in range(BANDS)]
        clear = [state[8 + b] * pltpu.roll(state[8 + b], 64, 1) for b in range(BANDS)]
        image = jnp.transpose(jnp.concatenate(colour + clear, axis=0))
        j_ref[pl.ds(row, 64, stride=4), :] = image[0:64]

    def column(k, cells):
        past = (k + 15) // 16
        deliver(past * (((k + 3) // 4 - 1) * 256 + (k + 3) % 4) + (1 - past) * 1024)
        state = [zero] * BANDS + [one] * BANDS
        for g in range(chunks):
            first_layer((g + 8) % chunks, k + (g + 8) // chunks)
            views(g, state)
            second_layer((g + 4) % chunks)
        if cells:
            second(k + 3, cells[1])
            first(k + 5, cells[0])
        for b in range(2 * BANDS):
            st_ref[b] = state[b]

    def slab(start):
        return pl.ds(pl.multiple_of(start, 8), 8)

    def send_slabs(c):
        def one_peer(hop, carry):
            peer = peer_x(hop)
            pltpu.make_async_remote_copy(
                src_ref=j_ref.at[slab(c * 256 + peer * 8)],
                dst_ref=jr_ref.at[slab(c * 256 + me_x * 8)],
                send_sem=send_x.at[c],
                recv_sem=recv_x.at[c],
                device_id=(peer, me_y),
                device_id_type=MESH,
            ).start()
            return carry

        for hop in sorted(range(1, count_x), key=lambda h: abs(h - count_x // 2)):
            one_peer(hop, 0)
        jr_ref[slab(c * 256 + me_x * 8), :] = j_ref[slab(c * 256 + me_x * 8), :]

    def slabs_moved(c):
        many = pl.ds(0, (count_x - 1) * 8)
        return pltpu.make_async_remote_copy(
            src_ref=j_ref.at[many],
            dst_ref=jr_ref.at[many],
            send_sem=send_x.at[c],
            recv_sem=recv_x.at[c],
            device_id=(xs[1], me_y),
            device_id_type=MESH,
        )

    def rows_moved():
        many = pl.ds(0, count_y - 1)
        return pltpu.make_async_remote_copy(
            src_ref=r_ref.at[many],
            dst_ref=rr_ref.at[many],
            send_sem=send_y,
            recv_sem=recv_y,
            device_id=(me_x, ys[1]),
            device_id_type=MESH,
        )

    for yp in range(-2, 5):
        first(yp, all_first if yp < 1 else outer_first)
    for yp in range(-1, 3):
        second(yp, all_second if yp < 2 else outer_second)
    for b in range(BANDS):
        yc_ref[b] = jnp.zeros((128, 128), jnp.float32)
        yt_ref[b] = jnp.ones((128, 128), jnp.float32)
    for g in range(8):
        first_layer(g, 0)
    for g in range(4):
        second_layer(g)

    def run(begin, end, cells):
        def one_column(k, carry):
            column(k, cells)

            @pl.when((k > 0) & (k % 4 == 0))
            def _():
                send_slabs(k // 4 - 1)

            return carry

        lax.fori_loop(begin, end, one_column, 0)

    run(0, 10, (outer_first, outer_second))
    run(10, 14, (all_first, all_second))
    run(14, 16, None)
    deliver(3 * 256 + 3)

    for b in range(BANDS):
        for h in range(2):
            colour = yc_ref[b, pl.ds(64 * h, 8, stride=8), :]
            clear = yt_ref[b, pl.ds(64 * h, 8, stride=8), :]
            for s in range(1, 8):
                colour = colour + clear * yc_ref[b, pl.ds(64 * h + s, 8, stride=8), :]
                clear = clear * yt_ref[b, pl.ds(64 * h + s, 8, stride=8), :]
            rs_ref[0, 16 * b + 8 * h : 16 * b + 8 * h + 8, :] = colour * LN2
            rs_ref[1, 16 * b + 8 * h : 16 * b + 8 * h + 8, :] = clear
    for kind in range(2):
        image = jnp.transpose(rs_ref[kind])
        for h in range(2):
            for p in range(8):
                r_ref[p, 8 * h : 8 * h + 8, 128 * kind : 128 * kind + 128] = image[64 * h + 8 * p : 64 * h + 8 * p + 8]


    def send_rows(hop, carry):
        peer = peer_y(hop)
        pltpu.make_async_remote_copy(
            src_ref=r_ref.at[peer],
            dst_ref=rr_ref.at[me_y],
            send_sem=send_y,
            recv_sem=recv_y,
            device_id=(me_x, peer),
            device_id_type=MESH,
        ).start()
        return carry

    for hop in sorted(range(1, count_y), key=lambda h: abs(h - count_y // 2)):
        send_rows(hop, 0)
    send_slabs(3)
    rr_ref[me_y] = r_ref[me_y]

    at_ref[...] = jnp.zeros_like(at_ref)

    def fold_x(c):
        slabs_moved(c).wait_recv()
        image, clear = zero, one
        for s in range(count_x):
            piece = jr_ref[c * 256 + s * 8 : c * 256 + s * 8 + 8, :]
            both = jnp.where(low, pltpu.roll(piece, 64, 1), piece)
            image = jnp.where(low, image, 0.0) + clear * piece
            clear = clear * both
        for z in range(2):
            at_ref[16 * z + 4 * c : 16 * z + 4 * c + 4, :] = image[4 * z : 4 * z + 4]

    for c in range(3):
        fold_x(c)

    rows_moved().wait_recv()
    colour, clear = rr_ref[0, :, 0:128], rr_ref[0, :, 128:256]
    for s in range(1, count_y):
        colour = colour + clear * rr_ref[s, :, 0:128]
        clear = clear * rr_ref[s, :, 128:256]
    for kind, image in enumerate((colour, clear)):
        for b in range(BANDS):
            shift = (128 - 16 * b) % 128
            front = image[0:8]
            back = image[8:16]
            front = pltpu.roll(front, shift, 1) if shift else front
            back = pltpu.roll(back, shift + 16, 1) if shift < 112 else back
            vy_ref[8 * kind + b] = jnp.where(lane < 16, front, back)[:, 0:32]

    fold_x(3)
    at_ref[...] = jnp.transpose(at_ref[...])
    line = lax.broadcasted_iota(jnp.int32, (16, 128), 1)
    for z in range(2):
        row = jnp.zeros((16, 128), jnp.float32)
        for s in range(8):
            piece = at_ref[pl.ds(s, 16, stride=8), :]
            shift = (16 * s - 16 * z) % 128
            piece = pltpu.roll(piece, shift, 1) if shift else piece
            row = jnp.where((line >> 4) == s, piece, row)
        vx_ref[:, z, :] = row

    for c in range(4):
        slabs_moved(c).wait_send()
    rows_moved().wait_send()


def march_call(field, transfer_in, transfer_out, count_x, count_y):
    vmem = pl.BlockSpec(memory_space=pltpu.VMEM)

    def held(*shape, dtype=jnp.float32):
        return pltpu.VMEM(shape, dtype)

    return pl.pallas_call(
        functools.partial(march, count_x, count_y),
        out_shape=(
            jax.ShapeDtypeStruct((16, 2, 128), jnp.float32),
            jax.ShapeDtypeStruct((16, 8, 32), jnp.float32),
        ),
        in_specs=[pl.BlockSpec(memory_space=pltpu.HBM)] * 3,
        out_specs=(vmem, vmem),
        scratch_shapes=[
            held(22, 144, 128),
            held(2, 3, 64, 128),
            held(2, 3, 64, 128),
            held(2, 16, 8, 128),
            held(4, 3, 8, 128),
            held(128, 64, dtype=jnp.bfloat16),
            held(128, 256, dtype=jnp.bfloat16),
            held(20, 23, 8, 128),
            held(18, 20, 8, 128),
            held(18, 20, 8, 128),
            held(18, 20, 8, 128),
            held(16 // GROUP, 64, 128 * GROUP, dtype=jnp.bfloat16),
            held(16 // GROUP, 128, 128 * GROUP),
            held(16 // GROUP, 128, 128 * GROUP),
            held(8, 128, 128),
            held(8, 128, 128),
            held(2, 128, 128),
            held(1280, 128),
            held(1024, 128),
            held(8, 16, 256),
            held(8, 16, 256),
            held(128, 128),
            held(16, 8, 128),
            held(2048, 128),
            held(8, 16, dtype=jnp.bfloat16),
            held(16, 16, dtype=jnp.bfloat16),
            pltpu.SemaphoreType.DMA((10,)),
            pltpu.SemaphoreType.DMA((2,)),
            pltpu.SemaphoreType.DMA((2,)),
            pltpu.SemaphoreType.DMA((2,)),
            pltpu.SemaphoreType.DMA((2,)),
            pltpu.SemaphoreType.DMA((4,)),
            pltpu.SemaphoreType.DMA((4,)),
            pltpu.SemaphoreType.DMA((4,)),
            pltpu.SemaphoreType.DMA((4,)),
            pltpu.SemaphoreType.DMA,
            pltpu.SemaphoreType.DMA,
        ],
        compiler_params=pltpu.CompilerParams(collective_id=0, has_side_effects=True, vmem_limit_bytes=24 << 20),
        name="march",
    )(field, transfer_in, transfer_out)


def emit(ax_ref, ay_ref, vx_ref, vy_ref, done):
    moves = (pltpu.make_async_copy(ax_ref, vx_ref, done.at[0]), pltpu.make_async_copy(ay_ref, vy_ref, done.at[1]))
    for move in moves:
        move.start()
    for move in moves:
        move.wait()


def emit_call(ax, ay):
    anywhere = pl.BlockSpec(memory_space=pl.ANY)
    return pl.pallas_call(
        emit,
        out_shape=(jax.ShapeDtypeStruct(ax.shape, ax.dtype), jax.ShapeDtypeStruct(ay.shape, ay.dtype)),
        in_specs=[anywhere, anywhere],
        out_specs=(anywhere, anywhere),
        scratch_shapes=[pltpu.SemaphoreType.DMA((2,))],
        compiler_params=pltpu.CompilerParams(vmem_limit_bytes=1 << 20),
        name="emit",
    )(ax, ay)


def body(scalar_field, transfer_in, transfer_out):
    count_x = lax.axis_size("bx")
    count_y = lax.axis_size("by")
    ax, ay = march_call(
        pltpu.with_memory_space_constraint(scalar_field.reshape(2048, 128), pltpu.HBM),
        pltpu.with_memory_space_constraint(transfer_in.T, pltpu.HBM),
        pltpu.with_memory_space_constraint(transfer_out, pltpu.HBM),
        count_x,
        count_y,
    )
    vx, vy = emit_call(ax, ay)
    return (vx.reshape(2, 8, 2, 128), vy.reshape(2, 8, 8, 32))


def solution(mesh):
    return jax.shard_map(
        body,
        mesh=mesh,
        in_specs=(P(None, "bx", "by"), P(), P()),
        out_specs=(P(None, None, "bx", "by"), P(None, None, "by", "bx")),
        check_vma=False,
    )
```

```python
import functools

import jax
import jax.numpy as jnp
from jax import lax
from jax.experimental import pallas as pl
from jax.experimental.pallas import tpu as pltpu
from jax.sharding import PartitionSpec as P

BANDS = 8
HID = 16
FEAT = 8
LOG2E = 1.4426950408889634
LN2 = 0.6931471805599453
MESH = pl.DeviceIdType.MESH
GROUP = 2


def lanes_of():
    return lax.broadcasted_iota(jnp.int32, (8, 128), 1)


def softplus(v):
    return jnp.maximum(v, lax.log2(1.0 + jnp.exp2(jnp.minimum(v, 126.0))))


def widen(big_ref, weights, scale):
    rows, cols = weights.shape
    up = lax.broadcasted_iota(jnp.int32, (8 * rows, rows), 0) >> 3
    up = (up == lax.broadcasted_iota(jnp.int32, (8 * rows, rows), 1)).astype(jnp.float32)
    out = lax.broadcasted_iota(jnp.int32, (cols, 8 * cols), 1) >> 3
    out = (out == lax.broadcasted_iota(jnp.int32, (cols, 8 * cols), 0)).astype(jnp.float32)
    tall = jnp.dot(up.astype(jnp.bfloat16), weights, preferred_element_type=jnp.float32)
    wide = jnp.dot(tall.astype(jnp.bfloat16), out.astype(jnp.bfloat16), preferred_element_type=jnp.float32)
    at_row = lax.broadcasted_iota(jnp.int32, wide.shape, 0) & 7
    at_col = lax.broadcasted_iota(jnp.int32, wide.shape, 1) & 7
    wide = jnp.where(at_row == at_col, wide * scale, 0.0)
    big_ref[:, 0 : wide.shape[1]] = wide.astype(jnp.bfloat16)
    if big_ref.shape[1] > wide.shape[1]:
        wide = wide - wide.astype(jnp.bfloat16).astype(jnp.float32)
        big_ref[:, wide.shape[1] :] = wide.astype(jnp.bfloat16)


def march(
    count_x, count_y, field_ref, win_hbm, wout_hbm, vx_ref, vy_ref,
    tb_ref, xs_ref, xr_ref, yr_ref, cr_ref,
    w1_ref, w2_ref, s1_ref, p_ref, b_ref, d_ref, x_ref, u_ref, ch_ref, yc_ref, yt_ref, rs_ref,
    j_ref, jr_ref, r_ref, rr_ref, at_ref, st_ref, f_ref, win_ref, wout_ref, load,
    sx, rx, sy, ry, sc, rc, send_x, recv_x, send_y, recv_y,
):
    me_x = lax.axis_index("bx")
    me_y = lax.axis_index("by")
    xs = (lax.rem(me_x + count_x - 1, count_x), lax.rem(me_x + 1, count_x))
    ys = (lax.rem(me_y + count_y - 1, count_y), lax.rem(me_y + 1, count_y))

    def peer_x(hop):
        return lax.rem(me_x + hop, count_x)

    def peer_y(hop):
        return lax.rem(me_y + hop, count_y)

    fetches = (
        pltpu.make_async_copy(win_hbm, win_ref, load.at[0]),
        pltpu.make_async_copy(wout_hbm, wout_ref, load.at[1]),
        pltpu.make_async_copy(field_ref, f_ref, load.at[2]),
    )
    for fetch in fetches:
        fetch.start()
    barrier = pltpu.get_barrier_semaphore()

    def greet_x(hop, carry):
        pl.semaphore_signal(barrier, inc=1, device_id=(peer_x(hop), me_y), device_id_type=MESH)
        return carry

    def greet_y(hop, carry):
        pl.semaphore_signal(barrier, inc=1, device_id=(me_x, peer_y(hop)), device_id_type=MESH)
        return carry

    for x in xs:
        for y in ys:
            pl.semaphore_signal(barrier, inc=1, device_id=(x, y), device_id_type=MESH)
    for hop in range(1, count_x):
        greet_x(hop, 0)
    for hop in range(1, count_y):
        greet_y(hop, 0)

    def plane(x):
        return f_ref[pl.ds(x, 64, stride=32), :]

    fetches[2].wait()
    for i in range(3):
        xs_ref[0, i] = plane(i)
        xs_ref[1, i] = plane(29 + i)
    pl.semaphore_wait(barrier, count_x + count_y + 2)

    copies = []
    for side in range(2):
        copies.append(
            pltpu.make_async_remote_copy(
                src_ref=xs_ref.at[side],
                dst_ref=xr_ref.at[1 - side],
                send_sem=sx.at[side],
                recv_sem=rx.at[1 - side],
                device_id=(xs[side], me_y),
                device_id_type=MESH,
            )
        )
        copies[-1].start()

    def turn(x, front, back):
        tb_ref[x + 3, 8:136, :] = jnp.transpose(jnp.concatenate([front, back], axis=0))

    edges = (pl.ds(8, 8), pl.ds(128, 8))
    ends = (pl.ds(3, 3), pl.ds(16, 3))
    for x in (0, 1, 2, 13, 14, 15):
        turn(x, plane(x), plane(16 + x))
    for side in range(2):
        for part in range(2):
            copies.append(
                pltpu.make_async_remote_copy(
                    src_ref=tb_ref.at[ends[side], edges[part]],
                    dst_ref=cr_ref.at[2 * (1 - side) + (1 - part)],
                    send_sem=sc.at[2 * side + part],
                    recv_sem=rc.at[2 * (1 - side) + (1 - part)],
                    device_id=(xs[side], ys[part]),
                    device_id_type=MESH,
                )
            )
            copies[-1].start()

    for x in range(3, 13):
        turn(x, plane(x), plane(16 + x))
    for part in range(2):
        copies.append(
            pltpu.make_async_remote_copy(
                src_ref=tb_ref.at[pl.ds(3, 16), edges[part]],
                dst_ref=yr_ref.at[1 - part],
                send_sem=sy.at[part],
                recv_sem=ry.at[1 - part],
                device_id=(me_x, ys[part]),
                device_id_type=MESH,
            )
        )
        copies[-1].start()

    lane = lanes_of()
    seg = lax.broadcasted_iota(jnp.int32, (8, 128), 0)
    z = lane & 63
    half = lane >> 6
    top = z == 0
    bottom = z == 63
    full_x = 32 * count_x
    full_y = 128 * count_y
    at_x = me_x * 32 + half * 16
    at_y = me_y * 128 + seg * 16

    def above(v):
        return jnp.where(top, 0.0, pltpu.roll(v, 1, 1))

    def below(v):
        return jnp.where(bottom, 0.0, pltpu.roll(v, 127, 1))

    def inside(xp, yp):
        gy = at_y + yp
        ok = (gy >= 0) & (gy < full_y)
        if xp < 0:
            ok = ok & (at_x + xp >= 0)
        if xp > 15:
            ok = ok & (at_x + xp < full_x)
        return ok

    def field(xp, yp):
        return tb_ref[xp + 3, pl.ds(yp + 8, 8, stride=16), :]

    def first(yp, cells, masked=True):
        mid = {xp: field(xp, yp) for xp in sorted({c + o for c in cells for o in (-1, 0, 1)})}
        for xp in cells:
            c = mid[xp]
            near = field(xp, yp - 1) + field(xp, yp + 1)
            near = near + (mid[xp - 1] + mid[xp + 1]) + (above(c) + below(c))
            s = 0.4 * c + 0.1 * near
            s1_ref[xp + 2, yp + 2] = jnp.where(inside(xp, yp), s, 0.0) if masked else s

    def second(yp, cells, masked=True):
        mid = {xp: s1_ref[xp + 2, yp + 2] for xp in sorted({c + o for c in cells for o in (-1, 0, 1)})}
        around = [above(mid[xp]) + below(mid[xp]) for xp in cells]
        rows = []
        for xp, ends in zip(cells, around):
            c = mid[xp]
            near = s1_ref[xp + 2, yp + 1] + s1_ref[xp + 2, yp + 3]
            near = near + (mid[xp - 1] + mid[xp + 1]) + ends
            s = 0.4 * c + 0.1 * near
            rows.append(jnp.where(inside(xp, yp), s, 0.0) if masked else s)
        ups = [above(s) for s in rows]
        downs = [below(s) for s in rows]
        for xp, s, up, down in zip(cells, rows, ups, downs):
            p_ref[xp + 1, yp + 1] = s
            b_ref[xp + 1, yp + 1] = 2.0 * s + (up + down)
            d_ref[xp + 1, yp + 1] = down - up

    inner_first, outer_first = range(1, 15), (-2, -1, 0, 15, 16, 17)
    inner_second, outer_second = range(2, 14), (-1, 0, 1, 14, 15, 16)
    all_first, all_second = range(-2, 18), range(-1, 17)

    def early_first(i, carry):
        for n in range(7):
            first(1 + 7 * i + n, inner_first, False)
        return carry

    def early_second(i, carry):
        for n in range(2):
            second(2 + 2 * i + n, inner_second, False)
        return carry

    lax.fori_loop(0, 2, early_first, 0)
    lax.fori_loop(0, 6, early_second, 0)

    inner_x = (me_x > 0, me_x < count_x - 1)
    inner_y = (me_y > 0, me_y < count_y - 1)
    fetches[0].wait()
    fetches[1].wait()
    widen(w1_ref, jnp.transpose(win_ref[...].astype(jnp.float32)).astype(jnp.bfloat16), 0.5)
    widen(w2_ref, wout_ref[...], LOG2E)
    for b in range(BANDS):
        yc_ref[b] = jnp.zeros((128, 128), jnp.float32)
        yt_ref[b] = jnp.ones((128, 128), jnp.float32)
    at_ref[...] = jnp.zeros_like(at_ref)

    for copy in copies:
        copy.wait_recv()
    for i in range(3):
        turn(i - 3, jnp.where(inner_x[0], xr_ref[0, i], 0.0), plane(13 + i))
        turn(16 + i, plane(16 + i), jnp.where(inner_x[1], xr_ref[1, i], 0.0))
    low = lanes_of() < 64
    rims = (pl.ds(0, 8), pl.ds(136, 8))
    for part in range(2):
        for x in range(16):
            tb_ref[x + 3, rims[part], :] = jnp.where(inner_y[part], yr_ref[part, x], 0.0)
        for i in range(3):
            far = jnp.where(inner_x[0], cr_ref[part, i], 0.0)
            edge = jnp.where(low, pltpu.roll(far, 64, 1), pltpu.roll(yr_ref[part, 13 + i], 64, 1))
            tb_ref[i, rims[part], :] = jnp.where(inner_y[part], edge, 0.0)
            far = jnp.where(inner_x[1], cr_ref[2 + part, i], 0.0)
            edge = jnp.where(low, pltpu.roll(yr_ref[part, i], 64, 1), pltpu.roll(far, 64, 1))
            tb_ref[19 + i, rims[part], :] = jnp.where(inner_y[part], edge, 0.0)
    for copy in copies:
        copy.wait_send()

    one = jnp.ones((8, 128), jnp.float32)
    zero = jnp.zeros((8, 128), jnp.float32)

    def features(i, k):
        s = p_ref[i, k]
        a = p_ref[i + 1, k + 1] - p_ref[i - 1, k - 1]
        c = p_ref[i + 1, k - 1] - p_ref[i - 1, k + 1]
        gx = (b_ref[i + 1, k] - b_ref[i - 1, k] + (a + c)) * (1.0 / 3.0)
        gy = (b_ref[i, k + 1] - b_ref[i, k - 1] + (a - c)) * (1.0 / 3.0)
        d = d_ref[i, k]
        gz = (d + d + (d_ref[i + 1, k] + d_ref[i - 1, k]) + (d_ref[i, k + 1] + d_ref[i, k - 1])) * (1.0 / 3.0)
        q = 1.0 + gx * gx + gy * gy + gz * gz
        m = q * lax.rsqrt(q)
        return s, gx, gy, gz, m, s * m, s * s, one

    def first_layer(g, k):
        slot = g
        for n in range(GROUP):
            rows = features(g * GROUP + n + 1, k + 1)
            for f in range(0, FEAT, 2):
                pair = jnp.concatenate([rows[f], rows[f + 1]], axis=0)
                x_ref[slot, 8 * f : 8 * f + 16, 128 * n : 128 * n + 128] = pair.astype(jnp.bfloat16)
        u_ref[slot] = jnp.dot(w1_ref[...], x_ref[slot], preferred_element_type=jnp.float32)

    def second_layer(g):
        slot = g
        u = u_ref[slot]
        hidden = (u + u * jnp.tanh(u)).astype(jnp.bfloat16)
        hidden = jnp.concatenate([hidden, hidden], axis=0)
        ch_ref[slot] = jnp.dot(w2_ref[...], hidden, preferred_element_type=jnp.float32)

    def views(g, state):
        slot = g
        for n in range(GROUP):
            row = (g * GROUP + n) * 8
            for b in range(BANDS):
                e = softplus(ch_ref[slot, 8 * b : 8 * b + 8, 128 * n : 128 * n + 128])
                t = softplus(ch_ref[slot, 64 + 8 * b : 72 + 8 * b, 128 * n : 128 * n + 128])
                q = jnp.exp2(t * (-1.0 / 512.0))
                tx = state[8 + b]
                nx = tx * q
                state[b] = state[b] + (tx - nx) * e
                state[8 + b] = nx
                ty = yt_ref[b, row : row + 8, :]
                ny = ty * q
                yc_ref[b, row : row + 8, :] = yc_ref[b, row : row + 8, :] + (ty - ny) * e
                yt_ref[b, row : row + 8, :] = ny

    chunks = 16 // GROUP

    def deliver(row):
        state = [st_ref[b] for b in range(2 * BANDS)]
        colour = [(state[b] + state[8 + b] * pltpu.roll(state[b], 64, 1)) * LN2 for b in range(BANDS)]
        clear = [state[8 + b] * pltpu.roll(state[8 + b], 64, 1) for b in range(BANDS)]
        image = jnp.transpose(jnp.concatenate(colour + clear, axis=0))
        j_ref[pl.ds(row, 64, stride=4), :] = image[0:64]

    def column(k, cells):
        past = (k + 15) // 16
        deliver(past * (((k + 3) // 4 - 1) * 256 + (k + 3) % 4) + (1 - past) * 1024)
        state = [zero] * BANDS + [one] * BANDS
        for g in range(chunks):
            first_layer((g + 8) % chunks, k + (g + 8) // chunks)
            views(g, state)
            second_layer((g + 4) % chunks)
        if cells:
            second(k + 3, cells[1])
            first(k + 5, cells[0])
        for b in range(2 * BANDS):
            st_ref[b] = state[b]

    def slab(start):
        return pl.ds(pl.multiple_of(start, 8), 8)

    def send_slabs(c):
        def one_peer(hop, carry):
            peer = peer_x(hop)
            pltpu.make_async_remote_copy(
                src_ref=j_ref.at[slab(c * 256 + peer * 8)],
                dst_ref=jr_ref.at[slab(c * 256 + me_x * 8)],
                send_sem=send_x.at[c],
                recv_sem=recv_x.at[c],
                device_id=(peer, me_y),
                device_id_type=MESH,
            ).start()
            return carry

        for hop in sorted(range(1, count_x), key=lambda h: abs(h - count_x // 2)):
            one_peer(hop, 0)
        jr_ref[slab(c * 256 + me_x * 8), :] = j_ref[slab(c * 256 + me_x * 8), :]

    def slabs_moved(c):
        many = pl.ds(0, (count_x - 1) * 8)
        return pltpu.make_async_remote_copy(
            src_ref=j_ref.at[many],
            dst_ref=jr_ref.at[many],
            send_sem=send_x.at[c],
            recv_sem=recv_x.at[c],
            device_id=(xs[1], me_y),
            device_id_type=MESH,
        )

    def rows_moved():
        many = pl.ds(0, count_y - 1)
        return pltpu.make_async_remote_copy(
            src_ref=r_ref.at[many],
            dst_ref=rr_ref.at[many],
            send_sem=send_y,
            recv_sem=recv_y,
            device_id=(me_x, ys[1]),
            device_id_type=MESH,
        )

    for yp in range(-2, 5):
        first(yp, all_first if yp < 1 else outer_first)
    for yp in range(-1, 3):
        second(yp, all_second if yp < 2 else outer_second)
    for g in range(8):
        first_layer(g, 0)
    for g in range(4):
        second_layer(g)

    def run(begin, end, cells):
        def one_column(k, carry):
            column(k, cells)

            @pl.when((k > 0) & (k % 4 == 0))
            def _():
                send_slabs(k // 4 - 1)

            return carry

        lax.fori_loop(begin, end, one_column, 0)

    run(0, 10, (outer_first, outer_second))
    run(10, 14, (all_first, all_second))
    run(14, 16, None)
    deliver(3 * 256 + 3)

    for b in range(BANDS):
        for h in range(2):
            colour = yc_ref[b, pl.ds(64 * h, 8, stride=8), :]
            clear = yt_ref[b, pl.ds(64 * h, 8, stride=8), :]
            for s in range(1, 8):
                colour = colour + clear * yc_ref[b, pl.ds(64 * h + s, 8, stride=8), :]
                clear = clear * yt_ref[b, pl.ds(64 * h + s, 8, stride=8), :]
            rs_ref[0, 16 * b + 8 * h : 16 * b + 8 * h + 8, :] = colour * LN2
            rs_ref[1, 16 * b + 8 * h : 16 * b + 8 * h + 8, :] = clear
    for kind in range(2):
        image = jnp.transpose(rs_ref[kind])
        for h in range(2):
            for p in range(8):
                r_ref[p, 8 * h : 8 * h + 8, 128 * kind : 128 * kind + 128] = image[64 * h + 8 * p : 64 * h + 8 * p + 8]


    def send_rows(hop, carry):
        peer = peer_y(hop)
        pltpu.make_async_remote_copy(
            src_ref=r_ref.at[peer],
            dst_ref=rr_ref.at[me_y],
            send_sem=send_y,
            recv_sem=recv_y,
            device_id=(me_x, peer),
            device_id_type=MESH,
        ).start()
        return carry

    for hop in sorted(range(1, count_y), key=lambda h: abs(h - count_y // 2)):
        send_rows(hop, 0)
    send_slabs(3)
    rr_ref[me_y] = r_ref[me_y]


    def fold_x(c):
        slabs_moved(c).wait_recv()
        image, clear = zero, one
        for s in range(count_x):
            piece = jr_ref[c * 256 + s * 8 : c * 256 + s * 8 + 8, :]
            both = jnp.where(low, pltpu.roll(piece, 64, 1), piece)
            image = jnp.where(low, image, 0.0) + clear * piece
            clear = clear * both
        for z in range(2):
            at_ref[16 * z + 4 * c : 16 * z + 4 * c + 4, :] = image[4 * z : 4 * z + 4]

    for c in range(3):
        fold_x(c)

    rows_moved().wait_recv()
    colour, clear = rr_ref[0, :, 0:128], rr_ref[0, :, 128:256]
    for s in range(1, count_y):
        colour = colour + clear * rr_ref[s, :, 0:128]
        clear = clear * rr_ref[s, :, 128:256]
    for kind, image in enumerate((colour, clear)):
        for b in range(BANDS):
            shift = (128 - 16 * b) % 128
            front = image[0:8]
            back = image[8:16]
            front = pltpu.roll(front, shift, 1) if shift else front
            back = pltpu.roll(back, shift + 16, 1) if shift < 112 else back
            vy_ref[8 * kind + b] = jnp.where(lane < 16, front, back)[:, 0:32]

    fold_x(3)
    at_ref[...] = jnp.transpose(at_ref[...])
    line = lax.broadcasted_iota(jnp.int32, (16, 128), 1)
    for z in range(2):
        row = jnp.zeros((16, 128), jnp.float32)
        for s in range(8):
            piece = at_ref[pl.ds(s, 16, stride=8), :]
            shift = (16 * s - 16 * z) % 128
            piece = pltpu.roll(piece, shift, 1) if shift else piece
            row = jnp.where((line >> 4) == s, piece, row)
        vx_ref[:, z, :] = row

    for c in range(4):
        slabs_moved(c).wait_send()
    rows_moved().wait_send()


def march_call(field, transfer_in, transfer_out, count_x, count_y):
    vmem = pl.BlockSpec(memory_space=pltpu.VMEM)

    def held(*shape, dtype=jnp.float32):
        return pltpu.VMEM(shape, dtype)

    return pl.pallas_call(
        functools.partial(march, count_x, count_y),
        out_shape=(
            jax.ShapeDtypeStruct((16, 2, 128), jnp.float32),
            jax.ShapeDtypeStruct((16, 8, 32), jnp.float32),
        ),
        in_specs=[pl.BlockSpec(memory_space=pltpu.HBM)] * 3,
        out_specs=(vmem, vmem),
        scratch_shapes=[
            held(22, 144, 128),
            held(2, 3, 64, 128),
            held(2, 3, 64, 128),
            held(2, 16, 8, 128),
            held(4, 3, 8, 128),
            held(128, 64, dtype=jnp.bfloat16),
            held(128, 256, dtype=jnp.bfloat16),
            held(20, 23, 8, 128),
            held(18, 20, 8, 128),
            held(18, 20, 8, 128),
            held(18, 20, 8, 128),
            held(16 // GROUP, 64, 128 * GROUP, dtype=jnp.bfloat16),
            held(16 // GROUP, 128, 128 * GROUP),
            held(16 // GROUP, 128, 128 * GROUP),
            held(8, 128, 128),
            held(8, 128, 128),
            held(2, 128, 128),
            held(1280, 128),
            held(1024, 128),
            held(8, 16, 256),
            held(8, 16, 256),
            held(128, 128),
            held(16, 8, 128),
            held(2048, 128),
            held(8, 16, dtype=jnp.bfloat16),
            held(16, 16, dtype=jnp.bfloat16),
            pltpu.SemaphoreType.DMA((3,)),
            pltpu.SemaphoreType.DMA((2,)),
            pltpu.SemaphoreType.DMA((2,)),
            pltpu.SemaphoreType.DMA((2,)),
            pltpu.SemaphoreType.DMA((2,)),
            pltpu.SemaphoreType.DMA((4,)),
            pltpu.SemaphoreType.DMA((4,)),
            pltpu.SemaphoreType.DMA((4,)),
            pltpu.SemaphoreType.DMA((4,)),
            pltpu.SemaphoreType.DMA,
            pltpu.SemaphoreType.DMA,
        ],
        compiler_params=pltpu.CompilerParams(collective_id=0, has_side_effects=True, vmem_limit_bytes=24 << 20),
        name="march",
    )(field, transfer_in, transfer_out)


def emit(ax_ref, ay_ref, vx_ref, vy_ref, done):
    moves = (pltpu.make_async_copy(ax_ref, vx_ref, done.at[0]), pltpu.make_async_copy(ay_ref, vy_ref, done.at[1]))
    for move in moves:
        move.start()
    for move in moves:
        move.wait()


def emit_call(ax, ay):
    anywhere = pl.BlockSpec(memory_space=pl.ANY)
    return pl.pallas_call(
        emit,
        out_shape=(jax.ShapeDtypeStruct(ax.shape, ax.dtype), jax.ShapeDtypeStruct(ay.shape, ay.dtype)),
        in_specs=[anywhere, anywhere],
        out_specs=(anywhere, anywhere),
        scratch_shapes=[pltpu.SemaphoreType.DMA((2,))],
        compiler_params=pltpu.CompilerParams(vmem_limit_bytes=1 << 20),
        name="emit",
    )(ax, ay)


def body(scalar_field, transfer_in, transfer_out):
    count_x = lax.axis_size("bx")
    count_y = lax.axis_size("by")
    ax, ay = march_call(
        pltpu.with_memory_space_constraint(scalar_field.reshape(2048, 128), pltpu.HBM),
        pltpu.with_memory_space_constraint(transfer_in.T, pltpu.HBM),
        pltpu.with_memory_space_constraint(transfer_out, pltpu.HBM),
        count_x,
        count_y,
    )
    vx, vy = emit_call(ax, ay)
    return (vx.reshape(2, 8, 2, 128), vy.reshape(2, 8, 8, 32))


def solution(mesh):
    return jax.shard_map(
        body,
        mesh=mesh,
        in_specs=(P(None, "bx", "by"), P(), P()),
        out_specs=(P(None, None, "bx", "by"), P(None, None, "by", "bx")),
        check_vma=False,
    )
```

```python
import functools

import jax
import jax.numpy as jnp
from jax import lax
from jax.experimental import pallas as pl
from jax.experimental.pallas import tpu as pltpu
from jax.sharding import PartitionSpec as P

BANDS = 8
HID = 16
FEAT = 8
LOG2E = 1.4426950408889634
LN2 = 0.6931471805599453
MESH = pl.DeviceIdType.MESH
GROUP = 2


def lanes_of():
    return lax.broadcasted_iota(jnp.int32, (8, 128), 1)


def softplus(v):
    return jnp.maximum(v, lax.log2(1.0 + jnp.exp2(jnp.minimum(v, 126.0))))


def widen(big_ref, weights, scale):
    rows, cols = weights.shape
    up = lax.broadcasted_iota(jnp.int32, (8 * rows, rows), 0) >> 3
    up = (up == lax.broadcasted_iota(jnp.int32, (8 * rows, rows), 1)).astype(jnp.float32)
    out = lax.broadcasted_iota(jnp.int32, (cols, 8 * cols), 1) >> 3
    out = (out == lax.broadcasted_iota(jnp.int32, (cols, 8 * cols), 0)).astype(jnp.float32)
    tall = jnp.dot(up.astype(jnp.bfloat16), weights, preferred_element_type=jnp.float32)
    wide = jnp.dot(tall.astype(jnp.bfloat16), out.astype(jnp.bfloat16), preferred_element_type=jnp.float32)
    at_row = lax.broadcasted_iota(jnp.int32, wide.shape, 0) & 7
    at_col = lax.broadcasted_iota(jnp.int32, wide.shape, 1) & 7
    wide = jnp.where(at_row == at_col, wide * scale, 0.0)
    big_ref[:, 0 : wide.shape[1]] = wide.astype(jnp.bfloat16)
    if big_ref.shape[1] > wide.shape[1]:
        wide = wide - wide.astype(jnp.bfloat16).astype(jnp.float32)
        big_ref[:, wide.shape[1] :] = wide.astype(jnp.bfloat16)


def march(
    count_x, count_y, field_ref, win_hbm, wout_hbm, vx_ref, vy_ref,
    tb_ref, xs_ref, xr_ref, yr_ref, cr_ref,
    w1_ref, w2_ref, s1_ref, p_ref, b_ref, d_ref, x_ref, u_ref, ch_ref, yc_ref, yt_ref, rs_ref,
    j_ref, jr_ref, r_ref, rr_ref, at_ref, st_ref, f_ref, win_ref, wout_ref, load,
    sx, rx, sy, ry, sc, rc, send_x, recv_x, send_y, recv_y,
):
    me_x = lax.axis_index("bx")
    me_y = lax.axis_index("by")
    xs = (lax.rem(me_x + count_x - 1, count_x), lax.rem(me_x + 1, count_x))
    ys = (lax.rem(me_y + count_y - 1, count_y), lax.rem(me_y + 1, count_y))

    def peer_x(hop):
        return lax.rem(me_x + hop, count_x)

    def peer_y(hop):
        return lax.rem(me_y + hop, count_y)

    fetches = (
        pltpu.make_async_copy(win_hbm, win_ref, load.at[0]),
        pltpu.make_async_copy(wout_hbm, wout_ref, load.at[1]),
        pltpu.make_async_copy(field_ref, f_ref, load.at[2]),
    )
    for fetch in fetches:
        fetch.start()
    barrier = pltpu.get_barrier_semaphore()

    def greet_x(hop, carry):
        pl.semaphore_signal(barrier, inc=1, device_id=(peer_x(hop), me_y), device_id_type=MESH)
        return carry

    def greet_y(hop, carry):
        pl.semaphore_signal(barrier, inc=1, device_id=(me_x, peer_y(hop)), device_id_type=MESH)
        return carry

    for x in xs:
        for y in ys:
            pl.semaphore_signal(barrier, inc=1, device_id=(x, y), device_id_type=MESH)
    for hop in range(1, count_x):
        greet_x(hop, 0)
    for hop in range(1, count_y):
        greet_y(hop, 0)

    def plane(x):
        return f_ref[pl.ds(x, 64, stride=32), :]

    fetches[2].wait()
    for i in range(3):
        xs_ref[0, i] = plane(i)
        xs_ref[1, i] = plane(29 + i)
    pl.semaphore_wait(barrier, count_x + count_y + 2)

    copies = []
    for side in range(2):
        copies.append(
            pltpu.make_async_remote_copy(
                src_ref=xs_ref.at[side],
                dst_ref=xr_ref.at[1 - side],
                send_sem=sx.at[side],
                recv_sem=rx.at[1 - side],
                device_id=(xs[side], me_y),
                device_id_type=MESH,
            )
        )
        copies[-1].start()

    def turn(x, front, back):
        tb_ref[x + 3, 8:136, :] = jnp.transpose(jnp.concatenate([front, back], axis=0))

    edges = (pl.ds(8, 8), pl.ds(128, 8))
    ends = (pl.ds(3, 3), pl.ds(16, 3))
    for x in (0, 1, 2, 13, 14, 15):
        turn(x, plane(x), plane(16 + x))
    for side in range(2):
        for part in range(2):
            copies.append(
                pltpu.make_async_remote_copy(
                    src_ref=tb_ref.at[ends[side], edges[part]],
                    dst_ref=cr_ref.at[2 * (1 - side) + (1 - part)],
                    send_sem=sc.at[2 * side + part],
                    recv_sem=rc.at[2 * (1 - side) + (1 - part)],
                    device_id=(xs[side], ys[part]),
                    device_id_type=MESH,
                )
            )
            copies[-1].start()

    for x in range(3, 13):
        turn(x, plane(x), plane(16 + x))
    for part in range(2):
        copies.append(
            pltpu.make_async_remote_copy(
                src_ref=tb_ref.at[pl.ds(3, 16), edges[part]],
                dst_ref=yr_ref.at[1 - part],
                send_sem=sy.at[part],
                recv_sem=ry.at[1 - part],
                device_id=(me_x, ys[part]),
                device_id_type=MESH,
            )
        )
        copies[-1].start()

    lane = lanes_of()
    seg = lax.broadcasted_iota(jnp.int32, (8, 128), 0)
    z = lane & 63
    half = lane >> 6
    top = z == 0
    bottom = z == 63
    full_x = 32 * count_x
    full_y = 128 * count_y
    at_x = me_x * 32 + half * 16
    at_y = me_y * 128 + seg * 16

    def above(v):
        return jnp.where(top, 0.0, pltpu.roll(v, 1, 1))

    def below(v):
        return jnp.where(bottom, 0.0, pltpu.roll(v, 127, 1))

    def inside(xp, yp):
        gy = at_y + yp
        ok = (gy >= 0) & (gy < full_y)
        if xp < 0:
            ok = ok & (at_x + xp >= 0)
        if xp > 15:
            ok = ok & (at_x + xp < full_x)
        return ok

    def field(xp, yp):
        return tb_ref[xp + 3, pl.ds(yp + 8, 8, stride=16), :]

    def first(yp, cells, masked=True):
        mid = {xp: field(xp, yp) for xp in sorted({c + o for c in cells for o in (-1, 0, 1)})}
        for xp in cells:
            c = mid[xp]
            near = field(xp, yp - 1) + field(xp, yp + 1)
            near = near + (mid[xp - 1] + mid[xp + 1]) + (above(c) + below(c))
            s = 0.4 * c + 0.1 * near
            s1_ref[xp + 2, yp + 2] = jnp.where(inside(xp, yp), s, 0.0) if masked else s

    def second(yp, cells, masked=True):
        mid = {xp: s1_ref[xp + 2, yp + 2] for xp in sorted({c + o for c in cells for o in (-1, 0, 1)})}
        around = [above(mid[xp]) + below(mid[xp]) for xp in cells]
        rows = []
        for xp, ends in zip(cells, around):
            c = mid[xp]
            near = s1_ref[xp + 2, yp + 1] + s1_ref[xp + 2, yp + 3]
            near = near + (mid[xp - 1] + mid[xp + 1]) + ends
            s = 0.4 * c + 0.1 * near
            rows.append(jnp.where(inside(xp, yp), s, 0.0) if masked else s)
        ups = [above(s) for s in rows]
        downs = [below(s) for s in rows]
        for xp, s, up, down in zip(cells, rows, ups, downs):
            p_ref[xp + 1, yp + 1] = s
            b_ref[xp + 1, yp + 1] = 2.0 * s + (up + down)
            d_ref[xp + 1, yp + 1] = down - up

    inner_first, outer_first = range(1, 15), (-2, -1, 0, 15, 16, 17)
    inner_second, outer_second = range(2, 14), (-1, 0, 1, 14, 15, 16)
    all_first, all_second = range(-2, 18), range(-1, 17)

    def early_first(i, carry):
        for n in range(7):
            first(1 + 7 * i + n, inner_first, False)
        return carry

    def early_second(i, carry):
        for n in range(2):
            second(2 + 2 * i + n, inner_second, False)
        return carry

    lax.fori_loop(0, 2, early_first, 0)
    lax.fori_loop(0, 6, early_second, 0)

    inner_x = (me_x > 0, me_x < count_x - 1)
    inner_y = (me_y > 0, me_y < count_y - 1)
    fetches[0].wait()
    fetches[1].wait()
    widen(w1_ref, jnp.transpose(win_ref[...].astype(jnp.float32)).astype(jnp.bfloat16), 0.5)
    widen(w2_ref, wout_ref[...], LOG2E)
    for b in range(BANDS):
        yc_ref[b] = jnp.zeros((128, 128), jnp.float32)
        yt_ref[b] = jnp.ones((128, 128), jnp.float32)
    at_ref[...] = jnp.zeros_like(at_ref)

    for copy in copies:
        copy.wait_recv()
    for i in range(3):
        turn(i - 3, jnp.where(inner_x[0], xr_ref[0, i], 0.0), plane(13 + i))
        turn(16 + i, plane(16 + i), jnp.where(inner_x[1], xr_ref[1, i], 0.0))
    low = lanes_of() < 64
    rims = (pl.ds(0, 8), pl.ds(136, 8))
    for part in range(2):
        for x in range(16):
            tb_ref[x + 3, rims[part], :] = jnp.where(inner_y[part], yr_ref[part, x], 0.0)
        for i in range(3):
            far = jnp.where(inner_x[0], cr_ref[part, i], 0.0)
            edge = jnp.where(low, pltpu.roll(far, 64, 1), pltpu.roll(yr_ref[part, 13 + i], 64, 1))
            tb_ref[i, rims[part], :] = jnp.where(inner_y[part], edge, 0.0)
            far = jnp.where(inner_x[1], cr_ref[2 + part, i], 0.0)
            edge = jnp.where(low, pltpu.roll(yr_ref[part, i], 64, 1), pltpu.roll(far, 64, 1))
            tb_ref[19 + i, rims[part], :] = jnp.where(inner_y[part], edge, 0.0)
    for copy in copies:
        copy.wait_send()

    one = jnp.ones((8, 128), jnp.float32)
    zero = jnp.zeros((8, 128), jnp.float32)

    def features(i, k):
        s = p_ref[i, k]
        a = p_ref[i + 1, k + 1] - p_ref[i - 1, k - 1]
        c = p_ref[i + 1, k - 1] - p_ref[i - 1, k + 1]
        gx = (b_ref[i + 1, k] - b_ref[i - 1, k] + (a + c)) * (1.0 / 3.0)
        gy = (b_ref[i, k + 1] - b_ref[i, k - 1] + (a - c)) * (1.0 / 3.0)
        d = d_ref[i, k]
        gz = (d + d + (d_ref[i + 1, k] + d_ref[i - 1, k]) + (d_ref[i, k + 1] + d_ref[i, k - 1])) * (1.0 / 3.0)
        q = 1.0 + gx * gx + gy * gy + gz * gz
        m = q * lax.rsqrt(q)
        return s, gx, gy, gz, m, s * m, s * s, one

    def first_layer(g, k):
        slot = g
        for n in range(GROUP):
            rows = features(g * GROUP + n + 1, k + 1)
            for f in range(0, FEAT, 2):
                pair = jnp.concatenate([rows[f], rows[f + 1]], axis=0)
                x_ref[slot, 8 * f : 8 * f + 16, 128 * n : 128 * n + 128] = pair.astype(jnp.bfloat16)
        u_ref[slot] = jnp.dot(w1_ref[...], x_ref[slot], preferred_element_type=jnp.float32)

    def second_layer(g):
        slot = g
        u = u_ref[slot]
        hidden = (u + u * jnp.tanh(u)).astype(jnp.bfloat16)
        hidden = jnp.concatenate([hidden, hidden], axis=0)
        ch_ref[slot] = jnp.dot(w2_ref[...], hidden, preferred_element_type=jnp.float32)

    def views(g, state):
        slot = g
        for n in range(GROUP):
            row = (g * GROUP + n) * 8
            for b in range(BANDS):
                e = softplus(ch_ref[slot, 8 * b : 8 * b + 8, 128 * n : 128 * n + 128])
                t = softplus(ch_ref[slot, 64 + 8 * b : 72 + 8 * b, 128 * n : 128 * n + 128])
                q = jnp.exp2(t * (-1.0 / 512.0))
                tx = state[8 + b]
                nx = tx * q
                state[b] = state[b] + (tx - nx) * e
                state[8 + b] = nx
                ty = yt_ref[b, row : row + 8, :]
                ny = ty * q
                yc_ref[b, row : row + 8, :] = yc_ref[b, row : row + 8, :] + (ty - ny) * e
                yt_ref[b, row : row + 8, :] = ny

    chunks = 16 // GROUP

    def deliver(row):
        state = [st_ref[b] for b in range(2 * BANDS)]
        colour = [(state[b] + state[8 + b] * pltpu.roll(state[b], 64, 1)) * LN2 for b in range(BANDS)]
        clear = [state[8 + b] * pltpu.roll(state[8 + b], 64, 1) for b in range(BANDS)]
        image = jnp.transpose(jnp.concatenate(colour + clear, axis=0))
        j_ref[pl.ds(row, 64, stride=4), :] = image[0:64]

    def column(k, cells):
        past = (k + 15) // 16
        deliver(past * (((k + 3) // 4 - 1) * 256 + (k + 3) % 4) + (1 - past) * 1024)
        state = [zero] * BANDS + [one] * BANDS
        for g in range(chunks):
            first_layer((g + 8) % chunks, k + (g + 8) // chunks)
            views(g, state)
            second_layer((g + 4) % chunks)
        if cells:
            second(k + 3, cells[1])
            first(k + 5, cells[0])
        for b in range(2 * BANDS):
            st_ref[b] = state[b]

    def slab(start):
        return pl.ds(pl.multiple_of(start, 8), 8)

    def send_slabs(c):
        def one_peer(hop, carry):
            peer = peer_x(hop)
            pltpu.make_async_remote_copy(
                src_ref=j_ref.at[slab(c * 256 + peer * 8)],
                dst_ref=jr_ref.at[slab(c * 256 + me_x * 8)],
                send_sem=send_x.at[c],
                recv_sem=recv_x.at[c],
                device_id=(peer, me_y),
                device_id_type=MESH,
            ).start()
            return carry

        for hop in sorted(range(1, count_x), key=lambda h: abs(h - count_x // 2)):
            one_peer(hop, 0)
        jr_ref[slab(c * 256 + me_x * 8), :] = j_ref[slab(c * 256 + me_x * 8), :]

    def slabs_moved(c):
        many = pl.ds(0, (count_x - 1) * 8)
        return pltpu.make_async_remote_copy(
            src_ref=j_ref.at[many],
            dst_ref=jr_ref.at[many],
            send_sem=send_x.at[c],
            recv_sem=recv_x.at[c],
            device_id=(xs[1], me_y),
            device_id_type=MESH,
        )

    def rows_moved():
        many = pl.ds(0, count_y - 1)
        return pltpu.make_async_remote_copy(
            src_ref=r_ref.at[many],
            dst_ref=rr_ref.at[many],
            send_sem=send_y,
            recv_sem=recv_y,
            device_id=(me_x, ys[1]),
            device_id_type=MESH,
        )

    for yp in range(-2, 5):
        first(yp, all_first if yp < 1 else outer_first)
    for yp in range(-1, 3):
        second(yp, all_second if yp < 2 else outer_second)
    for g in range(8):
        first_layer(g, 0)
    for g in range(4):
        second_layer(g)

    def run(begin, end, cells):
        def one_column(k, carry):
            column(k, cells)

            @pl.when((k > 0) & (k % 4 == 0))
            def _():
                send_slabs(k // 4 - 1)

            return carry

        lax.fori_loop(begin, end, one_column, 0)

    run(0, 10, (outer_first, outer_second))
    run(10, 14, (all_first, all_second))
    run(14, 16, None)
    deliver(3 * 256 + 3)
    send_slabs(3)

    for b in range(BANDS):
        for h in range(2):
            colour = yc_ref[b, pl.ds(64 * h, 8, stride=8), :]
            clear = yt_ref[b, pl.ds(64 * h, 8, stride=8), :]
            for s in range(1, 8):
                colour = colour + clear * yc_ref[b, pl.ds(64 * h + s, 8, stride=8), :]
                clear = clear * yt_ref[b, pl.ds(64 * h + s, 8, stride=8), :]
            rs_ref[0, 16 * b + 8 * h : 16 * b + 8 * h + 8, :] = colour * LN2
            rs_ref[1, 16 * b + 8 * h : 16 * b + 8 * h + 8, :] = clear
    for kind in range(2):
        image = jnp.transpose(rs_ref[kind])
        for h in range(2):
            for p in range(8):
                r_ref[p, 8 * h : 8 * h + 8, 128 * kind : 128 * kind + 128] = image[64 * h + 8 * p : 64 * h + 8 * p + 8]


    def send_rows(hop, carry):
        peer = peer_y(hop)
        pltpu.make_async_remote_copy(
            src_ref=r_ref.at[peer],
            dst_ref=rr_ref.at[me_y],
            send_sem=send_y,
            recv_sem=recv_y,
            device_id=(me_x, peer),
            device_id_type=MESH,
        ).start()
        return carry

    for hop in sorted(range(1, count_y), key=lambda h: abs(h - count_y // 2)):
        send_rows(hop, 0)
    rr_ref[me_y] = r_ref[me_y]


    def fold_x(c):
        slabs_moved(c).wait_recv()
        image, clear = zero, one
        for s in range(count_x):
            piece = jr_ref[c * 256 + s * 8 : c * 256 + s * 8 + 8, :]
            both = jnp.where(low, pltpu.roll(piece, 64, 1), piece)
            image = jnp.where(low, image, 0.0) + clear * piece
            clear = clear * both
        for z in range(2):
            at_ref[16 * z + 4 * c : 16 * z + 4 * c + 4, :] = image[4 * z : 4 * z + 4]

    for c in range(3):
        fold_x(c)

    rows_moved().wait_recv()
    colour, clear = rr_ref[0, :, 0:128], rr_ref[0, :, 128:256]
    for s in range(1, count_y):
        colour = colour + clear * rr_ref[s, :, 0:128]
        clear = clear * rr_ref[s, :, 128:256]
    for kind, image in enumerate((colour, clear)):
        for b in range(BANDS):
            shift = (128 - 16 * b) % 128
            front = image[0:8]
            back = image[8:16]
            front = pltpu.roll(front, shift, 1) if shift else front
            back = pltpu.roll(back, shift + 16, 1) if shift < 112 else back
            vy_ref[8 * kind + b] = jnp.where(lane < 16, front, back)[:, 0:32]

    fold_x(3)
    at_ref[...] = jnp.transpose(at_ref[...])
    line = lax.broadcasted_iota(jnp.int32, (16, 128), 1)
    for z in range(2):
        row = jnp.zeros((16, 128), jnp.float32)
        for s in range(8):
            piece = at_ref[pl.ds(s, 16, stride=8), :]
            shift = (16 * s - 16 * z) % 128
            piece = pltpu.roll(piece, shift, 1) if shift else piece
            row = jnp.where((line >> 4) == s, piece, row)
        vx_ref[:, z, :] = row

    for c in range(4):
        slabs_moved(c).wait_send()
    rows_moved().wait_send()


def march_call(field, transfer_in, transfer_out, count_x, count_y):
    vmem = pl.BlockSpec(memory_space=pltpu.VMEM)

    def held(*shape, dtype=jnp.float32):
        return pltpu.VMEM(shape, dtype)

    return pl.pallas_call(
        functools.partial(march, count_x, count_y),
        out_shape=(
            jax.ShapeDtypeStruct((16, 2, 128), jnp.float32),
            jax.ShapeDtypeStruct((16, 8, 32), jnp.float32),
        ),
        in_specs=[pl.BlockSpec(memory_space=pltpu.HBM)] * 3,
        out_specs=(vmem, vmem),
        scratch_shapes=[
            held(22, 144, 128),
            held(2, 3, 64, 128),
            held(2, 3, 64, 128),
            held(2, 16, 8, 128),
            held(4, 3, 8, 128),
            held(128, 64, dtype=jnp.bfloat16),
            held(128, 256, dtype=jnp.bfloat16),
            held(20, 23, 8, 128),
            held(18, 20, 8, 128),
            held(18, 20, 8, 128),
            held(18, 20, 8, 128),
            held(16 // GROUP, 64, 128 * GROUP, dtype=jnp.bfloat16),
            held(16 // GROUP, 128, 128 * GROUP),
            held(16 // GROUP, 128, 128 * GROUP),
            held(8, 128, 128),
            held(8, 128, 128),
            held(2, 128, 128),
            held(1280, 128),
            held(1024, 128),
            held(8, 16, 256),
            held(8, 16, 256),
            held(128, 128),
            held(16, 8, 128),
            held(2048, 128),
            held(8, 16, dtype=jnp.bfloat16),
            held(16, 16, dtype=jnp.bfloat16),
            pltpu.SemaphoreType.DMA((3,)),
            pltpu.SemaphoreType.DMA((2,)),
            pltpu.SemaphoreType.DMA((2,)),
            pltpu.SemaphoreType.DMA((2,)),
            pltpu.SemaphoreType.DMA((2,)),
            pltpu.SemaphoreType.DMA((4,)),
            pltpu.SemaphoreType.DMA((4,)),
            pltpu.SemaphoreType.DMA((4,)),
            pltpu.SemaphoreType.DMA((4,)),
            pltpu.SemaphoreType.DMA,
            pltpu.SemaphoreType.DMA,
        ],
        compiler_params=pltpu.CompilerParams(collective_id=0, has_side_effects=True, vmem_limit_bytes=24 << 20),
        name="march",
    )(field, transfer_in, transfer_out)


def emit(ax_ref, ay_ref, vx_ref, vy_ref, done):
    moves = (pltpu.make_async_copy(ax_ref, vx_ref, done.at[0]), pltpu.make_async_copy(ay_ref, vy_ref, done.at[1]))
    for move in moves:
        move.start()
    for move in moves:
        move.wait()


def emit_call(ax, ay):
    anywhere = pl.BlockSpec(memory_space=pl.ANY)
    return pl.pallas_call(
        emit,
        out_shape=(jax.ShapeDtypeStruct(ax.shape, ax.dtype), jax.ShapeDtypeStruct(ay.shape, ay.dtype)),
        in_specs=[anywhere, anywhere],
        out_specs=(anywhere, anywhere),
        scratch_shapes=[pltpu.SemaphoreType.DMA((2,))],
        compiler_params=pltpu.CompilerParams(vmem_limit_bytes=1 << 20),
        name="emit",
    )(ax, ay)


def body(scalar_field, transfer_in, transfer_out):
    count_x = lax.axis_size("bx")
    count_y = lax.axis_size("by")
    ax, ay = march_call(
        pltpu.with_memory_space_constraint(scalar_field.reshape(2048, 128), pltpu.HBM),
        pltpu.with_memory_space_constraint(transfer_in.T, pltpu.HBM),
        pltpu.with_memory_space_constraint(transfer_out, pltpu.HBM),
        count_x,
        count_y,
    )
    vx, vy = emit_call(ax, ay)
    return (vx.reshape(2, 8, 2, 128), vy.reshape(2, 8, 8, 32))


def solution(mesh):
    return jax.shard_map(
        body,
        mesh=mesh,
        in_specs=(P(None, "bx", "by"), P(), P()),
        out_specs=(P(None, None, "bx", "by"), P(None, None, "by", "bx")),
        check_vma=False,
    )
```
